512 devices in a mesh: dp: 4 (over z_hi, core), row: 4 (over z_lo), col: 32 (over x, y).
Axes of the slice: x: 4, y: 8, z: 8 (z_hi: 2, z_lo: 4; z = z_hi * 4 + z_lo), core: 2. Of those that a mesh axis runs over, the one named last changes fastest.
Arguments:
- tokens: bfloat16 [4, 128, 256, 256], P('dp', 'row', 'col'), may hold values from -6 to 6
- timesteps: int32 [4], P('dp'), may hold values from 0 to 999
- cotangent: bfloat16 [4, 128, 256, 256], P('dp', 'row', 'col'), may hold values from -6 to 6
- qkv_weight: bfloat16 [256, 768], replicated, may hold values from -0.375 to 0.375
- output_weight: bfloat16 [256, 256], replicated, may hold values from -0.375 to 0.375
- time_weight: bfloat16 [256, 256], replicated, may hold values from -0.375 to 0.375
Outputs:
- result: bfloat16 [4, 128, 256, 256], P('dp', 'row', 'col')
- grad_tokens: bfloat16 [4, 128, 256, 256], P('dp', 'row', 'col')
- grad_qkv: float32 [256, 768], replicated
- grad_output: float32 [256, 256], replicated
- grad_time: float32 [256, 256], replicated
The draws below stay inside these ranges and needn't reach their ends.
All inputs are finite; a program needn't handle non-finite values.
Results may differ from the reference program's by a relative error of at most 0.0084.
Values may be sent and summed in bfloat16 or wider, within the bound.
No kernel may reach another device: no remote copies, remote signals or barrier semaphores. Data moves between devices by JAX's collectives and lax.ppermute only.
A program may use at most 64 MiB of HBM per device.

```python
import math
import jax
import jax.numpy as jnp
from jax import lax

D = 256
HEAD_DIM = 64
HEADS = 4
CF = 256
RADIUS = 3
IMAGES = 4
NH = 128
NW = 256


def set_ends(entries, key, least, high):
    shape = entries.shape
    index_at = [jax.random.randint(jax.random.fold_in(key, axis), (), 0, shape[axis]) for axis in range(len(shape))]
    entries = entries.at[tuple(index_at)].set(least)
    longest = shape.index(max(shape))
    index_at[longest] = (index_at[longest] + 1) % shape[longest]
    return entries.at[tuple(index_at)].set(high)


def levels(key, extent, shards, smallest, largest):
    loudness, own = 1.0, jax.random.fold_in(key, 6)
    for dim, parts in shards:
        draws = jnp.exp(jax.random.uniform(jax.random.fold_in(own, dim), (parts,), jnp.float32, smallest / len(shards), largest / len(shards)))
        loudness = loudness * jnp.repeat(draws, extent[dim] // parts).reshape([-1 if axis == dim else 1 for axis in range(len(extent))])
    return loudness


def centred(own_key, shape, scale, most, pieces=(), kind=jnp.bfloat16):
    values = jax.random.normal(own_key, shape, jnp.float32) * scale
    if len(pieces) > 0:
        values = levels(own_key, shape, pieces, -0.22, 0.18) * values
    return jnp.clip(values, min=-most, max=most).astype(kind)


def setup_inputs(seed: int = 0) -> dict:
    arg_keys = jax.random.split(jax.random.key(seed), 7)
    return {
        "tokens": centred(arg_keys[0], (IMAGES, NH, NW, D), 1.0, 6.0, ((0, 4), (1, 4), (2, 32))),
        "timesteps": set_ends(jax.random.randint(arg_keys[1], (IMAGES,), 0, 1000), jax.random.fold_in(arg_keys[1], 1), 0, 999).astype(jnp.int32),
        "cotangent": centred(arg_keys[2], (IMAGES, NH, NW, D), 1.0, 6.0, ((0, 4), (1, 4), (2, 32))),
        "qkv_weight": centred(arg_keys[3], (D, 3 * D), D ** -0.5, 0.375),
        "output_weight": centred(arg_keys[4], (D, D), D ** -0.5, 0.375),
        "time_weight": centred(arg_keys[5], (CF, D), CF ** -0.5, 0.375),
    }


score_scale = 6.0
epsilon = 1e-06

def fourier(step_value):
    half_count = CF // 2
    ladder = jnp.arange(half_count, dtype=jnp.float32)
    frequency = jnp.exp(ladder * (-math.log(1000.0) / half_count))
    phase_angle = step_value.astype(jnp.float32) * frequency
    return jnp.concatenate([jnp.cos(phase_angle), jnp.sin(phase_angle)])

def norm_back(values, inverse, grad_normed, factor):
    inner_mean = lax.optimization_barrier(jnp.mean(grad_normed * values, axis=-1, keepdims=True))
    return factor * inverse * (grad_normed - values * inverse * inverse * inner_mean)

def rounded(values):
    return lax.optimization_barrier(values.astype(jnp.bfloat16)).astype(jnp.float32)

def image_pass(picture, step_value, cotangent_image, qkv_weight, output_weight, time_weight):
    height = picture.shape[0]
    breadth = picture.shape[1]
    features = fourier(step_value)
    adaptive = 1.0 + jnp.dot(features, time_weight.astype(jnp.float32), precision=lax.Precision.HIGHEST)
    pixels = picture.astype(jnp.float32)
    inverse = lax.rsqrt(lax.optimization_barrier(jnp.mean(pixels * pixels, axis=-1, keepdims=True)) + epsilon)
    normed = (pixels * inverse * adaptive).astype(jnp.bfloat16)
    flat_normed = normed.reshape(height * breadth, D)
    project = jnp.dot(flat_normed, qkv_weight, preferred_element_type=jnp.float32)
    project = project.reshape(height, breadth, 3, HEADS, HEAD_DIM)
    query_raw = project[:, :, 0]
    key_raw = project[:, :, 1]
    value_raw = project[:, :, 2]
    query_inv = lax.rsqrt(lax.optimization_barrier(jnp.mean(query_raw * query_raw, axis=-1, keepdims=True)) + epsilon)
    key_inv = lax.rsqrt(lax.optimization_barrier(jnp.mean(key_raw * key_raw, axis=-1, keepdims=True)) + epsilon)
    query_factor = score_scale / HEAD_DIM
    query_wide = rounded(query_raw * query_inv * query_factor)
    key_wide = rounded(key_raw * key_inv)
    value_wide = rounded(value_raw)
    spread = ((RADIUS, RADIUS), (RADIUS, RADIUS), (0, 0), (0, 0))
    key_pad = jnp.pad(key_wide, spread)
    value_pad = jnp.pad(value_wide, spread)
    row_place = jnp.arange(height, dtype=jnp.int32)[:, None]
    col_place = jnp.arange(breadth, dtype=jnp.int32)[None, :]
    offsets = [(row_shift, col_shift) for row_shift in range(-RADIUS, RADIUS + 1) for col_shift in range(-RADIUS, RADIUS + 1)]

    def shifted(padded, row_shift, col_shift):
        return padded[RADIUS + row_shift:RADIUS + row_shift + height, RADIUS + col_shift:RADIUS + col_shift + breadth]
    exponent_list = []
    for row_shift, col_shift in offsets:
        inside = (row_place + row_shift >= 0) & (row_place + row_shift < height) & (col_place + col_shift >= 0) & (col_place + col_shift < breadth)
        scores = lax.optimization_barrier(jnp.sum(query_wide * shifted(key_pad, row_shift, col_shift), axis=-1))
        exponent_list.append(jnp.where(inside[:, :, None], jnp.exp(scores - score_scale), 0.0))
    denominator = exponent_list[0]
    for position in range(1, len(exponent_list)):
        denominator = denominator + exponent_list[position]
    weight_list = [rounded(term / denominator) for term in exponent_list]
    attended = jnp.zeros((height, breadth, HEADS, HEAD_DIM), jnp.float32)
    for position in range(len(offsets)):
        row_shift, col_shift = offsets[position]
        attended = attended + weight_list[position][..., None] * shifted(value_pad, row_shift, col_shift)
    attended = attended.astype(jnp.bfloat16).reshape(height * breadth, D)
    mixed_out = jnp.dot(attended, output_weight, preferred_element_type=jnp.float32)
    result = (pixels + mixed_out.reshape(height, breadth, D)).astype(jnp.bfloat16)
    flat_cotan = cotangent_image.reshape(height * breadth, D)
    grad_output = jnp.dot(attended.T, flat_cotan, preferred_element_type=jnp.float32)
    grad_attended = jnp.dot(flat_cotan, output_weight.T, preferred_element_type=jnp.float32)
    grad_wide = rounded(grad_attended).reshape(height, breadth, HEADS, HEAD_DIM)
    slope_list = []
    for row_shift, col_shift in offsets:
        slope_list.append(lax.optimization_barrier(jnp.sum(grad_wide * shifted(value_pad, row_shift, col_shift), axis=-1)))
    middle = weight_list[0] * slope_list[0]
    for position in range(1, len(offsets)):
        middle = middle + weight_list[position] * slope_list[position]
    grad_query = jnp.zeros((height, breadth, HEADS, HEAD_DIM), jnp.float32)
    grad_key_pad = jnp.zeros((height + 2 * RADIUS, breadth + 2 * RADIUS, HEADS, HEAD_DIM), jnp.float32)
    grad_value_pad = jnp.zeros((height + 2 * RADIUS, breadth + 2 * RADIUS, HEADS, HEAD_DIM), jnp.float32)
    for position in range(len(offsets)):
        row_shift, col_shift = offsets[position]
        grad_score = rounded(weight_list[position] * (slope_list[position] - middle))
        grad_query = grad_query + grad_score[..., None] * shifted(key_pad, row_shift, col_shift)
        row_low = RADIUS + row_shift
        col_low = RADIUS + col_shift
        grad_key_pad = grad_key_pad.at[row_low:row_low + height, col_low:col_low + breadth].add(grad_score[..., None] * query_wide)
        grad_value_pad = grad_value_pad.at[row_low:row_low + height, col_low:col_low + breadth].add(weight_list[position][..., None] * grad_wide)
    grad_key = grad_key_pad[RADIUS:RADIUS + height, RADIUS:RADIUS + breadth]
    grad_value = grad_value_pad[RADIUS:RADIUS + height, RADIUS:RADIUS + breadth]
    grad_query_raw = norm_back(query_raw, query_inv, grad_query, query_factor)
    grad_key_raw = norm_back(key_raw, key_inv, grad_key, 1.0)
    grad_project = jnp.stack([grad_query_raw, grad_key_raw, grad_value], axis=2).reshape(height * breadth, 3 * D).astype(jnp.bfloat16)
    grad_qkv = jnp.dot(flat_normed.T, grad_project, preferred_element_type=jnp.float32)
    grad_normed = jnp.dot(grad_project, qkv_weight.T, preferred_element_type=jnp.float32).reshape(height, breadth, D)
    scaled = grad_normed * adaptive
    grad_pixels = norm_back(pixels, inverse, scaled, 1.0)
    grad_tokens = (cotangent_image.astype(jnp.float32) + grad_pixels).astype(jnp.bfloat16)
    grad_adaptive = lax.optimization_barrier(jnp.sum(grad_normed * pixels * inverse, axis=(0, 1)))
    grad_time = features[:, None] * grad_adaptive[None, :]
    return (result, grad_tokens, grad_qkv, grad_output, grad_time)

def reference(tokens, timesteps, cotangent, qkv_weight, output_weight, time_weight):

    def one_image(inputs):
        return image_pass(inputs[0], inputs[1], inputs[2], qkv_weight, output_weight, time_weight)
    outcome = lax.map(one_image, (tokens, timesteps, cotangent))
    return (outcome[0], outcome[1], lax.optimization_barrier(jnp.sum(outcome[2], axis=0)), lax.optimization_barrier(jnp.sum(outcome[3], axis=0)), lax.optimization_barrier(jnp.sum(outcome[4], axis=0)))
```

```python
import math

import jax
import jax.numpy as jnp
from jax import lax
from jax.sharding import PartitionSpec as P

HEAD_DIM = 64
CF = 256
RADIUS = 3
TILE_ROWS = 16


score_scale = 6.0
epsilon = 1e-06


def extended(block, sides, width):
    for axis, dim in sides:
        count = lax.axis_size(axis)
        forward = [(i, i + 1) for i in range(count - 1)]
        backward = [(target, source) for source, target in forward]
        low = lax.ppermute(
            lax.slice_in_dim(block, block.shape[dim] - width, None, axis=dim), axis, forward
        )
        high = lax.ppermute(lax.slice_in_dim(block, 0, width, axis=dim), axis, backward)
        block = jnp.concatenate([low, block, high], axis=dim)
    return block


def fourier(step_value):
    half_count = CF // 2
    ladder = jnp.arange(half_count, dtype=jnp.float32)
    frequency = jnp.exp(ladder * (-math.log(1000.0) / half_count))
    phase_angle = step_value.astype(jnp.float32) * frequency
    return jnp.concatenate([jnp.cos(phase_angle), jnp.sin(phase_angle)])


def norm_back(values, inverse, grad_normed, factor):
    inner_mean = jnp.mean(grad_normed * values, axis=-1, keepdims=True)
    return factor * inverse * (grad_normed - values * inverse * inverse * inner_mean)


def tile_mask(tile_start, row_first, col_first, tile_rows, breadth, total_rows, total_cols):
    padded_cols = breadth + 2 * RADIUS
    query_place = jnp.arange(tile_rows * breadth, dtype=jnp.int32)
    key_place = jnp.arange((tile_rows + 2 * RADIUS) * padded_cols, dtype=jnp.int32)
    query_row = (query_place // breadth)[:, None]
    query_col = (query_place % breadth)[:, None]
    key_row = (key_place // padded_cols)[None, :]
    key_col = (key_place % padded_cols)[None, :]
    nearby = (
        (key_row - query_row >= 0)
        & (key_row - query_row <= 2 * RADIUS)
        & (key_col - query_col >= 0)
        & (key_col - query_col <= 2 * RADIUS)
    )
    global_row = row_first + tile_start + key_row - RADIUS
    global_col = col_first + key_col - RADIUS
    inside = (
        (global_row >= 0)
        & (global_row < total_rows)
        & (global_col >= 0)
        & (global_col < total_cols)
    )
    return jnp.where(nearby & inside, 1.0, 0.0).astype(jnp.float32)


def tile_weights(query_tile, key_block, key_mask):
    scores = jnp.einsum("qhe,khe->hqk", query_tile, key_block, preferred_element_type=jnp.float32)
    exponent = jnp.exp(scores - score_scale) * key_mask[None]
    denominator = jnp.sum(exponent, axis=2, keepdims=True)
    return (exponent / denominator).astype(jnp.bfloat16)


def on_device(tokens, timesteps, cotangent, qkv_weight, output_weight, time_weight):
    picture = tokens[0]
    height, breadth, model_width = picture.shape
    head_count = model_width // HEAD_DIM
    tile_rows = TILE_ROWS
    tile_count = height // tile_rows
    query_count = tile_rows * breadth
    key_rows = tile_rows + 2 * RADIUS
    padded_cols = breadth + 2 * RADIUS
    key_count = key_rows * padded_cols
    row_first = lax.axis_index("row") * height
    col_first = lax.axis_index("col") * breadth
    total_rows = height * lax.axis_size("row")
    total_cols = breadth * lax.axis_size("col")
    features = fourier(timesteps[0])
    adaptive = 1.0 + jnp.dot(
        features, time_weight.astype(jnp.float32), precision=lax.Precision.HIGHEST
    )
    pixels = picture.astype(jnp.float32)
    inverse = lax.rsqrt(jnp.mean(pixels * pixels, axis=-1, keepdims=True) + epsilon)
    normed = (pixels * inverse * adaptive).astype(jnp.bfloat16)
    flat_normed = normed.reshape(height * breadth, model_width)
    project = jnp.dot(flat_normed, qkv_weight, preferred_element_type=jnp.float32)
    project = project.reshape(height, breadth, 3, head_count, HEAD_DIM)
    query_raw = project[:, :, 0]
    key_raw = project[:, :, 1]
    value_raw = project[:, :, 2]
    query_inv = lax.rsqrt(jnp.mean(query_raw * query_raw, axis=-1, keepdims=True) + epsilon)
    key_inv = lax.rsqrt(jnp.mean(key_raw * key_raw, axis=-1, keepdims=True) + epsilon)
    query_factor = score_scale / HEAD_DIM
    query_unit = (query_raw * query_inv * query_factor).astype(jnp.bfloat16)
    key_unit = (key_raw * key_inv).astype(jnp.bfloat16)
    value_unit = value_raw.astype(jnp.bfloat16)
    key_value = jnp.concatenate(
        [
            key_unit.reshape(height, breadth, model_width),
            value_unit.reshape(height, breadth, model_width),
        ],
        axis=-1,
    )
    key_value_pad = extended(key_value, (("row", 0), ("col", 1)), RADIUS)
    query_tiles = query_unit.reshape(tile_count, query_count, head_count, HEAD_DIM)

    def tile_inputs(tile_index):
        pair_block = lax.dynamic_slice_in_dim(key_value_pad, tile_index * tile_rows, key_rows, 0)
        pair_block = pair_block.reshape(key_count, 2, head_count, HEAD_DIM)
        key_mask = tile_mask(
            tile_index * tile_rows, row_first, col_first, tile_rows, breadth, total_rows, total_cols
        )
        return (pair_block[:, 0], pair_block[:, 1], key_mask)

    def forward_tile(tile_index):
        key_block, value_block, key_mask = tile_inputs(tile_index)
        weights = tile_weights(query_tiles[tile_index], key_block, key_mask)
        attended_tile = jnp.einsum(
            "hqk,khe->qhe", weights, value_block, preferred_element_type=jnp.float32
        )
        return attended_tile.astype(jnp.bfloat16).reshape(query_count, model_width)

    attended = lax.map(forward_tile, jnp.arange(tile_count, dtype=jnp.int32)).reshape(
        height * breadth, model_width
    )
    mixed_out = jnp.dot(attended, output_weight, preferred_element_type=jnp.float32)
    result = (pixels + mixed_out.reshape(height, breadth, model_width)).astype(jnp.bfloat16)
    flat_cotan = cotangent[0].reshape(height * breadth, model_width)
    grad_output = jnp.dot(attended.T, flat_cotan, preferred_element_type=jnp.float32)
    grad_attended = jnp.dot(flat_cotan, output_weight.T, preferred_element_type=jnp.float32).astype(
        jnp.bfloat16
    )
    grad_tiles = grad_attended.reshape(tile_count, query_count, head_count, HEAD_DIM)

    def backward_tile(grad_pad, tile_index):
        key_block, value_block, key_mask = tile_inputs(tile_index)
        query_tile = query_tiles[tile_index]
        grad_tile = grad_tiles[tile_index]
        weights = tile_weights(query_tile, key_block, key_mask)
        weight_wide = weights.astype(jnp.float32)
        slope_term = jnp.einsum(
            "qhe,khe->hqk", grad_tile, value_block, preferred_element_type=jnp.float32
        )
        middle = jnp.sum(weight_wide * slope_term, axis=2, keepdims=True)
        grad_score = (weight_wide * (slope_term - middle)).astype(jnp.bfloat16)
        grad_query = jnp.einsum(
            "hqk,khe->qhe", grad_score, key_block, preferred_element_type=jnp.float32
        )
        grad_key = jnp.einsum(
            "hqk,qhe->khe", grad_score, query_tile, preferred_element_type=jnp.float32
        )
        grad_value = jnp.einsum(
            "hqk,qhe->khe", weights, grad_tile, preferred_element_type=jnp.float32
        )
        tile_piece = jnp.concatenate(
            [grad_key.reshape(key_count, model_width), grad_value.reshape(key_count, model_width)],
            axis=-1,
        )
        tile_piece = tile_piece.reshape(key_rows, padded_cols, 2 * model_width)
        row_start = tile_index * tile_rows
        previous = lax.dynamic_slice_in_dim(grad_pad, row_start, key_rows, 0)
        grad_pad = lax.dynamic_update_slice_in_dim(grad_pad, previous + tile_piece, row_start, 0)
        return (grad_pad, grad_query)

    empty_pad = jnp.zeros((height + 2 * RADIUS, padded_cols, 2 * model_width), jnp.float32)
    grad_pad, grad_query_tiles = lax.scan(
        backward_tile, empty_pad, jnp.arange(tile_count, dtype=jnp.int32)
    )
    edge_rows = jnp.concatenate([grad_pad[:RADIUS], grad_pad[height + RADIUS :]], axis=0)
    received_rows = extended(edge_rows.astype(jnp.bfloat16), (("row", 0),), RADIUS).astype(
        edge_rows.dtype
    )
    inner_rows = grad_pad[RADIUS : height + RADIUS]
    inner_rows = inner_rows.at[:RADIUS].add(received_rows[:RADIUS])
    inner_rows = inner_rows.at[height - RADIUS :].add(received_rows[3 * RADIUS :])
    edge_cols = jnp.concatenate([inner_rows[:, :RADIUS], inner_rows[:, breadth + RADIUS :]], axis=1)
    received_cols = extended(edge_cols.astype(jnp.bfloat16), (("col", 1),), RADIUS).astype(
        edge_cols.dtype
    )
    own_cells = inner_rows[:, RADIUS : breadth + RADIUS]
    own_cells = own_cells.at[:, :RADIUS].add(received_cols[:, :RADIUS])
    own_cells = own_cells.at[:, breadth - RADIUS :].add(received_cols[:, 3 * RADIUS :])
    grad_key = own_cells[..., :model_width].reshape(height, breadth, head_count, HEAD_DIM)
    grad_value = own_cells[..., model_width:].reshape(height, breadth, head_count, HEAD_DIM)
    grad_query = grad_query_tiles.reshape(height, breadth, head_count, HEAD_DIM)
    grad_query_raw = norm_back(query_raw, query_inv, grad_query, query_factor)
    grad_key_raw = norm_back(key_raw, key_inv, grad_key, 1.0)
    grad_project = (
        jnp.stack([grad_query_raw, grad_key_raw, grad_value], axis=2)
        .reshape(height * breadth, 3 * model_width)
        .astype(jnp.bfloat16)
    )
    grad_qkv = jnp.dot(flat_normed.T, grad_project, preferred_element_type=jnp.float32)
    grad_normed = jnp.dot(grad_project, qkv_weight.T, preferred_element_type=jnp.float32).reshape(
        height, breadth, model_width
    )
    scaled = grad_normed * adaptive
    grad_pixels = norm_back(pixels, inverse, scaled, 1.0)
    grad_tokens = (cotangent[0].astype(jnp.float32) + grad_pixels).astype(jnp.bfloat16)
    grad_adaptive = jnp.sum(grad_normed * pixels * inverse, axis=(0, 1))
    total_qkv, total_output, total_time = summed(grad_qkv, grad_output, grad_adaptive, timesteps[0])
    return (result[None], grad_tokens[None], total_qkv, total_output, total_time)


def swap(pieces, axes):
    return lax.all_to_all(pieces, axes, 0, 0, tiled=True)


def summed(grad_qkv, grad_output, grad_adaptive, step_value):
    width = grad_qkv.shape[1] + grad_output.shape[1]
    rows = grad_qkv.shape[0]
    images = lax.axis_size("dp")
    parts = lax.axis_size("col")
    others = lax.axis_size("dp") * lax.axis_size("row")
    block = rows // parts
    lanes = grad_adaptive.shape[0] * images // block
    mine = (jnp.arange(images) == lax.axis_index("dp"))[:, None]
    side = jnp.where(mine, grad_adaptive[None], 0.0).reshape(1, block, lanes)
    high = (step_value // 32).astype(jnp.float32)
    low = (step_value % 32).astype(jnp.float32)
    steps = jnp.where(mine, jnp.stack([high, low])[None], 0.0).reshape(1, 1, 2 * images)
    steps = jnp.pad(steps, ((0, 0), (0, block - 1), (0, lanes - 2 * images)))
    side = jnp.pad(jnp.concatenate([side, steps], axis=0), ((0, parts - 2), (0, 0), (0, 0)))
    whole = jnp.concatenate([grad_qkv, grad_output, side.reshape(rows, lanes)], axis=1)
    pieces = whole.astype(jnp.bfloat16).reshape(parts, block, width + lanes)
    piece = jnp.sum(swap(pieces, "col").astype(jnp.float32), axis=0).astype(jnp.bfloat16)
    copies = lax.optimization_barrier(jnp.broadcast_to(piece[None], (others,) + piece.shape))
    piece = jnp.sum(swap(copies, ("dp", "row")).astype(jnp.float32), axis=0).astype(jnp.bfloat16)
    copies = lax.optimization_barrier(jnp.broadcast_to(piece[None], (parts,) + piece.shape))
    whole = swap(copies, "col").astype(jnp.float32)
    side = whole[:2, :, width:]
    whole = whole.reshape(rows, width + lanes)
    adaptives = side[0].reshape(images, grad_adaptive.shape[0])
    steps = side[1, 0, : 2 * images].reshape(images, 2) / (parts * lax.axis_size("row"))
    features = jax.vmap(fourier)(steps[:, 0] * 32.0 + steps[:, 1])
    total_time = jnp.sum(features[:, :, None] * adaptives[:, None, :], axis=0)
    return whole[:, : grad_qkv.shape[1]], whole[:, grad_qkv.shape[1] : width], total_time


def solution(mesh):
    in_specs = (P("dp", "row", "col", None), P("dp"), P("dp", "row", "col", None), P(), P(), P())
    out_specs = (P("dp", "row", "col", None), P("dp", "row", "col", None), P(), P(), P())
    return jax.shard_map(
        on_device, mesh=mesh, in_specs=in_specs, out_specs=out_specs, check_vma=False
    )
```

```python
import functools
import math

import jax
import jax.numpy as jnp
from jax import lax
from jax.experimental import pallas as pl
from jax.experimental.pallas import tpu as pltpu
from jax.sharding import PartitionSpec as P

HEAD_DIM = 64
CF = 256
RADIUS = 3
REACH = 2 * RADIUS
SPAN = 2
WINDOW = SPAN + REACH

score_scale = 6.0
epsilon = 1e-06


def fourier(step_value):
    half_count = CF // 2
    ladder = jnp.arange(half_count, dtype=jnp.float32)
    frequency = jnp.exp(ladder * (-math.log(1000.0) / half_count))
    phase_angle = step_value.astype(jnp.float32) * frequency
    return jnp.concatenate([jnp.cos(phase_angle), jnp.sin(phase_angle)])


def exchange(to_next, to_previous, axis):
    count = lax.axis_size(axis)
    forward = [(i, i + 1) for i in range(count - 1)]
    backward = [(target, source) for source, target in forward]
    return lax.ppermute(to_next, axis, forward), lax.ppermute(to_previous, axis, backward)


def nn(left, right):
    return lax.dot_general(left, right, (((1,), (0,)), ((), ())), preferred_element_type=jnp.float32)


def nt(left, right):
    return lax.dot_general(left, right, (((1,), (1,)), ((), ())), preferred_element_type=jnp.float32)


def tn(left, right):
    return lax.dot_general(left, right, (((0,), (0,)), ((), ())), preferred_element_type=jnp.float32)


def block_kernel(
    sizes,
    place_ref,
    tok_ref,
    cot_ref,
    low_ref,
    high_ref,
    adaptive_ref,
    qkv_ref,
    out_ref,
    result_ref,
    grad_tokens_ref,
    whole_ref,
    query_ref,
    key_ref,
    value_ref,
    grad_ref,
    mask_ref,
    attended_ref,
    grad_query_ref,
    grad_key_ref,
    grad_value_ref,
):
    height, total_rows, total_cols = sizes
    cols, rows, width = tok_ref.shape
    heads = width // HEAD_DIM
    around = cols + 2 * REACH
    query_cols = cols + REACH
    lanes = heads * SPAN * rows
    row_first = place_ref[0]
    col_first = place_ref[1]
    image = place_ref[2]
    step_value = place_ref[3]
    adaptive = adaptive_ref[...]
    factor = score_scale / HEAD_DIM

    own_head = lax.broadcasted_iota(jnp.int32, (width, width), 0) // HEAD_DIM
    other_head = lax.broadcasted_iota(jnp.int32, (width, width), 1) // HEAD_DIM
    average = jnp.where(own_head == other_head, 1.0 / HEAD_DIM, 0.0).astype(jnp.bfloat16)

    def head_mean(values):
        coarse = values.astype(jnp.bfloat16)
        fine = (values - coarse.astype(jnp.float32)).astype(jnp.bfloat16)
        return nn(coarse, average) + nn(fine, average)

    def normalized(pixels):
        inverse = lax.rsqrt(jnp.mean(pixels * pixels, axis=-1, keepdims=True) + epsilon)
        return inverse, (pixels * inverse * adaptive).astype(jnp.bfloat16)

    def put(first, count, project):
        query_raw = project[:, :width]
        key_raw = project[:, width : 2 * width]
        query_inv = lax.rsqrt(head_mean(query_raw * query_raw) + epsilon)
        key_inv = lax.rsqrt(head_mean(key_raw * key_raw) + epsilon)
        here = pl.ds(first, count)
        query_ref[here] = (query_raw * query_inv * factor).astype(jnp.bfloat16).reshape(count, rows, width)
        key_ref[here] = (key_raw * key_inv).astype(jnp.bfloat16).reshape(count, rows, width)
        value_ref[here] = project[:, 2 * width :].astype(jnp.bfloat16).reshape(count, rows, width)
        return query_raw, query_inv, key_raw, key_inv

    for ref, first in ((low_ref, 0), (high_ref, REACH + cols)):
        pixels = ref[:REACH].astype(jnp.float32).reshape(REACH * rows, width)
        put(first, REACH, nn(normalized(pixels)[1], qkv_ref[...]))
    pixels = tok_ref[...].astype(jnp.float32).reshape(cols * rows, width)
    inverse, normed = normalized(pixels)
    query_raw, query_inv, key_raw, key_inv = put(REACH, cols, nn(normed, qkv_ref[...]))

    cot_own = cot_ref[...].reshape(cols * rows, width)
    grad_ref[pl.ds(RADIUS, cols)] = nt(cot_own, out_ref[...]).astype(jnp.bfloat16).reshape(cols, rows, width)
    for ref, first in ((low_ref, 0), (high_ref, RADIUS + cols)):
        side = ref[REACH:].reshape(RADIUS * rows, width)
        grad_ref[pl.ds(first, RADIUS)] = nt(side, out_ref[...]).astype(jnp.bfloat16).reshape(RADIUS, rows, width)

    shape = (WINDOW, rows, lanes)
    key_row = lax.broadcasted_iota(jnp.int32, shape, 1)
    key_col = lax.broadcasted_iota(jnp.int32, shape, 0)
    lane = lax.broadcasted_iota(jnp.int32, (1, 1, lanes), 2) % (SPAN * rows)
    query_col = lane // rows
    query_row = lane % rows
    row_gap = key_row - query_row
    col_gap = key_col - query_col
    image_row = row_first + key_row - REACH
    allowed = (row_gap >= -RADIUS) & (row_gap <= RADIUS) & (col_gap >= 0) & (col_gap <= REACH)
    allowed = allowed & (image_row >= 0) & (image_row < total_rows)
    mask_ref[...] = jnp.where(allowed, 1.0, 0.0)

    grad_key_ref[...] = jnp.zeros_like(grad_key_ref)
    grad_value_ref[...] = jnp.zeros_like(grad_value_ref)
    lane_head = lax.broadcasted_iota(jnp.int32, (1, width), 1) // HEAD_DIM
    picks = [jnp.where(lane_head == head, 1.0, 0.0) for head in range(heads)]
    narrow = [pick.astype(jnp.bfloat16) for pick in picks]
    column = lax.broadcasted_iota(jnp.int32, (WINDOW, 1, 1), 0)

    def spread(values):
        return jnp.concatenate([values * pick for pick in narrow], axis=0)

    def gathered(values):
        total = values[: SPAN * rows] * picks[0]
        for head in range(1, heads):
            total = total + values[head * SPAN * rows : (head + 1) * SPAN * rows] * picks[head]
        return total

    def step(index, carry):
        start = SPAN * index
        near = pl.ds(start, WINDOW)
        keys = key_ref[near].reshape(WINDOW * rows, width)
        values = value_ref[near].reshape(WINDOW * rows, width)
        queries = spread(query_ref[pl.ds(start + RADIUS, SPAN)].reshape(SPAN * rows, width))
        grads = spread(grad_ref[pl.ds(start, SPAN)].reshape(SPAN * rows, width))
        image_col = col_first + start + column - REACH
        inside = jnp.where((image_col >= 0) & (image_col < total_cols), 1.0, 0.0)
        mask = (mask_ref[...] * inside).reshape(WINDOW * rows, lanes)
        exponent = jnp.exp(nt(keys, queries) - score_scale) * mask
        denominator = jnp.maximum(jnp.sum(exponent, axis=0, keepdims=True), 1e-30)
        weights = (exponent * (1.0 / denominator)).astype(jnp.bfloat16)
        wide = weights.astype(jnp.float32)
        slope = nt(values, grads)
        middle = jnp.sum(wide * slope, axis=0, keepdims=True)
        grad_score = (wide * (slope - middle)).astype(jnp.bfloat16)
        attended = gathered(tn(weights, values)).astype(jnp.bfloat16)
        attended_ref[pl.ds(start, SPAN)] = attended.reshape(SPAN, rows, width)
        grad_query_ref[pl.ds(start, SPAN)] = gathered(tn(grad_score, keys)).reshape(SPAN, rows, width)
        grad_key_ref[near] += nn(grad_score, queries).reshape(WINDOW, rows, width)
        grad_value_ref[near] += nn(weights, grads).reshape(WINDOW, rows, width)
        return carry

    lax.fori_loop(0, query_cols // SPAN, step, 0)

    row = lax.broadcasted_iota(jnp.int32, (cols, rows, 1), 1)
    own = jnp.where((row >= REACH) & (row < REACH + height), 1.0, 0.0).reshape(cols * rows, 1)
    attended = attended_ref[pl.ds(RADIUS, cols)].reshape(cols * rows, width)
    result = pixels + nn(attended, out_ref[...])
    result_ref[...] = result.astype(jnp.bfloat16).reshape(cols, rows, width)
    cotan = cot_own.astype(jnp.float32)
    grad_output = tn(attended, (cotan * own).astype(jnp.bfloat16))

    def back(raw, inv, grad, scale):
        return scale * inv * (grad - raw * inv * inv * head_mean(grad * raw))

    grad_query = grad_query_ref[pl.ds(RADIUS, cols)].reshape(cols * rows, width)
    grad_key = grad_key_ref[pl.ds(REACH, cols)].reshape(cols * rows, width)
    grad_value = grad_value_ref[pl.ds(REACH, cols)].reshape(cols * rows, width)
    grad_project = jnp.concatenate(
        [
            (back(query_raw, query_inv, grad_query, factor) * own).astype(jnp.bfloat16),
            (back(key_raw, key_inv, grad_key, 1.0) * own).astype(jnp.bfloat16),
            (grad_value * own).astype(jnp.bfloat16),
        ],
        axis=1,
    )
    grad_qkv = tn(normed, grad_project)
    grad_normed = nt(grad_project, qkv_ref[...])
    scaled = grad_normed * adaptive
    inner = jnp.mean(scaled * pixels, axis=-1, keepdims=True)
    grad_pixels = inverse * (scaled - pixels * (inverse * inverse * inner))
    grad_tokens_ref[...] = (cotan + grad_pixels).astype(jnp.bfloat16).reshape(cols, rows, width)
    grad_adaptive = jnp.sum(grad_normed * (pixels * inverse), axis=0, keepdims=True)

    whole_ref[:, : 3 * width] = grad_qkv.astype(jnp.bfloat16)
    whole_ref[:, 3 * width : 4 * width] = grad_output.astype(jnp.bfloat16)
    extra = whole_ref.shape[1] - 4 * width
    line = lax.broadcasted_iota(jnp.int32, (2 * SLOT, extra), 0)
    lane = lax.broadcasted_iota(jnp.int32, (2 * SLOT, extra), 1)
    pieces = width // extra
    side = jnp.zeros((2 * SLOT, extra), jnp.float32)
    for piece in range(pieces):
        part = grad_adaptive[:, piece * extra : (piece + 1) * extra]
        side = jnp.where(line == pieces * image + piece, part, side)
    high = (step_value // 32).astype(jnp.float32)
    low = (step_value % 32).astype(jnp.float32)
    side = jnp.where((line == SLOT) & (lane == 2 * image), high, side)
    side = jnp.where((line == SLOT) & (lane == 2 * image + 1), low, side)
    whole_ref[:, 4 * width :] = jnp.zeros((width, extra), jnp.bfloat16)
    whole_ref[: 2 * SLOT, 4 * width :] = side.astype(jnp.bfloat16)


SLOT = 8
EXTRA = 128


def block_call(sizes, place, tok, cot, low, high, adaptive, qkv_weight, output_weight):
    cols, rows, width = tok.shape
    around = cols + 2 * REACH
    query_cols = cols + REACH
    lanes = width // HEAD_DIM * SPAN * rows
    vmem = pl.BlockSpec(memory_space=pltpu.VMEM)
    return pl.pallas_call(
        functools.partial(block_kernel, sizes),
        out_shape=(
            jax.ShapeDtypeStruct((cols, rows, width), jnp.bfloat16),
            jax.ShapeDtypeStruct((cols, rows, width), jnp.bfloat16),
            jax.ShapeDtypeStruct((width, 4 * width + EXTRA), jnp.bfloat16),
        ),
        in_specs=[pl.BlockSpec(memory_space=pltpu.SMEM)] + [vmem] * 7,
        out_specs=(vmem,) * 3,
        scratch_shapes=[
            pltpu.VMEM((around, rows, width), jnp.bfloat16),
            pltpu.VMEM((around, rows, width), jnp.bfloat16),
            pltpu.VMEM((around, rows, width), jnp.bfloat16),
            pltpu.VMEM((query_cols, rows, width), jnp.bfloat16),
            pltpu.VMEM((WINDOW, rows, lanes), jnp.float32),
            pltpu.VMEM((query_cols, rows, width), jnp.bfloat16),
            pltpu.VMEM((query_cols, rows, width), jnp.float32),
            pltpu.VMEM((around, rows, width), jnp.float32),
            pltpu.VMEM((around, rows, width), jnp.float32),
        ],
        compiler_params=pltpu.CompilerParams(vmem_limit_bytes=48 * 2**20),
        cost_estimate=pl.CostEstimate(flops=8_000_000_000, bytes_accessed=4_000_000, transcendentals=1_000_000),
        name="block",
    )(place, tok, cot, low, high, adaptive, qkv_weight, output_weight)


def on_device(tokens, timesteps, cotangent, qkv_weight, output_weight, time_weight):
    height, cols, width = tokens.shape[1:]
    row_first = lax.axis_index("row") * height
    col_first = lax.axis_index("col") * cols
    total_rows = height * lax.axis_size("row")
    total_cols = cols * lax.axis_size("col")
    tok = tokens[0].transpose(1, 0, 2)
    cot = cotangent[0].transpose(1, 0, 2)
    both = jnp.concatenate([tok, cot], axis=0)
    above, below = exchange(both[:, height - REACH :], both[:, :REACH], "row")
    spare = -(height + 2 * REACH) % 16
    blank = jnp.zeros((2 * cols, spare, width), jnp.bfloat16)
    both = jnp.concatenate([above, both, below, blank], axis=1)
    tok, cot = both[:cols], both[cols:]
    to_next = jnp.concatenate([tok[cols - REACH :], cot[cols - RADIUS :]], axis=0)
    to_previous = jnp.concatenate([tok[:REACH], cot[:RADIUS]], axis=0)
    left, right = exchange(to_next, to_previous, "col")
    features = fourier(timesteps[0])
    adaptive = 1.0 + jnp.dot(
        features[None], time_weight.astype(jnp.float32), precision=lax.Precision.HIGHEST
    )
    place = jnp.stack([row_first, col_first, lax.axis_index("dp"), timesteps[0]]).astype(jnp.int32)
    result, grad_tokens, whole = block_call(
        (height, total_rows, total_cols), place, tok, cot, left, right, adaptive, qkv_weight, output_weight
    )
    result = result[:, REACH : REACH + height].transpose(1, 0, 2)
    grad_tokens = grad_tokens[:, REACH : REACH + height].transpose(1, 0, 2)
    total_qkv, total_output, total_time = summed(whole, width)
    return (result[None], grad_tokens[None], total_qkv, total_output, total_time)


def swap(pieces, axes):
    return lax.all_to_all(pieces, axes, 0, 0, tiled=True)


def summed(whole, width):
    rows, across = whole.shape
    images = lax.axis_size("dp")
    parts = lax.axis_size("col")
    others = lax.axis_size("dp") * lax.axis_size("row")
    pieces = whole.reshape(parts, rows // parts, across)
    piece = jnp.sum(swap(pieces, "col").astype(jnp.float32), axis=0).astype(jnp.bfloat16)
    copies = lax.optimization_barrier(jnp.broadcast_to(piece[None], (others,) + piece.shape))
    piece = jnp.sum(swap(copies, ("dp", "row")).astype(jnp.float32), axis=0).astype(jnp.bfloat16)
    copies = lax.optimization_barrier(jnp.broadcast_to(piece[None], (parts,) + piece.shape))
    whole = swap(copies, "col").astype(jnp.float32).reshape(rows, across)
    adaptives = whole[:SLOT, 4 * width :].reshape(images, width)
    steps = whole[SLOT, 4 * width : 4 * width + 2 * images].reshape(images, 2)
    steps = steps / (parts * lax.axis_size("row"))
    features = jax.vmap(fourier)(steps[:, 0] * 32.0 + steps[:, 1])
    total_time = jnp.sum(features[:, :, None] * adaptives[:, None, :], axis=0)
    return whole[:, : 3 * width], whole[:, 3 * width : 4 * width], total_time


def solution(mesh):
    in_specs = (P("dp", "row", "col", None), P("dp"), P("dp", "row", "col", None), P(), P(), P())
    out_specs = (P("dp", "row", "col", None), P("dp", "row", "col", None), P(), P(), P())
    return jax.shard_map(
        on_device, mesh=mesh, in_specs=in_specs, out_specs=out_specs, check_vma=False
    )
```

```python
import functools
import math

import jax
import jax.numpy as jnp
from jax import lax
from jax.experimental import pallas as pl
from jax.experimental.pallas import tpu as pltpu
from jax.sharding import PartitionSpec as P

HEAD_DIM = 64
CF = 256
RADIUS = 3
REACH = 2 * RADIUS
SPAN = 2
WINDOW = SPAN + REACH

score_scale = 6.0
epsilon = 1e-06


def fourier(step_value):
    half_count = CF // 2
    ladder = jnp.arange(half_count, dtype=jnp.float32)
    frequency = jnp.exp(ladder * (-math.log(1000.0) / half_count))
    phase_angle = step_value.astype(jnp.float32) * frequency
    return jnp.concatenate([jnp.cos(phase_angle), jnp.sin(phase_angle)])


def exchange(to_next, to_previous, axis):
    count = lax.axis_size(axis)
    forward = [(i, i + 1) for i in range(count - 1)]
    backward = [(target, source) for source, target in forward]
    return lax.ppermute(to_next, axis, forward), lax.ppermute(to_previous, axis, backward)


def nn(left, right):
    return lax.dot_general(left, right, (((1,), (0,)), ((), ())), preferred_element_type=jnp.float32)


def nt(left, right):
    return lax.dot_general(left, right, (((1,), (1,)), ((), ())), preferred_element_type=jnp.float32)


def tn(left, right):
    return lax.dot_general(left, right, (((0,), (0,)), ((), ())), preferred_element_type=jnp.float32)


def average_matrix(width):
    own_head = lax.broadcasted_iota(jnp.int32, (width, width), 0) // HEAD_DIM
    other_head = lax.broadcasted_iota(jnp.int32, (width, width), 1) // HEAD_DIM
    return jnp.where(own_head == other_head, 1.0 / HEAD_DIM, 0.0).astype(jnp.bfloat16)


def head_mean(values, average):
    coarse = values.astype(jnp.bfloat16)
    fine = (values - coarse.astype(jnp.float32)).astype(jnp.bfloat16)
    return nn(coarse, average) + nn(fine, average)


def normalized(pixels, adaptive):
    inverse = lax.rsqrt(jnp.mean(pixels * pixels, axis=-1, keepdims=True) + epsilon)
    return inverse, (pixels * inverse * adaptive).astype(jnp.bfloat16)


def project_to(pixels, adaptive, qkv_ref, average, query_ref, key_ref, value_ref, here):
    width = pixels.shape[-1]
    shape = (-1,) + query_ref.shape[1:]
    inverse, normed = normalized(pixels, adaptive)
    project = nn(normed, qkv_ref[...])
    query_raw = project[:, :width]
    key_raw = project[:, width : 2 * width]
    query_inv = lax.rsqrt(head_mean(query_raw * query_raw, average) + epsilon)
    key_inv = lax.rsqrt(head_mean(key_raw * key_raw, average) + epsilon)
    factor = score_scale / HEAD_DIM
    query_ref[here] = (query_raw * query_inv * factor).astype(jnp.bfloat16).reshape(shape)
    key_ref[here] = (key_raw * key_inv).astype(jnp.bfloat16).reshape(shape)
    value_ref[here] = project[:, 2 * width :].astype(jnp.bfloat16).reshape(shape)
    return inverse, normed, query_raw, query_inv, key_raw, key_inv


def own_kernel(
    total_rows,
    place_ref,
    tok_ref,
    cot_ref,
    adaptive_ref,
    qkv_ref,
    out_ref,
    query_ref,
    key_ref,
    value_ref,
    grad_ref,
    mask_ref,
    query_raw_ref,
    query_inv_ref,
    key_raw_ref,
    key_inv_ref,
):
    cols, rows, width = tok_ref.shape
    lanes = mask_ref.shape[2]
    row_first = place_ref[0]
    pixels = tok_ref[...].astype(jnp.float32).reshape(cols * rows, width)
    _, _, query_raw, query_inv, key_raw, key_inv = project_to(
        pixels, adaptive_ref[...], qkv_ref, average_matrix(width), query_ref, key_ref, value_ref, pl.ds(0, cols)
    )
    query_raw_ref[...] = query_raw
    query_inv_ref[...] = query_inv
    key_raw_ref[...] = key_raw
    key_inv_ref[...] = key_inv
    cot_own = cot_ref[...].reshape(cols * rows, width)
    grad_ref[...] = nt(cot_own, out_ref[...]).astype(jnp.bfloat16).reshape(cols, rows, width)

    shape = (WINDOW, rows, lanes)
    key_row = lax.broadcasted_iota(jnp.int32, shape, 1)
    key_col = lax.broadcasted_iota(jnp.int32, shape, 0)
    lane = lax.broadcasted_iota(jnp.int32, (1, 1, lanes), 2) % (SPAN * rows)
    query_col = lane // rows
    query_row = lane % rows
    row_gap = key_row - query_row
    col_gap = key_col - query_col
    image_row = row_first + key_row - REACH
    allowed = (row_gap >= -RADIUS) & (row_gap <= RADIUS) & (col_gap >= 0) & (col_gap <= REACH)
    allowed = allowed & (image_row >= 0) & (image_row < total_rows)
    mask_ref[...] = jnp.where(allowed, 1.0, 0.0)


def block_kernel(
    sizes,
    place_ref,
    tok_ref,
    cot_ref,
    low_ref,
    high_ref,
    adaptive_ref,
    qkv_ref,
    out_ref,
    own_query_ref,
    own_key_ref,
    own_value_ref,
    own_grad_ref,
    mask_ref,
    query_raw_ref,
    query_inv_ref,
    key_raw_ref,
    key_inv_ref,
    result_ref,
    grad_tokens_ref,
    mine_ref,
    other_ref,
    query_ref,
    key_ref,
    value_ref,
    grad_ref,
    attended_ref,
    grad_query_ref,
    grad_key_ref,
    grad_value_ref,
    whole_ref,
):
    height, total_cols = sizes
    cols, rows, width = tok_ref.shape
    heads = width // HEAD_DIM
    query_cols = cols + REACH
    lanes = heads * SPAN * rows
    col_first = place_ref[1]
    image = place_ref[2]
    core = place_ref[3]
    step_value = place_ref[4]
    adaptive = adaptive_ref[...]
    factor = score_scale / HEAD_DIM
    average = average_matrix(width)

    for ref, first in ((low_ref, 0), (high_ref, REACH + cols)):
        pixels = ref[:REACH].astype(jnp.float32).reshape(REACH * rows, width)
        project_to(pixels, adaptive, qkv_ref, average, query_ref, key_ref, value_ref, pl.ds(first, REACH))
    query_ref[pl.ds(REACH, cols)] = own_query_ref[...]
    key_ref[pl.ds(REACH, cols)] = own_key_ref[...]
    value_ref[pl.ds(REACH, cols)] = own_value_ref[...]
    grad_ref[pl.ds(RADIUS, cols)] = own_grad_ref[...]
    for ref, first in ((low_ref, 0), (high_ref, RADIUS + cols)):
        side = ref[REACH:].reshape(RADIUS * rows, width)
        grad_ref[pl.ds(first, RADIUS)] = nt(side, out_ref[...]).astype(jnp.bfloat16).reshape(RADIUS, rows, width)

    grad_key_ref[...] = jnp.zeros_like(grad_key_ref)
    grad_value_ref[...] = jnp.zeros_like(grad_value_ref)
    lane_head = lax.broadcasted_iota(jnp.int32, (1, width), 1) // HEAD_DIM
    picks = [jnp.where(lane_head == head, 1.0, 0.0) for head in range(heads)]
    narrow = [pick.astype(jnp.bfloat16) for pick in picks]
    column = lax.broadcasted_iota(jnp.int32, (WINDOW, 1, 1), 0)

    def spread(values):
        return jnp.concatenate([values * pick for pick in narrow], axis=0)

    def gathered(values):
        total = values[: SPAN * rows] * picks[0]
        for head in range(1, heads):
            total = total + values[head * SPAN * rows : (head + 1) * SPAN * rows] * picks[head]
        return total

    def step(index, carry):
        start = SPAN * index
        near = pl.ds(start, WINDOW)
        keys = key_ref[near].reshape(WINDOW * rows, width)
        values = value_ref[near].reshape(WINDOW * rows, width)
        queries = spread(query_ref[pl.ds(start + RADIUS, SPAN)].reshape(SPAN * rows, width))
        grads = spread(grad_ref[pl.ds(start, SPAN)].reshape(SPAN * rows, width))
        image_col = col_first + start + column - REACH
        inside = jnp.where((image_col >= 0) & (image_col < total_cols), 1.0, 0.0)
        mask = (mask_ref[...] * inside).reshape(WINDOW * rows, lanes)
        exponent = jnp.exp(nt(keys, queries) - score_scale) * mask
        denominator = jnp.maximum(jnp.sum(exponent, axis=0, keepdims=True), 1e-30)
        weights = (exponent * (1.0 / denominator)).astype(jnp.bfloat16)
        wide = weights.astype(jnp.float32)
        slope = nt(values, grads)
        middle = jnp.sum(wide * slope, axis=0, keepdims=True)
        grad_score = (wide * (slope - middle)).astype(jnp.bfloat16)
        attended = gathered(tn(weights, values)).astype(jnp.bfloat16)
        attended_ref[pl.ds(start, SPAN)] = attended.reshape(SPAN, rows, width)
        grad_query_ref[pl.ds(start, SPAN)] = gathered(tn(grad_score, keys)).reshape(SPAN, rows, width)
        grad_key_ref[near] += nn(grad_score, queries).reshape(WINDOW, rows, width)
        grad_value_ref[near] += nn(weights, grads).reshape(WINDOW, rows, width)
        return carry

    lax.fori_loop(0, query_cols // SPAN, step, 0)

    pixels = tok_ref[...].astype(jnp.float32).reshape(cols * rows, width)
    inverse, normed = normalized(pixels, adaptive)
    cot_own = cot_ref[...].reshape(cols * rows, width)
    row = lax.broadcasted_iota(jnp.int32, (cols, rows, 1), 1)
    own = jnp.where((row >= REACH) & (row < REACH + height), 1.0, 0.0).reshape(cols * rows, 1)
    attended = attended_ref[pl.ds(RADIUS, cols)].reshape(cols * rows, width)
    result = pixels + nn(attended, out_ref[...])
    result_ref[...] = result.astype(jnp.bfloat16).reshape(cols, rows, width)
    cotan = cot_own.astype(jnp.float32)
    whole_ref[:, 3 * width :] = tn(attended, (cotan * own).astype(jnp.bfloat16))

    def back(raw, inv, grad, scale):
        return scale * inv * (grad - raw * inv * inv * head_mean(grad * raw, average))

    grad_query = grad_query_ref[pl.ds(RADIUS, cols)].reshape(cols * rows, width)
    grad_key = grad_key_ref[pl.ds(REACH, cols)].reshape(cols * rows, width)
    grad_value = grad_value_ref[pl.ds(REACH, cols)].reshape(cols * rows, width)
    grad_project = jnp.concatenate(
        [
            (back(query_raw_ref[...], query_inv_ref[...], grad_query, factor) * own).astype(jnp.bfloat16),
            (back(key_raw_ref[...], key_inv_ref[...], grad_key, 1.0) * own).astype(jnp.bfloat16),
            (grad_value * own).astype(jnp.bfloat16),
        ],
        axis=1,
    )
    whole_ref[:, : 3 * width] = tn(normed, grad_project)
    grad_normed = nt(grad_project, qkv_ref[...])
    scaled = grad_normed * adaptive
    inner = jnp.mean(scaled * pixels, axis=-1, keepdims=True)
    grad_pixels = inverse * (scaled - pixels * (inverse * inverse * inner))
    grad_tokens_ref[...] = (cotan + grad_pixels).astype(jnp.bfloat16).reshape(cols, rows, width)
    grad_adaptive = jnp.sum(grad_normed * (pixels * inverse), axis=0, keepdims=True)

    half = width // CORES
    across = 4 * width // LANES
    blocks = mine_ref.shape[0]
    line = lax.broadcasted_iota(jnp.int32, (SLOT, LANES), 0)
    lane = lax.broadcasted_iota(jnp.int32, (SLOT, LANES), 1)
    high = (step_value // 32).astype(jnp.float32)
    low = (step_value % 32).astype(jnp.float32)
    for ref, which in ((mine_ref, core), (other_ref, 1 - core)):
        part = whole_ref[pl.ds(pl.multiple_of(which * half, half), half), :].astype(jnp.bfloat16)
        for block in range(blocks):
            top = block // across * LINES
            first = block % across * LANES
            ref[block, :LINES] = part[top : top + LINES, first : first + LANES]
            if block < width // LANES:
                side = jnp.where(line == image, grad_adaptive[:, block * LANES : (block + 1) * LANES], 0.0)
                if block == 0:
                    there = line == SLOT // 2 + image
                    side = jnp.where(there & (lane == 0), high, side)
                    side = jnp.where(there & (lane == 1), low, side)
                ref[block, LINES:] = side.astype(jnp.bfloat16)
            else:
                ref[block, LINES:] = jnp.zeros((SLOT, LANES), jnp.bfloat16)


def finish_kernel(senders, place_ref, mine_ref, other_ref, qkv_ref, output_ref, time_ref):
    width = output_ref.shape[0]
    images = senders[0]
    half = width // CORES
    across = 4 * width // LANES
    core = place_ref[3]
    for ref, which in ((mine_ref, core), (other_ref, 1 - core)):
        for block in range(mine_ref.shape[0]):
            top = pl.multiple_of(which * half, half) + block // across * LINES
            first = block % across * LANES
            values = ref[block, :LINES].astype(jnp.float32)
            if first < 3 * width:
                qkv_ref[pl.ds(top, LINES), first : first + LANES] = values
            else:
                output_ref[pl.ds(top, LINES), first - 3 * width : first - 3 * width + LANES] = values
    sides = [mine_ref[block, LINES:].astype(jnp.float32) for block in range(width // LANES)]
    adaptives = jnp.concatenate(sides, axis=1)
    adaptives = jnp.where(lax.broadcasted_iota(jnp.int32, adaptives.shape, 0) < images, adaptives, 0.0)
    ladder = lax.broadcasted_iota(jnp.int32, (1, CF // 2), 1).astype(jnp.float32)
    frequency = jnp.exp(ladder * (-math.log(1000.0) / (CF // 2)))
    steps = (sides[0][:, 0:1] * 32.0 + sides[0][:, 1:2]) / senders[1]
    steps = jnp.concatenate([steps[SLOT // 2 :], steps[: SLOT // 2] * 0.0], axis=0)
    angle = steps * frequency
    features = jnp.concatenate([jnp.cos(angle), jnp.sin(angle)], axis=1)
    time_ref[...] = lax.dot_general(
        features,
        adaptives,
        (((0,), (0,)), ((), ())),
        precision=lax.Precision.HIGHEST,
        preferred_element_type=jnp.float32,
    )


CORES = 2
SLOT = 8
LINES = 32
LANES = 128


def on_device(tokens, timesteps, cotangent, qkv_weight, output_weight, time_weight):
    height, cols, width = tokens.shape[1:]
    row_first = lax.axis_index("row") * height
    col_first = lax.axis_index("col") * cols
    total_rows = height * lax.axis_size("row")
    total_cols = cols * lax.axis_size("col")
    tok = tokens[0].transpose(1, 0, 2)
    cot = cotangent[0].transpose(1, 0, 2)
    both = jnp.concatenate([tok, cot], axis=0)
    above, below = exchange(both[:, height - REACH :], both[:, :REACH], "row")
    rows = -(-(height + 2 * REACH) // 16) * 16
    blank = jnp.zeros((2 * cols, rows - height - 2 * REACH, width), jnp.bfloat16)
    both = jnp.concatenate([above, both, below, blank], axis=1)
    tok, cot = both[:cols], both[cols:]
    to_next = jnp.concatenate([tok[cols - REACH :], cot[cols - RADIUS :]], axis=0)
    to_previous = jnp.concatenate([tok[:REACH], cot[:RADIUS]], axis=0)
    left, right = exchange(to_next, to_previous, "col")
    features = fourier(timesteps[0])
    adaptive = 1.0 + jnp.dot(
        features[None], time_weight.astype(jnp.float32), precision=lax.Precision.HIGHEST
    )
    image = lax.axis_index(("zone", "core"))
    place = [row_first, col_first, image, lax.axis_index("core"), timesteps[0]]
    place = jnp.stack(place).astype(jnp.int32)

    around = cols + 2 * REACH
    query_cols = cols + REACH
    lanes = width // HEAD_DIM * SPAN * rows
    smem = pl.BlockSpec(memory_space=pltpu.SMEM)
    vmem = pl.BlockSpec(memory_space=pltpu.VMEM)
    limits = pltpu.CompilerParams(vmem_limit_bytes=40 * 2**20)
    block = jax.ShapeDtypeStruct((cols, rows, width), jnp.bfloat16)
    flat = jax.ShapeDtypeStruct((cols * rows, width), jnp.float32)
    prepared = pl.pallas_call(
        functools.partial(own_kernel, total_rows),
        out_shape=(block,) * 4 + (jax.ShapeDtypeStruct((WINDOW, rows, lanes), jnp.float32),) + (flat,) * 4,
        in_specs=[smem] + [vmem] * 5,
        out_specs=(vmem,) * 9,
        compiler_params=limits,
        cost_estimate=pl.CostEstimate(flops=1_000_000_000, bytes_accessed=4_000_000, transcendentals=200_000),
        name="own",
    )(place, tok, cot, adaptive, qkv_weight, output_weight)
    pieces = width // CORES // LINES * (4 * width // LANES)
    chunks = jax.ShapeDtypeStruct((pieces, LINES + SLOT, LANES), jnp.bfloat16)
    wide = pltpu.VMEM((around, rows, width), jnp.bfloat16)
    result, grad_tokens, mine, other = pl.pallas_call(
        functools.partial(block_kernel, (height, total_cols)),
        out_shape=(block, block, chunks, chunks),
        in_specs=[smem] + [vmem] * 16,
        out_specs=(vmem,) * 4,
        scratch_shapes=[
            wide,
            wide,
            wide,
            pltpu.VMEM((query_cols, rows, width), jnp.bfloat16),
            pltpu.VMEM((query_cols, rows, width), jnp.bfloat16),
            pltpu.VMEM((query_cols, rows, width), jnp.float32),
            pltpu.VMEM((around, rows, width), jnp.float32),
            pltpu.VMEM((around, rows, width), jnp.float32),
            pltpu.VMEM((width, 4 * width), jnp.float32),
        ],
        compiler_params=limits,
        cost_estimate=pl.CostEstimate(flops=8_000_000_000, bytes_accessed=4_000_000, transcendentals=1_000_000),
        name="block",
    )(place, tok, cot, left, right, adaptive, qkv_weight, output_weight, *prepared)
    result = result[:, REACH : REACH + height].transpose(1, 0, 2)
    grad_tokens = grad_tokens[:, REACH : REACH + height].transpose(1, 0, 2)

    mine, other = summed(mine, other)
    total_qkv, total_output, total_time = pl.pallas_call(
        functools.partial(finish_kernel, (lax.axis_size("zone") * CORES, lax.axis_size("row") * lax.axis_size("col"))),
        out_shape=(
            jax.ShapeDtypeStruct((width, 3 * width), jnp.float32),
            jax.ShapeDtypeStruct((width, width), jnp.float32),
            jax.ShapeDtypeStruct((CF, width), jnp.float32),
        ),
        in_specs=[smem, vmem, vmem],
        out_specs=(vmem,) * 3,
        name="finish",
    )(place, mine, other)
    return (result[None], grad_tokens[None], total_qkv, total_output, total_time)


def swap(pieces, axes):
    return lax.all_to_all(pieces, axes, 0, 0, tiled=True)


def total(pieces):
    return jnp.sum(pieces.astype(jnp.float32), axis=0).astype(jnp.bfloat16)


def copied(piece, axes):
    count = lax.axis_size(axes)
    return lax.optimization_barrier(jnp.broadcast_to(piece[None], (count,) + piece.shape))


def summed(mine, other):
    partner = [(0, 1), (1, 0)]
    mine = total(jnp.stack([mine, lax.ppermute(other, "core", partner)]))
    piece = total(swap(mine, "col"))
    piece = total(swap(copied(piece, ("zone", "row")), ("zone", "row")))
    mine = swap(copied(piece, "col"), "col")
    return mine, lax.ppermute(mine, "core", partner)


def solution(mesh):
    shape = (mesh.shape["dp"] // CORES, CORES, mesh.shape["row"], mesh.shape["col"])
    mesh = jax.sharding.Mesh(mesh.devices.reshape(shape), ("zone", "core", "row", "col"))
    grid = P(("zone", "core"), "row", "col", None)
    in_specs = (grid, P(("zone", "core")), grid, P(), P(), P())
    out_specs = (grid, grid, P(), P(), P())
    return jax.shard_map(
        on_device, mesh=mesh, in_specs=in_specs, out_specs=out_specs, check_vma=False
    )
```

```python
import functools
import math

import jax
import jax.numpy as jnp
from jax import lax
from jax.experimental import pallas as pl
from jax.experimental.pallas import tpu as pltpu
from jax.sharding import PartitionSpec as P

HEAD_DIM = 64
CF = 256
RADIUS = 3
REACH = 2 * RADIUS
EDGE = 8
SPAN = 2
WINDOW = SPAN + REACH

score_scale = 6.0
epsilon = 1e-06


def fourier(step_value):
    half_count = CF // 2
    ladder = jnp.arange(half_count, dtype=jnp.float32)
    frequency = jnp.exp(ladder * (-math.log(1000.0) / half_count))
    phase_angle = step_value.astype(jnp.float32) * frequency
    return jnp.concatenate([jnp.cos(phase_angle), jnp.sin(phase_angle)])


def shifted(block, row_step, col_step):
    down = lax.axis_size("row")
    across = lax.axis_size("col")
    pairs = [
        (row * across + col, (row + row_step) * across + col + col_step)
        for row in range(down)
        for col in range(across)
        if 0 <= row + row_step < down and 0 <= col + col_step < across
    ]
    return lax.ppermute(block, ("row", "col"), pairs)


def nn(left, right):
    return lax.dot_general(left, right, (((1,), (0,)), ((), ())), preferred_element_type=jnp.float32)


def nt(left, right):
    return lax.dot_general(left, right, (((1,), (1,)), ((), ())), preferred_element_type=jnp.float32)


def tn(left, right):
    return lax.dot_general(left, right, (((0,), (0,)), ((), ())), preferred_element_type=jnp.float32)


def average_matrix(width):
    own_head = lax.broadcasted_iota(jnp.int32, (width, width), 0) // HEAD_DIM
    other_head = lax.broadcasted_iota(jnp.int32, (width, width), 1) // HEAD_DIM
    return jnp.where(own_head == other_head, 1.0 / HEAD_DIM, 0.0).astype(jnp.bfloat16)


def head_mean(values, average):
    coarse = values.astype(jnp.bfloat16)
    fine = (values - coarse.astype(jnp.float32)).astype(jnp.bfloat16)
    return nn(coarse, average) + nn(fine, average)


def normalized(pixels, adaptive):
    inverse = lax.rsqrt(jnp.mean(pixels * pixels, axis=-1, keepdims=True) + epsilon)
    return inverse, (pixels * inverse * adaptive).astype(jnp.bfloat16)


def projected(pixels, adaptive, qkv_ref, average):
    width = pixels.shape[-1]
    inverse, normed = normalized(pixels, adaptive)
    project = nn(normed, qkv_ref[...])
    query_raw = project[:, :width]
    key_raw = project[:, width : 2 * width]
    query_inv = lax.rsqrt(head_mean(query_raw * query_raw, average) + epsilon)
    key_inv = lax.rsqrt(head_mean(key_raw * key_raw, average) + epsilon)
    query = query_raw * query_inv * (score_scale / HEAD_DIM)
    return inverse, normed, query, key_raw * key_inv, project[:, 2 * width :], (query_raw, query_inv, key_raw, key_inv)


def own_kernel(
    total_rows,
    place_ref,
    tok_ref,
    cot_ref,
    adaptive_ref,
    qkv_ref,
    out_ref,
    query_ref,
    key_ref,
    value_ref,
    grad_ref,
    mask_ref,
    query_raw_ref,
    query_inv_ref,
    key_raw_ref,
    key_inv_ref,
):
    cols, height, width = tok_ref.shape
    _, rows, lanes = mask_ref.shape
    row_first = place_ref[0]
    pixels = tok_ref[...].astype(jnp.float32).reshape(cols * height, width)
    _, _, query, key, value, raw = projected(pixels, adaptive_ref[...], qkv_ref, average_matrix(width))
    query_ref[...] = query.astype(jnp.bfloat16).reshape(cols, height, width)
    key_ref[...] = key.astype(jnp.bfloat16).reshape(cols, height, width)
    value_ref[...] = value.astype(jnp.bfloat16).reshape(cols, height, width)
    for ref, values in zip((query_raw_ref, query_inv_ref, key_raw_ref, key_inv_ref), raw):
        ref[...] = values
    cot_own = cot_ref[...].reshape(cols * height, width)
    grad_ref[...] = nt(cot_own, out_ref[...]).astype(jnp.bfloat16).reshape(cols, height, width)

    def row_at(position):
        halo = jnp.where(position < height + EDGE, position - height - EDGE, position - EDGE)
        return jnp.where(position < height, position, halo)

    key_row = row_at(lax.broadcasted_iota(jnp.int32, (1, rows, 1), 1))
    key_col = lax.broadcasted_iota(jnp.int32, (WINDOW, 1, 1), 0)
    lane = lax.broadcasted_iota(jnp.int32, (1, 1, lanes), 2) % (SPAN * rows)
    query_row = row_at(lane % rows)
    query_col = lane // rows
    row_gap = key_row - query_row
    col_gap = key_col - query_col
    image_row = jnp.broadcast_to(row_first + key_row, row_gap.shape)
    near_row = (row_gap >= -RADIUS) & (row_gap <= RADIUS) & (image_row >= 0) & (image_row < total_rows)
    near_col = (col_gap >= 0) & (col_gap <= REACH)
    mask_ref[...] = jnp.where(near_row, 1.0, 0.0) * jnp.where(near_col, 1.0, 0.0)


def block_kernel(
    total_cols,
    place_ref,
    tok_ref,
    cot_ref,
    above_ref,
    below_ref,
    left_ref,
    left_above_ref,
    left_below_ref,
    right_ref,
    right_above_ref,
    right_below_ref,
    adaptive_ref,
    qkv_ref,
    out_ref,
    own_query_ref,
    own_key_ref,
    own_value_ref,
    own_grad_ref,
    mask_ref,
    query_raw_ref,
    query_inv_ref,
    key_raw_ref,
    key_inv_ref,
    result_ref,
    grad_tokens_ref,
    mine_ref,
    other_ref,
    query_ref,
    key_ref,
    value_ref,
    grad_ref,
    attended_ref,
    grad_query_ref,
    grad_key_ref,
    grad_value_ref,
    whole_ref,
):
    cols, height, width = tok_ref.shape
    rows = mask_ref.shape[1]
    heads = width // HEAD_DIM
    query_cols = cols + REACH
    col_first = place_ref[1]
    image = place_ref[2]
    core = place_ref[3]
    step_value = place_ref[4]
    adaptive = adaptive_ref[...]
    factor = score_scale / HEAD_DIM
    average = average_matrix(width)

    last = REACH + cols
    pieces = (
        (left_ref, REACH, 0, 0),
        (right_ref, REACH, last, 0),
        (above_ref, cols, REACH, height),
        (below_ref, cols, REACH, height + EDGE),
        (left_above_ref, REACH, 0, height),
        (left_below_ref, REACH, 0, height + EDGE),
        (right_above_ref, REACH, last, height),
        (right_below_ref, REACH, last, height + EDGE),
    )

    def place_rows(values, targets):
        first = 0
        for ref, count, tall, col, row in targets:
            part = values[first : first + count * tall].reshape(count, tall, width)
            ref[pl.ds(col, count), pl.ds(row, tall)] = part.astype(jnp.bfloat16)
            first += count * tall

    for group in (pieces[:2], pieces[2:]):
        pixels = jnp.concatenate(
            [ref[:count].astype(jnp.float32).reshape(count * ref.shape[1], width) for ref, count, _, _ in group], axis=0
        )
        _, _, query, key, value, _ = projected(pixels, adaptive, qkv_ref, average)
        for values, target in ((query, query_ref), (key, key_ref), (value, value_ref)):
            place_rows(values, [(target, count, ref.shape[1], col, row) for ref, count, col, row in group])
    sides = []
    targets = []
    for ref, count, col, row in pieces:
        tall = ref.shape[1]
        sides.append(ref[count:].astype(jnp.float32).reshape(-1, width))
        targets.append((grad_ref, ref.shape[0] - count, tall, 0 if col == 0 else col - RADIUS, row))
    side = jnp.concatenate(sides, axis=0).astype(jnp.bfloat16)
    place_rows(nt(side, out_ref[...]), targets)
    for target, source, col in (
        (query_ref, own_query_ref, REACH),
        (key_ref, own_key_ref, REACH),
        (value_ref, own_value_ref, REACH),
        (grad_ref, own_grad_ref, RADIUS),
    ):
        target[pl.ds(col, cols), pl.ds(0, height)] = source[...]

    grad_key_ref[...] = jnp.zeros_like(grad_key_ref)
    grad_value_ref[...] = jnp.zeros_like(grad_value_ref)
    lane_head = lax.broadcasted_iota(jnp.int32, (1, width), 1) // HEAD_DIM
    picks = [jnp.where(lane_head == head, 1.0, 0.0) for head in range(heads)]
    narrow = [pick.astype(jnp.bfloat16) for pick in picks]

    def spread(values):
        return jnp.concatenate([values * pick for pick in narrow], axis=0)

    def gathered(values):
        total = values[: SPAN * rows] * picks[0]
        for head in range(1, heads):
            total = total + values[head * SPAN * rows : (head + 1) * SPAN * rows] * picks[head]
        return total.reshape(SPAN, rows, width)[:, :height]

    for start in range(0, query_cols, SPAN):
        near = pl.ds(start, WINDOW)
        keys = key_ref[near].reshape(WINDOW * rows, width)
        values = value_ref[near].reshape(WINDOW * rows, width)
        queries = spread(query_ref[pl.ds(start + RADIUS, SPAN)].reshape(SPAN * rows, width))
        grads = spread(grad_ref[pl.ds(start, SPAN)].reshape(SPAN * rows, width))
        masks = []
        for column in range(WINDOW):
            mask = mask_ref[column]
            if start + column < REACH or start + column >= last:
                image_col = col_first + (start + column - REACH)
                mask = mask * jnp.where((image_col >= 0) & (image_col < total_cols), 1.0, 0.0)
            masks.append(mask)
        exponent = jnp.exp(nt(keys, queries) - score_scale) * jnp.concatenate(masks, axis=0)
        denominator = jnp.maximum(jnp.sum(exponent, axis=0, keepdims=True), 1e-30)
        weights = (exponent * (1.0 / denominator)).astype(jnp.bfloat16)
        wide = weights.astype(jnp.float32)
        slope = nt(values, grads)
        middle = jnp.sum(wide * slope, axis=0, keepdims=True)
        grad_score = (wide * (slope - middle)).astype(jnp.bfloat16)
        low = max(start + RADIUS, REACH)
        high = min(start + RADIUS + SPAN, last)
        if low < high:
            skip = slice(low - start - RADIUS, high - start - RADIUS)
            there = pl.ds(low - REACH, high - low)
            attended_ref[there] = gathered(tn(weights, values))[skip].astype(jnp.bfloat16)
            grad_query_ref[there] = gathered(tn(grad_score, keys))[skip]
        low = max(start, REACH)
        high = min(start + WINDOW, last)
        there = pl.ds(low - REACH, high - low)
        shape = (WINDOW, rows, heads * SPAN * rows)
        kept = (high - low, height, width)
        kept_score = grad_score.reshape(shape)[low - start : high - start, :height].reshape(-1, shape[2])
        kept_weights = weights.reshape(shape)[low - start : high - start, :height].reshape(-1, shape[2])
        grad_key_ref[there] += nn(kept_score, queries).reshape(kept)
        grad_value_ref[there] += nn(kept_weights, grads).reshape(kept)

    tokens = cols * height
    pixels = tok_ref[...].astype(jnp.float32).reshape(tokens, width)
    inverse, normed = normalized(pixels, adaptive)
    cot_own = cot_ref[...].reshape(tokens, width)
    attended = attended_ref[...].reshape(tokens, width)
    result = pixels + nn(attended, out_ref[...])
    result_ref[...] = result.astype(jnp.bfloat16).reshape(cols, height, width)
    whole_ref[:, 3 * width :] = tn(attended, cot_own)

    def back(raw, inv, grad, scale):
        return scale * inv * (grad - raw * inv * inv * head_mean(grad * raw, average))

    grad_query = grad_query_ref[...].reshape(tokens, width)
    grad_key = grad_key_ref[...].reshape(tokens, width)
    grad_project = jnp.concatenate(
        [
            back(query_raw_ref[...], query_inv_ref[...], grad_query, factor).astype(jnp.bfloat16),
            back(key_raw_ref[...], key_inv_ref[...], grad_key, 1.0).astype(jnp.bfloat16),
            grad_value_ref[...].reshape(tokens, width).astype(jnp.bfloat16),
        ],
        axis=1,
    )
    whole_ref[:, : 3 * width] = tn(normed, grad_project)
    grad_normed = nt(grad_project, qkv_ref[...])
    scaled = grad_normed * adaptive
    inner = jnp.mean(scaled * pixels, axis=-1, keepdims=True)
    grad_pixels = inverse * (scaled - pixels * (inverse * inverse * inner))
    grad_tokens = cot_own.astype(jnp.float32) + grad_pixels
    grad_tokens_ref[...] = grad_tokens.astype(jnp.bfloat16).reshape(cols, height, width)
    grad_adaptive = jnp.sum(grad_normed * (pixels * inverse), axis=0, keepdims=True)

    half = width // CORES
    across = 4 * width // LANES
    line = lax.broadcasted_iota(jnp.int32, (SLOT, LANES), 0)
    lane = lax.broadcasted_iota(jnp.int32, (SLOT, LANES), 1)
    high = (step_value // 32).astype(jnp.float32)
    low = (step_value % 32).astype(jnp.float32)
    for ref, which in ((mine_ref, core), (other_ref, 1 - core)):
        part = whole_ref[pl.ds(pl.multiple_of(which * half, half), half), :].astype(jnp.bfloat16)
        for block in range(ref.shape[0]):
            top = block // across * LINES
            first = block % across * LANES
            ref[block, :LINES] = part[top : top + LINES, first : first + LANES]
            if block < width // LANES:
                side = jnp.where(line == image, grad_adaptive[:, block * LANES : (block + 1) * LANES], 0.0)
                if block == 0:
                    there = line == SLOT // 2 + image
                    side = jnp.where(there & (lane == 0), high, side)
                    side = jnp.where(there & (lane == 1), low, side)
                ref[block, LINES:] = side.astype(jnp.bfloat16)
            else:
                ref[block, LINES:] = jnp.zeros((SLOT, LANES), jnp.bfloat16)


def finish_kernel(senders, place_ref, mine_ref, other_ref, qkv_ref, output_ref, time_ref):
    width = output_ref.shape[0]
    images = senders[0]
    half = width // CORES
    across = 4 * width // LANES
    core = place_ref[3]
    for ref, which in ((mine_ref, core), (other_ref, 1 - core)):
        for block in range(mine_ref.shape[0]):
            top = pl.multiple_of(which * half, half) + block // across * LINES
            first = block % across * LANES
            values = ref[block, :LINES].astype(jnp.float32)
            if first < 3 * width:
                qkv_ref[pl.ds(top, LINES), first : first + LANES] = values
            else:
                output_ref[pl.ds(top, LINES), first - 3 * width : first - 3 * width + LANES] = values
    sides = [mine_ref[block, LINES:].astype(jnp.float32) for block in range(width // LANES)]
    adaptives = jnp.concatenate(sides, axis=1)
    adaptives = jnp.where(lax.broadcasted_iota(jnp.int32, adaptives.shape, 0) < images, adaptives, 0.0)
    ladder = lax.broadcasted_iota(jnp.int32, (1, CF // 2), 1).astype(jnp.float32)
    frequency = jnp.exp(ladder * (-math.log(1000.0) / (CF // 2)))
    steps = (sides[0][:, 0:1] * 32.0 + sides[0][:, 1:2]) / senders[1]
    steps = jnp.concatenate([steps[SLOT // 2 :], steps[: SLOT // 2] * 0.0], axis=0)
    angle = steps * frequency
    features = jnp.concatenate([jnp.cos(angle), jnp.sin(angle)], axis=1)
    time_ref[...] = lax.dot_general(
        features,
        adaptives,
        (((0,), (0,)), ((), ())),
        precision=lax.Precision.HIGHEST,
        preferred_element_type=jnp.float32,
    )


CORES = 2
SLOT = 8
LINES = 32
LANES = 128


def on_device(tokens, timesteps, cotangent, qkv_weight, output_weight, time_weight):
    height, cols, width = tokens.shape[1:]
    row_first = lax.axis_index("row") * height
    col_first = lax.axis_index("col") * cols
    total_rows = height * lax.axis_size("row")
    total_cols = cols * lax.axis_size("col")
    tok = tokens[0].transpose(1, 0, 2)
    cot = cotangent[0].transpose(1, 0, 2)
    rows = height + 2 * EDGE
    to_right = jnp.concatenate([tok[cols - REACH :], cot[cols - RADIUS :]], axis=0)
    to_left = jnp.concatenate([tok[:REACH], cot[:RADIUS]], axis=0)
    both = jnp.concatenate([tok, cot], axis=0)
    left = shifted(to_right, 0, 1)
    right = shifted(to_left, 0, -1)
    above = shifted(both[:, height - EDGE :], 1, 0)
    below = shifted(both[:, :EDGE], -1, 0)
    left_above = shifted(to_right[:, height - EDGE :], 1, 1)
    left_below = shifted(to_right[:, :EDGE], -1, 1)
    right_above = shifted(to_left[:, height - EDGE :], 1, -1)
    right_below = shifted(to_left[:, :EDGE], -1, -1)
    halos = (above, below, left, left_above, left_below, right, right_above, right_below)
    features = fourier(timesteps[0])
    adaptive = 1.0 + jnp.dot(
        features[None], time_weight.astype(jnp.float32), precision=lax.Precision.HIGHEST
    )
    image = lax.axis_index(("zone", "core"))
    place = [row_first, col_first, image, lax.axis_index("core"), timesteps[0]]
    place = jnp.stack(place).astype(jnp.int32)

    around = cols + 2 * REACH
    query_cols = cols + REACH
    lanes = width // HEAD_DIM * SPAN * rows
    smem = pl.BlockSpec(memory_space=pltpu.SMEM)
    vmem = pl.BlockSpec(memory_space=pltpu.VMEM)
    limits = pltpu.CompilerParams(vmem_limit_bytes=40 * 2**20)
    block = jax.ShapeDtypeStruct((cols, height, width), jnp.bfloat16)
    flat = jax.ShapeDtypeStruct((cols * height, width), jnp.float32)
    prepared = pl.pallas_call(
        functools.partial(own_kernel, total_rows),
        out_shape=(block,) * 4 + (jax.ShapeDtypeStruct((WINDOW, rows, lanes), jnp.float32),) + (flat,) * 4,
        in_specs=[smem] + [vmem] * 5,
        out_specs=(vmem,) * 9,
        compiler_params=limits,
        cost_estimate=pl.CostEstimate(flops=1_000_000_000, bytes_accessed=4_000_000, transcendentals=200_000),
        name="own",
    )(place, tok, cot, adaptive, qkv_weight, output_weight)
    pieces = width // CORES // LINES * (4 * width // LANES)
    chunks = jax.ShapeDtypeStruct((pieces, LINES + SLOT, LANES), jnp.bfloat16)
    wide = pltpu.VMEM((around, rows, width), jnp.bfloat16)
    result, grad_tokens, mine, other = pl.pallas_call(
        functools.partial(block_kernel, total_cols),
        out_shape=(block, block, chunks, chunks),
        in_specs=[smem] + [vmem] * 22,
        out_specs=(vmem,) * 4,
        scratch_shapes=[
            wide,
            wide,
            wide,
            pltpu.VMEM((query_cols, rows, width), jnp.bfloat16),
            pltpu.VMEM((cols, height, width), jnp.bfloat16),
            pltpu.VMEM((cols, height, width), jnp.float32),
            pltpu.VMEM((cols, height, width), jnp.float32),
            pltpu.VMEM((cols, height, width), jnp.float32),
            pltpu.VMEM((width, 4 * width), jnp.float32),
        ],
        compiler_params=limits,
        cost_estimate=pl.CostEstimate(flops=8_000_000_000, bytes_accessed=4_000_000, transcendentals=1_000_000),
        name="block",
    )(place, tok, cot, *halos, adaptive, qkv_weight, output_weight, *prepared)
    result = result.transpose(1, 0, 2)
    grad_tokens = grad_tokens.transpose(1, 0, 2)

    mine, other = summed(mine, other)
    total_qkv, total_output, total_time = pl.pallas_call(
        functools.partial(finish_kernel, (lax.axis_size("zone") * CORES, lax.axis_size("row") * lax.axis_size("col"))),
        out_shape=(
            jax.ShapeDtypeStruct((width, 3 * width), jnp.float32),
            jax.ShapeDtypeStruct((width, width), jnp.float32),
            jax.ShapeDtypeStruct((CF, width), jnp.float32),
        ),
        in_specs=[smem, vmem, vmem],
        out_specs=(vmem,) * 3,
        compiler_params=pltpu.CompilerParams(vmem_limit_bytes=16 * 2**20),
        name="finish",
    )(place, mine, other)
    return (result[None], grad_tokens[None], total_qkv, total_output, total_time)


def swap(pieces, axes):
    return lax.all_to_all(pieces, axes, 0, 0, tiled=True)


def total(pieces):
    return jnp.sum(pieces.astype(jnp.float32), axis=0).astype(jnp.bfloat16)


def copied(piece, axes):
    count = lax.axis_size(axes)
    return lax.optimization_barrier(jnp.broadcast_to(piece[None], (count,) + piece.shape))


def summed(mine, other):
    partner = [(0, 1), (1, 0)]
    mine = total(jnp.stack([mine, lax.ppermute(other, "core", partner)]))
    piece = total(swap(mine, "col"))
    piece = total(swap(copied(piece, ("zone", "row")), ("zone", "row")))
    mine = swap(copied(piece, "col"), "col")
    return mine, lax.ppermute(mine, "core", partner)


def solution(mesh):
    shape = (mesh.shape["dp"] // CORES, CORES, mesh.shape["row"], mesh.shape["col"])
    mesh = jax.sharding.Mesh(mesh.devices.reshape(shape), ("zone", "core", "row", "col"))
    grid = P(("zone", "core"), "row", "col", None)
    in_specs = (grid, P(("zone", "core")), grid, P(), P(), P())
    out_specs = (grid, grid, P(), P(), P())
    return jax.shard_map(
        on_device, mesh=mesh, in_specs=in_specs, out_specs=out_specs, check_vma=False
    )
```

```python
import functools
import math

import jax
import jax.numpy as jnp
from jax import lax
from jax.experimental import pallas as pl
from jax.experimental.pallas import tpu as pltpu
from jax.sharding import PartitionSpec as P

HEAD_DIM = 64
CF = 256
RADIUS = 3
REACH = 2 * RADIUS
EDGE = 8
SPAN = 2
WINDOW = SPAN + REACH

score_scale = 6.0
epsilon = 1e-06


def fourier(step_value):
    half_count = CF // 2
    ladder = jnp.arange(half_count, dtype=jnp.float32)
    frequency = jnp.exp(ladder * (-math.log(1000.0) / half_count))
    phase_angle = step_value.astype(jnp.float32) * frequency
    return jnp.concatenate([jnp.cos(phase_angle), jnp.sin(phase_angle)])


def exchange(to_next, to_previous, axis):
    count = lax.axis_size(axis)
    forward = [(i, i + 1) for i in range(count - 1)]
    backward = [(target, source) for source, target in forward]
    return lax.ppermute(to_next, axis, forward), lax.ppermute(to_previous, axis, backward)


def nn(left, right):
    return lax.dot_general(left, right, (((1,), (0,)), ((), ())), preferred_element_type=jnp.float32)


def nt(left, right):
    return lax.dot_general(left, right, (((1,), (1,)), ((), ())), preferred_element_type=jnp.float32)


def tn(left, right):
    return lax.dot_general(left, right, (((0,), (0,)), ((), ())), preferred_element_type=jnp.float32)


def average_matrix(width):
    own_head = lax.broadcasted_iota(jnp.int32, (width, width), 0) // HEAD_DIM
    other_head = lax.broadcasted_iota(jnp.int32, (width, width), 1) // HEAD_DIM
    return jnp.where(own_head == other_head, 1.0 / HEAD_DIM, 0.0).astype(jnp.bfloat16)


def head_mean(values, average):
    coarse = values.astype(jnp.bfloat16)
    fine = (values - coarse.astype(jnp.float32)).astype(jnp.bfloat16)
    return nn(coarse, average) + nn(fine, average)


def normalized(pixels, adaptive):
    inverse = lax.rsqrt(jnp.mean(pixels * pixels, axis=-1, keepdims=True) + epsilon)
    return inverse, (pixels * inverse * adaptive).astype(jnp.bfloat16)


def projected(pixels, adaptive, qkv_ref, average):
    width = pixels.shape[-1]
    inverse, normed = normalized(pixels, adaptive)
    project = nn(normed, qkv_ref[...])
    query_raw = project[:, :width]
    key_raw = project[:, width : 2 * width]
    query_inv = lax.rsqrt(head_mean(query_raw * query_raw, average) + epsilon)
    key_inv = lax.rsqrt(head_mean(key_raw * key_raw, average) + epsilon)
    query = query_raw * query_inv * (score_scale / HEAD_DIM)
    return inverse, normed, query, key_raw * key_inv, project[:, 2 * width :], (query_raw, query_inv, key_raw, key_inv)


def head_picks(width):
    lane_head = lax.broadcasted_iota(jnp.int32, (1, width), 1) // HEAD_DIM
    return [jnp.where(lane_head == head, 1.0, 0.0) for head in range(width // HEAD_DIM)]


def attend(keys, values, queries, grads, mask, rows, height, wanted, first, count):
    width = keys.shape[-1]
    picks = head_picks(width)
    narrow = [pick.astype(jnp.bfloat16) for pick in picks]

    def spread(part):
        return jnp.concatenate([part * pick for pick in narrow], axis=0)

    def gathered(part):
        total = part[: SPAN * rows] * picks[0]
        for head in range(1, len(picks)):
            total = total + part[head * SPAN * rows : (head + 1) * SPAN * rows] * picks[head]
        return total.reshape(SPAN, rows, width)[:, :height]

    def kept(part):
        shape = (WINDOW, rows, part.shape[1])
        return part.reshape(shape)[first : first + count, :height].reshape(-1, part.shape[1])

    queries = spread(queries)
    grads = spread(grads)
    exponent = jnp.exp(nt(keys, queries) - score_scale) * mask
    denominator = jnp.maximum(jnp.sum(exponent, axis=0, keepdims=True), 1e-30)
    weights = (exponent * (1.0 / denominator)).astype(jnp.bfloat16)
    wide = weights.astype(jnp.float32)
    slope = nt(values, grads)
    middle = jnp.sum(wide * slope, axis=0, keepdims=True)
    grad_score = (wide * (slope - middle)).astype(jnp.bfloat16)
    attended = grad_query = None
    if wanted:
        attended = gathered(tn(weights, values)).astype(jnp.bfloat16)
        grad_query = gathered(tn(grad_score, keys))
    shape = (count, height, width)
    return attended, grad_query, nn(kept(grad_score), queries).reshape(shape), nn(kept(weights), grads).reshape(shape)


def own_kernel(
    total_rows,
    place_ref,
    tok_ref,
    cot_ref,
    adaptive_ref,
    qkv_ref,
    out_ref,
    query_ref,
    key_ref,
    value_ref,
    grad_ref,
    mask_ref,
    query_raw_ref,
    query_inv_ref,
    key_raw_ref,
    key_inv_ref,
    attended_ref,
    grad_query_ref,
    grad_key_ref,
    grad_value_ref,
):
    cols, rows, width = tok_ref.shape
    lanes = mask_ref.shape[2]
    height = rows - 2 * EDGE
    row_first = place_ref[0]
    pixels = tok_ref[...].astype(jnp.float32).reshape(cols * rows, width)
    _, _, query, key, value, raw = projected(pixels, adaptive_ref[...], qkv_ref, average_matrix(width))
    query = query.astype(jnp.bfloat16)
    key = key.astype(jnp.bfloat16)
    value = value.astype(jnp.bfloat16)
    grad = nt(cot_ref[...].reshape(cols * rows, width), out_ref[...]).astype(jnp.bfloat16)
    for ref, values in ((query_ref, query), (key_ref, key), (value_ref, value), (grad_ref, grad)):
        ref[...] = values.reshape(cols, rows, width)
    for ref, values in zip((query_raw_ref, query_inv_ref, key_raw_ref, key_inv_ref), raw):
        ref[...] = values.reshape(cols, rows, width)[:, :height]

    def row_at(position):
        halo = jnp.where(position < height + EDGE, position - height - EDGE, position - EDGE)
        return jnp.where(position < height, position, halo)

    key_row = row_at(lax.broadcasted_iota(jnp.int32, (1, rows, 1), 1))
    key_col = lax.broadcasted_iota(jnp.int32, (WINDOW, 1, 1), 0)
    lane = lax.broadcasted_iota(jnp.int32, (1, 1, lanes), 2) % (SPAN * rows)
    query_row = row_at(lane % rows)
    query_col = lane // rows
    row_gap = key_row - query_row
    col_gap = key_col - query_col
    image_row = jnp.broadcast_to(row_first + key_row, row_gap.shape)
    near_row = (row_gap >= -RADIUS) & (row_gap <= RADIUS) & (image_row >= 0) & (image_row < total_rows)
    near_col = (col_gap >= 0) & (col_gap <= REACH)
    mask = jnp.where(near_row, 1.0, 0.0) * jnp.where(near_col, 1.0, 0.0)
    mask_ref[...] = mask

    pair = slice(RADIUS * rows, (RADIUS + SPAN) * rows)
    attended_ref[...], grad_query_ref[...], grad_key_ref[...], grad_value_ref[...] = attend(
        key, value, query[pair], grad[pair], mask.reshape(cols * rows, lanes), rows, height, True, 0, cols
    )


def block_kernel(
    total_cols,
    place_ref,
    tok_ref,
    cot_ref,
    left_ref,
    right_ref,
    adaptive_ref,
    qkv_ref,
    out_ref,
    own_query_ref,
    own_key_ref,
    own_value_ref,
    own_grad_ref,
    mask_ref,
    query_raw_ref,
    query_inv_ref,
    key_raw_ref,
    key_inv_ref,
    own_attended_ref,
    own_grad_query_ref,
    own_grad_key_ref,
    own_grad_value_ref,
    result_ref,
    grad_tokens_ref,
    mine_ref,
    other_ref,
    query_ref,
    key_ref,
    value_ref,
    grad_ref,
    attended_ref,
    grad_query_ref,
    grad_key_ref,
    grad_value_ref,
    whole_ref,
):
    cols, rows, width = tok_ref.shape
    height = rows - 2 * EDGE
    query_cols = cols + REACH
    last = REACH + cols
    col_first = place_ref[1]
    image = place_ref[2]
    core = place_ref[3]
    step_value = place_ref[4]
    adaptive = adaptive_ref[...]
    factor = score_scale / HEAD_DIM
    average = average_matrix(width)

    for ref, col in ((left_ref, 0), (right_ref, last)):
        pixels = ref[:REACH].astype(jnp.float32).reshape(REACH * rows, width)
        _, _, query, key, value, _ = projected(pixels, adaptive, qkv_ref, average)
        here = pl.ds(col, REACH)
        query_ref[here] = query.astype(jnp.bfloat16).reshape(REACH, rows, width)
        key_ref[here] = key.astype(jnp.bfloat16).reshape(REACH, rows, width)
        value_ref[here] = value.astype(jnp.bfloat16).reshape(REACH, rows, width)
        side = ref[REACH:].reshape(RADIUS * rows, width)
        grad = nt(side, out_ref[...]).astype(jnp.bfloat16).reshape(RADIUS, rows, width)
        grad_ref[pl.ds(0 if col == 0 else col - RADIUS, RADIUS)] = grad
    query_ref[pl.ds(REACH, cols)] = own_query_ref[...]
    key_ref[pl.ds(REACH, cols)] = own_key_ref[...]
    value_ref[pl.ds(REACH, cols)] = own_value_ref[...]
    grad_ref[pl.ds(RADIUS, cols)] = own_grad_ref[...]
    attended_ref[pl.ds(RADIUS, SPAN)] = own_attended_ref[...]
    grad_query_ref[pl.ds(RADIUS, SPAN)] = own_grad_query_ref[...]
    grad_key_ref[...] = own_grad_key_ref[...]
    grad_value_ref[...] = own_grad_value_ref[...]

    for start in range(0, query_cols, SPAN):
        if start == REACH:
            continue
        near = pl.ds(start, WINDOW)
        masks = []
        for column in range(WINDOW):
            mask = mask_ref[column]
            if start + column < REACH or start + column >= last:
                image_col = col_first + (start + column - REACH)
                mask = mask * jnp.where((image_col >= 0) & (image_col < total_cols), 1.0, 0.0)
            masks.append(mask)
        low = max(start, REACH)
        high = min(start + WINDOW, last)
        query_low = max(start + RADIUS, REACH)
        query_high = min(start + RADIUS + SPAN, last)
        attended, grad_query, grad_key, grad_value = attend(
            key_ref[near].reshape(WINDOW * rows, width),
            value_ref[near].reshape(WINDOW * rows, width),
            query_ref[pl.ds(start + RADIUS, SPAN)].reshape(SPAN * rows, width),
            grad_ref[pl.ds(start, SPAN)].reshape(SPAN * rows, width),
            jnp.concatenate(masks, axis=0),
            rows,
            height,
            query_low < query_high,
            low - start,
            high - low,
        )
        if query_low < query_high:
            own = slice(query_low - start - RADIUS, query_high - start - RADIUS)
            there = pl.ds(query_low - REACH, query_high - query_low)
            attended_ref[there] = attended[own]
            grad_query_ref[there] = grad_query[own]
        there = pl.ds(low - REACH, high - low)
        grad_key_ref[there] += grad_key
        grad_value_ref[there] += grad_value

    tokens = cols * height
    pixels = tok_ref[:, :height].astype(jnp.float32).reshape(tokens, width)
    inverse, normed = normalized(pixels, adaptive)
    cot_own = cot_ref[:, :height].reshape(tokens, width)
    attended = attended_ref[...].reshape(tokens, width)
    result = pixels + nn(attended, out_ref[...])
    result_ref[...] = result.astype(jnp.bfloat16).reshape(cols, height, width)
    whole_ref[:, 3 * width :] = tn(attended, cot_own)

    def back(raw, inv, grad, scale):
        return scale * inv * (grad - raw * inv * inv * head_mean(grad * raw, average))

    grad_query = grad_query_ref[...].reshape(tokens, width)
    grad_key = grad_key_ref[...].reshape(tokens, width)
    grad_project = jnp.concatenate(
        [
            back(query_raw_ref[...].reshape(tokens, width), query_inv_ref[...].reshape(tokens, width), grad_query, factor).astype(jnp.bfloat16),
            back(key_raw_ref[...].reshape(tokens, width), key_inv_ref[...].reshape(tokens, width), grad_key, 1.0).astype(jnp.bfloat16),
            grad_value_ref[...].reshape(tokens, width).astype(jnp.bfloat16),
        ],
        axis=1,
    )
    whole_ref[:, : 3 * width] = tn(normed, grad_project)
    grad_normed = nt(grad_project, qkv_ref[...])
    scaled = grad_normed * adaptive
    inner = jnp.mean(scaled * pixels, axis=-1, keepdims=True)
    grad_pixels = inverse * (scaled - pixels * (inverse * inverse * inner))
    grad_tokens = cot_own.astype(jnp.float32) + grad_pixels
    grad_tokens_ref[...] = grad_tokens.astype(jnp.bfloat16).reshape(cols, height, width)
    grad_adaptive = jnp.sum(grad_normed * (pixels * inverse), axis=0, keepdims=True)

    half = width // CORES
    across = 4 * width // LANES
    line = lax.broadcasted_iota(jnp.int32, (SLOT, LANES), 0)
    lane = lax.broadcasted_iota(jnp.int32, (SLOT, LANES), 1)
    high = (step_value // 32).astype(jnp.float32)
    low = (step_value % 32).astype(jnp.float32)
    for ref, which in ((mine_ref, core), (other_ref, 1 - core)):
        part = whole_ref[pl.ds(pl.multiple_of(which * half, half), half), :].astype(jnp.bfloat16)
        for block in range(ref.shape[0]):
            top = block // across * LINES
            first = block % across * LANES
            ref[block, :LINES] = part[top : top + LINES, first : first + LANES]
            if block < width // LANES:
                side = jnp.where(line == image, grad_adaptive[:, block * LANES : (block + 1) * LANES], 0.0)
                if block == 0:
                    there = line == SLOT // 2 + image
                    side = jnp.where(there & (lane == 0), high, side)
                    side = jnp.where(there & (lane == 1), low, side)
                ref[block, LINES:] = side.astype(jnp.bfloat16)
            else:
                ref[block, LINES:] = jnp.zeros((SLOT, LANES), jnp.bfloat16)


def finish_kernel(senders, place_ref, mine_ref, other_ref, qkv_ref, output_ref, time_ref):
    width = output_ref.shape[0]
    images = senders[0]
    half = width // CORES
    across = 4 * width // LANES
    core = place_ref[3]
    for ref, which in ((mine_ref, core), (other_ref, 1 - core)):
        for block in range(mine_ref.shape[0]):
            top = pl.multiple_of(which * half, half) + block // across * LINES
            first = block % across * LANES
            values = ref[block, :LINES].astype(jnp.float32)
            if first < 3 * width:
                qkv_ref[pl.ds(top, LINES), first : first + LANES] = values
            else:
                output_ref[pl.ds(top, LINES), first - 3 * width : first - 3 * width + LANES] = values
    sides = [mine_ref[block, LINES:].astype(jnp.float32) for block in range(width // LANES)]
    adaptives = jnp.concatenate(sides, axis=1)
    adaptives = jnp.where(lax.broadcasted_iota(jnp.int32, adaptives.shape, 0) < images, adaptives, 0.0)
    ladder = lax.broadcasted_iota(jnp.int32, (1, CF // 2), 1).astype(jnp.float32)
    frequency = jnp.exp(ladder * (-math.log(1000.0) / (CF // 2)))
    steps = (sides[0][:, 0:1] * 32.0 + sides[0][:, 1:2]) / senders[1]
    steps = jnp.concatenate([steps[SLOT // 2 :], steps[: SLOT // 2] * 0.0], axis=0)
    angle = steps * frequency
    features = jnp.concatenate([jnp.cos(angle), jnp.sin(angle)], axis=1)
    time_ref[...] = lax.dot_general(
        features,
        adaptives,
        (((0,), (0,)), ((), ())),
        precision=lax.Precision.HIGHEST,
        preferred_element_type=jnp.float32,
    )


CORES = 2
SLOT = 8
LINES = 32
LANES = 128


def on_device(tokens, timesteps, cotangent, qkv_weight, output_weight, time_weight):
    height, cols, width = tokens.shape[1:]
    row_first = lax.axis_index("row") * height
    col_first = lax.axis_index("col") * cols
    total_rows = height * lax.axis_size("row")
    total_cols = cols * lax.axis_size("col")
    rows = height + 2 * EDGE
    both = jnp.concatenate([tokens[0].transpose(1, 0, 2), cotangent[0].transpose(1, 0, 2)], axis=0)
    above, below = exchange(both[:, height - EDGE :], both[:, :EDGE], "row")
    both = jnp.concatenate([both, above, below], axis=1)
    tok, cot = both[:cols], both[cols:]
    to_next = jnp.concatenate([tok[cols - REACH :], cot[cols - RADIUS :]], axis=0)
    to_previous = jnp.concatenate([tok[:REACH], cot[:RADIUS]], axis=0)
    left, right = exchange(to_next, to_previous, "col")
    features = fourier(timesteps[0])
    adaptive = 1.0 + jnp.dot(
        features[None], time_weight.astype(jnp.float32), precision=lax.Precision.HIGHEST
    )
    image = lax.axis_index(("zone", "core"))
    place = [row_first, col_first, image, lax.axis_index("core"), timesteps[0]]
    place = jnp.stack(place).astype(jnp.int32)

    around = cols + 2 * REACH
    query_cols = cols + REACH
    lanes = width // HEAD_DIM * SPAN * rows
    smem = pl.BlockSpec(memory_space=pltpu.SMEM)
    vmem = pl.BlockSpec(memory_space=pltpu.VMEM)
    limits = pltpu.CompilerParams(vmem_limit_bytes=40 * 2**20)
    tall = jax.ShapeDtypeStruct((cols, rows, width), jnp.bfloat16)
    block = jax.ShapeDtypeStruct((cols, height, width), jnp.bfloat16)
    exact = jax.ShapeDtypeStruct((cols, height, width), jnp.float32)
    mask = jax.ShapeDtypeStruct((WINDOW, rows, lanes), jnp.float32)
    pair = (
        jax.ShapeDtypeStruct((SPAN, height, width), jnp.bfloat16),
        jax.ShapeDtypeStruct((SPAN, height, width), jnp.float32),
    )
    prepared = pl.pallas_call(
        functools.partial(own_kernel, total_rows),
        out_shape=(tall,) * 4 + (mask,) + (exact,) * 4 + pair + (exact,) * 2,
        in_specs=[smem] + [vmem] * 5,
        out_specs=(vmem,) * 13,
        compiler_params=limits,
        cost_estimate=pl.CostEstimate(flops=1_000_000_000, bytes_accessed=4_000_000, transcendentals=200_000),
        name="own",
    )(place, tok, cot, adaptive, qkv_weight, output_weight)
    pieces = width // CORES // LINES * (4 * width // LANES)
    chunks = jax.ShapeDtypeStruct((pieces, LINES + SLOT, LANES), jnp.bfloat16)
    wide = pltpu.VMEM((around, rows, width), jnp.bfloat16)
    result, grad_tokens, mine, other = pl.pallas_call(
        functools.partial(block_kernel, total_cols),
        out_shape=(block, block, chunks, chunks),
        in_specs=[smem] + [vmem] * 20,
        out_specs=(vmem,) * 4,
        scratch_shapes=[
            wide,
            wide,
            wide,
            pltpu.VMEM((query_cols, rows, width), jnp.bfloat16),
            pltpu.VMEM((cols, height, width), jnp.bfloat16),
            pltpu.VMEM((cols, height, width), jnp.float32),
            pltpu.VMEM((cols, height, width), jnp.float32),
            pltpu.VMEM((cols, height, width), jnp.float32),
            pltpu.VMEM((width, 4 * width), jnp.float32),
        ],
        compiler_params=limits,
        cost_estimate=pl.CostEstimate(flops=8_000_000_000, bytes_accessed=4_000_000, transcendentals=1_000_000),
        name="block",
    )(place, tok, cot, left, right, adaptive, qkv_weight, output_weight, *prepared)
    result = result.transpose(1, 0, 2)
    grad_tokens = grad_tokens.transpose(1, 0, 2)

    mine, other = summed(mine, other)
    total_qkv, total_output, total_time = pl.pallas_call(
        functools.partial(finish_kernel, (lax.axis_size("zone") * CORES, lax.axis_size("row") * lax.axis_size("col"))),
        out_shape=(
            jax.ShapeDtypeStruct((width, 3 * width), jnp.float32),
            jax.ShapeDtypeStruct((width, width), jnp.float32),
            jax.ShapeDtypeStruct((CF, width), jnp.float32),
        ),
        in_specs=[smem, vmem, vmem],
        out_specs=(vmem,) * 3,
        compiler_params=pltpu.CompilerParams(vmem_limit_bytes=16 * 2**20),
        name="finish",
    )(place, mine, other)
    return (result[None], grad_tokens[None], total_qkv, total_output, total_time)


def swap(pieces, axes):
    return lax.all_to_all(pieces, axes, 0, 0, tiled=True)


def total(pieces):
    return jnp.sum(pieces.astype(jnp.float32), axis=0).astype(jnp.bfloat16)


def copied(piece, axes):
    count = lax.axis_size(axes)
    return lax.optimization_barrier(jnp.broadcast_to(piece[None], (count,) + piece.shape))


def summed(mine, other):
    partner = [(0, 1), (1, 0)]
    mine = total(jnp.stack([mine, lax.ppermute(other, "core", partner)]))
    piece = total(swap(mine, "col"))
    piece = total(swap(copied(piece, ("zone", "row")), ("zone", "row")))
    mine = swap(copied(piece, "col"), "col")
    return mine, lax.ppermute(mine, "core", partner)


def solution(mesh):
    shape = (mesh.shape["dp"] // CORES, CORES, mesh.shape["row"], mesh.shape["col"])
    mesh = jax.sharding.Mesh(mesh.devices.reshape(shape), ("zone", "core", "row", "col"))
    grid = P(("zone", "core"), "row", "col", None)
    in_specs = (grid, P(("zone", "core")), grid, P(), P(), P())
    out_specs = (grid, grid, P(), P(), P())
    return jax.shard_map(
        on_device, mesh=mesh, in_specs=in_specs, out_specs=out_specs, check_vma=False
    )
```

```python
import functools
import math

import jax
import jax.numpy as jnp
from jax import lax
from jax.experimental import pallas as pl
from jax.experimental.layout import Layout, with_layout_constraint
from jax.experimental.pallas import tpu as pltpu
from jax.sharding import PartitionSpec as P

HEAD_DIM = 64
CF = 256
RADIUS = 3
REACH = 2 * RADIUS
EDGE = 8
SPAN = 2
WINDOW = SPAN + REACH

score_scale = 6.0
epsilon = 1e-06


def fourier(step_value):
    half_count = CF // 2
    ladder = jnp.arange(half_count, dtype=jnp.float32)
    frequency = jnp.exp(ladder * (-math.log(1000.0) / half_count))
    phase_angle = step_value.astype(jnp.float32) * frequency
    return jnp.concatenate([jnp.cos(phase_angle), jnp.sin(phase_angle)])


def exchange(to_next, to_previous, axis):
    count = lax.axis_size(axis)
    forward = [(i, i + 1) for i in range(count - 1)]
    backward = [(target, source) for source, target in forward]
    from_previous = lax.ppermute(to_next, axis, forward)
    from_next = lax.ppermute(to_previous, axis, backward)
    return from_previous, from_next


def nn(left, right):
    return lax.dot_general(left, right, (((1,), (0,)), ((), ())), preferred_element_type=jnp.float32)


def nt(left, right):
    return lax.dot_general(left, right, (((1,), (1,)), ((), ())), preferred_element_type=jnp.float32)


def tn(left, right):
    return lax.dot_general(left, right, (((0,), (0,)), ((), ())), preferred_element_type=jnp.float32)


def average_matrix(width):
    own_head = lax.broadcasted_iota(jnp.int32, (width, width), 0) // HEAD_DIM
    other_head = lax.broadcasted_iota(jnp.int32, (width, width), 1) // HEAD_DIM
    return jnp.where(own_head == other_head, 1.0 / HEAD_DIM, 0.0).astype(jnp.bfloat16)


def head_mean(values, average):
    coarse = values.astype(jnp.bfloat16)
    fine = (values - coarse.astype(jnp.float32)).astype(jnp.bfloat16)
    return nn(coarse, average) + nn(fine, average)


def normalized(pixels, adaptive):
    inverse = lax.rsqrt(jnp.mean(pixels * pixels, axis=-1, keepdims=True) + epsilon)
    return inverse, (pixels * inverse * adaptive).astype(jnp.bfloat16)


def projected(pixels, adaptive, qkv_ref, average):
    width = pixels.shape[-1]
    inverse, normed = normalized(pixels, adaptive)
    project = nn(normed, qkv_ref[...])
    query_raw = project[:, :width]
    key_raw = project[:, width : 2 * width]
    query_inv = lax.rsqrt(head_mean(query_raw * query_raw, average) + epsilon)
    key_inv = lax.rsqrt(head_mean(key_raw * key_raw, average) + epsilon)
    query = query_raw * query_inv * (score_scale / HEAD_DIM)
    return inverse, normed, query, key_raw * key_inv, project[:, 2 * width :], (query_raw, query_inv, key_raw, key_inv)


def head_picks(width):
    lane_head = lax.broadcasted_iota(jnp.int32, (1, width), 1) // HEAD_DIM
    return [jnp.where(lane_head == head, 1.0, 0.0) for head in range(width // HEAD_DIM)]


def attend(keys, values, queries, grads, mask, rows, height, wanted, first, count):
    width = keys.shape[-1]
    picks = head_picks(width)
    narrow = [pick.astype(jnp.bfloat16) for pick in picks]

    def spread(part):
        return jnp.concatenate([part * pick for pick in narrow], axis=0)

    def gathered(part):
        total = part[: SPAN * rows] * picks[0]
        for head in range(1, len(picks)):
            total = total + part[head * SPAN * rows : (head + 1) * SPAN * rows] * picks[head]
        return total.reshape(SPAN, rows, width)[:, :height]

    def kept(part):
        shape = (WINDOW, rows, part.shape[1])
        return part.reshape(shape)[first : first + count, :height].reshape(-1, part.shape[1])

    queries = spread(queries)
    grads = spread(grads)
    exponent = jnp.exp(nt(keys, queries) - score_scale) * mask
    denominator = jnp.maximum(jnp.sum(exponent, axis=0, keepdims=True), 1e-30)
    weights = (exponent * (1.0 / denominator)).astype(jnp.bfloat16)
    wide = weights.astype(jnp.float32)
    slope = nt(values, grads)
    middle = jnp.sum(wide * slope, axis=0, keepdims=True)
    grad_score = (wide * (slope - middle)).astype(jnp.bfloat16)
    attended = grad_query = None
    if wanted:
        attended = gathered(tn(weights, values)).astype(jnp.bfloat16)
        grad_query = gathered(tn(grad_score, keys))
    shape = (count, height, width)
    return attended, grad_query, nn(kept(grad_score), queries).reshape(shape), nn(kept(weights), grads).reshape(shape)


def own_kernel(
    total_rows,
    place_ref,
    tok_ref,
    cot_ref,
    adaptive_ref,
    qkv_ref,
    out_ref,
    query_ref,
    key_ref,
    value_ref,
    grad_ref,
    mask_ref,
    query_raw_ref,
    query_inv_ref,
    key_raw_ref,
    key_inv_ref,
    attended_ref,
    grad_query_ref,
    grad_key_ref,
    grad_value_ref,
):
    cols, rows, width = tok_ref.shape
    lanes = mask_ref.shape[2]
    height = rows - 2 * EDGE
    row_first = place_ref[0]
    pixels = tok_ref[...].astype(jnp.float32).reshape(cols * rows, width)
    _, _, query, key, value, raw = projected(pixels, adaptive_ref[...], qkv_ref, average_matrix(width))
    query = query.astype(jnp.bfloat16)
    key = key.astype(jnp.bfloat16)
    value = value.astype(jnp.bfloat16)
    grad = nt(cot_ref[...].reshape(cols * rows, width), out_ref[...]).astype(jnp.bfloat16)
    for ref, values in ((query_ref, query), (key_ref, key), (value_ref, value), (grad_ref, grad)):
        ref[...] = values.reshape(cols, rows, width)
    for ref, values in zip((query_raw_ref, query_inv_ref, key_raw_ref, key_inv_ref), raw):
        ref[...] = values.reshape(cols, rows, width)[:, :height]

    def row_at(position):
        halo = jnp.where(position < height + EDGE, position - height - EDGE, position - EDGE)
        return jnp.where(position < height, position, halo)

    key_row = row_at(lax.broadcasted_iota(jnp.int32, (1, rows, 1), 1))
    key_col = lax.broadcasted_iota(jnp.int32, (WINDOW, 1, 1), 0)
    lane = lax.broadcasted_iota(jnp.int32, (1, 1, lanes), 2) % (SPAN * rows)
    query_row = row_at(lane % rows)
    query_col = lane // rows
    row_gap = key_row - query_row
    col_gap = key_col - query_col
    image_row = jnp.broadcast_to(row_first + key_row, row_gap.shape)
    near_row = (row_gap >= -RADIUS) & (row_gap <= RADIUS) & (image_row >= 0) & (image_row < total_rows)
    near_col = (col_gap >= 0) & (col_gap <= REACH)
    mask = jnp.where(near_row, 1.0, 0.0) * jnp.where(near_col, 1.0, 0.0)
    mask_ref[...] = mask

    pair = slice(RADIUS * rows, (RADIUS + SPAN) * rows)
    attended_ref[...], grad_query_ref[...], grad_key_ref[...], grad_value_ref[...] = attend(
        key, value, query[pair], grad[pair], mask.reshape(cols * rows, lanes), rows, height, True, 0, cols
    )


def side_pairs(
    starts,
    total_cols,
    place_ref,
    side_ref,
    adaptive_ref,
    qkv_ref,
    out_ref,
    own,
    mask_ref,
    side,
    attended_ref,
    grad_query_ref,
    grad_key_ref,
    grad_value_ref,
):
    cols, rows, width = own[0].shape
    height = rows - 2 * EDGE
    last = REACH + cols
    col_first = place_ref[1]
    left = starts[0] == 0
    pixels = side_ref[:REACH].astype(jnp.float32).reshape(REACH * rows, width)
    _, _, query, key, value, _ = projected(pixels, adaptive_ref[...], qkv_ref, average_matrix(width))
    for ref, values in zip(side, (query, key, value)):
        ref[...] = values.astype(jnp.bfloat16).reshape(REACH, rows, width)
    grad = nt(side_ref[REACH:].reshape(RADIUS * rows, width), out_ref[...])
    side[3][...] = grad.astype(jnp.bfloat16).reshape(RADIUS, rows, width)

    def columns(which, low, high):
        beside = side[which]
        base = (REACH - beside.shape[0]) if left else last
        parts = []
        if left and low < REACH:
            parts.append(beside[low - base : min(high, REACH) - base])
        if max(low, REACH) < min(high, last):
            parts.append(own[which][max(low, REACH) - REACH : min(high, last) - REACH])
        if not left and high > last:
            parts.append(beside[max(low, last) - base : high - base])
        joined = parts[0] if len(parts) == 1 else jnp.concatenate(parts, axis=0)
        return joined.reshape((high - low) * rows, width)

    done = 0
    for start in starts:
        masks = []
        for column in range(start, start + WINDOW):
            mask = mask_ref[column - start]
            if column < REACH or column >= last:
                image_col = col_first + (column - REACH)
                mask = mask * jnp.where((image_col >= 0) & (image_col < total_cols), 1.0, 0.0)
            masks.append(mask)
        low, high = max(start, REACH), min(start + WINDOW, last)
        first = start + RADIUS
        query_low, query_high = max(first, REACH), min(first + SPAN, last)
        attended, grad_query, grad_key, grad_value = attend(
            columns(1, start, start + WINDOW),
            columns(2, start, start + WINDOW),
            columns(0, first, first + SPAN),
            columns(3, first, first + SPAN),
            jnp.concatenate(masks, axis=0),
            rows,
            height,
            query_low < query_high,
            low - start,
            high - low,
        )
        if query_low < query_high:
            there = pl.ds(done, query_high - query_low)
            attended_ref[there] = attended[query_low - first : query_high - first]
            grad_query_ref[there] = grad_query[query_low - first : query_high - first]
            done += query_high - query_low
        there = pl.ds(low - REACH, high - low)
        grad_key_ref[there] += grad_key
        grad_value_ref[there] += grad_value


def left_kernel(
    starts,
    total_cols,
    place_ref,
    side_ref,
    adaptive_ref,
    qkv_ref,
    out_ref,
    query_ref,
    key_ref,
    value_ref,
    grad_ref,
    mask_ref,
    own_grad_key_ref,
    own_grad_value_ref,
    attended_ref,
    grad_query_ref,
    grad_key_ref,
    grad_value_ref,
    *side,
):
    grad_key_ref[...] = own_grad_key_ref[...]
    grad_value_ref[...] = own_grad_value_ref[...]
    own = (query_ref, key_ref, value_ref, grad_ref)
    results = (attended_ref, grad_query_ref, grad_key_ref, grad_value_ref)
    side_pairs(starts, total_cols, place_ref, side_ref, adaptive_ref, qkv_ref, out_ref, own, mask_ref, side, *results)


def right_kernel(
    starts,
    total_cols,
    place_ref,
    tok_ref,
    cot_ref,
    side_ref,
    adaptive_ref,
    qkv_ref,
    out_ref,
    query_ref,
    key_ref,
    value_ref,
    grad_ref,
    mask_ref,
    query_raw_ref,
    query_inv_ref,
    key_raw_ref,
    key_inv_ref,
    own_attended_ref,
    own_grad_query_ref,
    left_attended_ref,
    left_grad_query_ref,
    left_grad_key_ref,
    left_grad_value_ref,
    result_ref,
    grad_tokens_ref,
    mine_ref,
    other_ref,
    attended_ref,
    grad_query_ref,
    grad_key_ref,
    grad_value_ref,
    whole_ref,
    *side,
):
    cols, rows, width = tok_ref.shape
    height = rows - 2 * EDGE
    image = place_ref[2]
    core = place_ref[3]
    step_value = place_ref[4]
    adaptive = adaptive_ref[...]
    factor = score_scale / HEAD_DIM
    average = average_matrix(width)
    grad_key_ref[...] = left_grad_key_ref[...]
    grad_value_ref[...] = left_grad_value_ref[...]
    own = (query_ref, key_ref, value_ref, grad_ref)
    results = (attended_ref, grad_query_ref, grad_key_ref, grad_value_ref)
    side_pairs(starts, total_cols, place_ref, side_ref, adaptive_ref, qkv_ref, out_ref, own, mask_ref, side, *results)

    tokens = cols * height
    pixels = tok_ref[:, :height].astype(jnp.float32).reshape(tokens, width)
    inverse, normed = normalized(pixels, adaptive)
    cot_own = cot_ref[:, :height].reshape(tokens, width)
    parts = (left_attended_ref[...], own_attended_ref[...], attended_ref[...])
    attended = jnp.concatenate(parts, axis=0).reshape(tokens, width)
    result = pixels + nn(attended, out_ref[...])
    result_ref[...] = result.astype(jnp.bfloat16).reshape(cols, height, width)
    whole_ref[:, 3 * width :] = tn(attended, cot_own)

    def back(raw, inv, grad, scale):
        return scale * inv * (grad - raw * inv * inv * head_mean(grad * raw, average))

    parts = (left_grad_query_ref[...], own_grad_query_ref[...], grad_query_ref[...])
    grad_query = jnp.concatenate(parts, axis=0).reshape(tokens, width)
    grad_key = grad_key_ref[...].reshape(tokens, width)
    grad_project = jnp.concatenate(
        [
            back(query_raw_ref[...].reshape(tokens, width), query_inv_ref[...].reshape(tokens, width), grad_query, factor).astype(jnp.bfloat16),
            back(key_raw_ref[...].reshape(tokens, width), key_inv_ref[...].reshape(tokens, width), grad_key, 1.0).astype(jnp.bfloat16),
            grad_value_ref[...].reshape(tokens, width).astype(jnp.bfloat16),
        ],
        axis=1,
    )
    whole_ref[:, : 3 * width] = tn(normed, grad_project)
    grad_normed = nt(grad_project, qkv_ref[...])
    scaled = grad_normed * adaptive
    inner = jnp.mean(scaled * pixels, axis=-1, keepdims=True)
    grad_pixels = inverse * (scaled - pixels * (inverse * inverse * inner))
    grad_tokens = cot_own.astype(jnp.float32) + grad_pixels
    grad_tokens_ref[...] = grad_tokens.astype(jnp.bfloat16).reshape(cols, height, width)
    grad_adaptive = jnp.sum(grad_normed * (pixels * inverse), axis=0, keepdims=True)

    half = width // CORES
    across = 4 * width // LANES
    line = lax.broadcasted_iota(jnp.int32, (SLOT, LANES), 0)
    lane = lax.broadcasted_iota(jnp.int32, (SLOT, LANES), 1)
    high = (step_value // 32).astype(jnp.float32)
    low = (step_value % 32).astype(jnp.float32)
    for ref, which in ((mine_ref, core), (other_ref, 1 - core)):
        part = whole_ref[pl.ds(pl.multiple_of(which * half, half), half), :].astype(jnp.bfloat16)
        for block in range(ref.shape[0]):
            top = block // across * LINES
            first = block % across * LANES
            ref[block, :LINES] = part[top : top + LINES, first : first + LANES]
            if block < width // LANES:
                side = jnp.where(line == image, grad_adaptive[:, block * LANES : (block + 1) * LANES], 0.0)
                if block == 0:
                    there = line == SLOT // 2 + image
                    side = jnp.where(there & (lane == 0), high, side)
                    side = jnp.where(there & (lane == 1), low, side)
                ref[block, LINES:] = side.astype(jnp.bfloat16)
            else:
                ref[block, LINES:] = jnp.zeros((SLOT, LANES), jnp.bfloat16)


def finish_kernel(senders, place_ref, mine_ref, other_ref, qkv_ref, output_ref, time_ref):
    width = output_ref.shape[0]
    images = senders[0]
    half = width // CORES
    across = 4 * width // LANES
    core = place_ref[3]
    for ref, which in ((mine_ref, core), (other_ref, 1 - core)):
        for block in range(mine_ref.shape[0]):
            top = pl.multiple_of(which * half, half) + block // across * LINES
            first = block % across * LANES
            values = ref[block, :LINES].astype(jnp.float32)
            if first < 3 * width:
                qkv_ref[pl.ds(top, LINES), first : first + LANES] = values
            else:
                output_ref[pl.ds(top, LINES), first - 3 * width : first - 3 * width + LANES] = values
    sides = [mine_ref[block, LINES:].astype(jnp.float32) for block in range(width // LANES)]
    adaptives = jnp.concatenate(sides, axis=1)
    adaptives = jnp.where(lax.broadcasted_iota(jnp.int32, adaptives.shape, 0) < images, adaptives, 0.0)
    ladder = lax.broadcasted_iota(jnp.int32, (1, CF // 2), 1).astype(jnp.float32)
    frequency = jnp.exp(ladder * (-math.log(1000.0) / (CF // 2)))
    steps = (sides[0][:, 0:1] * 32.0 + sides[0][:, 1:2]) / senders[1]
    steps = jnp.concatenate([steps[SLOT // 2 :], steps[: SLOT // 2] * 0.0], axis=0)
    angle = steps * frequency
    features = jnp.concatenate([jnp.cos(angle), jnp.sin(angle)], axis=1)
    time_ref[...] = lax.dot_general(
        features,
        adaptives,
        (((0,), (0,)), ((), ())),
        precision=lax.Precision.HIGHEST,
        preferred_element_type=jnp.float32,
    )


CORES = 2
SLOT = 8
LINES = 32
LANES = 128


def on_device(tokens, timesteps, cotangent, qkv_weight, output_weight, time_weight):
    height, cols, width = tokens.shape[1:]
    row_first = lax.axis_index("row") * height
    col_first = lax.axis_index("col") * cols
    total_rows = height * lax.axis_size("row")
    total_cols = cols * lax.axis_size("col")
    rows = height + 2 * EDGE

    def lying(values):
        return with_layout_constraint(values, Layout(major_to_minor=(0, 1, 2)))

    def edge_rows(low, high):
        return lying(jnp.concatenate([tokens[0, low:high], cotangent[0, low:high]], axis=0))

    both = jnp.concatenate([tokens[0].transpose(1, 0, 2), cotangent[0].transpose(1, 0, 2)], axis=0)
    above, below = exchange(edge_rows(height - EDGE, height), edge_rows(0, EDGE), "row")
    above, below = (lying(rows_).transpose(1, 0, 2).reshape(cols, 2, EDGE, width) for rows_ in (above, below))
    above, below = (rows_.transpose(1, 0, 2, 3).reshape(2 * cols, EDGE, width) for rows_ in (above, below))
    both = jnp.concatenate([both, above, below], axis=1)
    tok, cot = both[:cols], both[cols:]
    to_next = jnp.concatenate([tok[cols - REACH :], cot[cols - RADIUS :]], axis=0)
    to_previous = jnp.concatenate([tok[:REACH], cot[:RADIUS]], axis=0)
    left, right = exchange(to_next, to_previous, "col")
    features = fourier(timesteps[0])
    adaptive = 1.0 + jnp.dot(
        features[None], time_weight.astype(jnp.float32), precision=lax.Precision.HIGHEST
    )
    image = lax.axis_index(("zone", "core"))
    place = [row_first, col_first, image, lax.axis_index("core"), timesteps[0]]
    place = jnp.stack(place).astype(jnp.int32)

    lanes = width // HEAD_DIM * SPAN * rows
    smem = pl.BlockSpec(memory_space=pltpu.SMEM)
    vmem = pl.BlockSpec(memory_space=pltpu.VMEM)
    limits = pltpu.CompilerParams(vmem_limit_bytes=40 * 2**20)
    tall = jax.ShapeDtypeStruct((cols, rows, width), jnp.bfloat16)
    block = jax.ShapeDtypeStruct((cols, height, width), jnp.bfloat16)
    exact = jax.ShapeDtypeStruct((cols, height, width), jnp.float32)
    masked = jax.ShapeDtypeStruct((WINDOW, rows, lanes), jnp.float32)
    pair = (
        jax.ShapeDtypeStruct((SPAN, height, width), jnp.bfloat16),
        jax.ShapeDtypeStruct((SPAN, height, width), jnp.float32),
    )
    prepared = pl.pallas_call(
        functools.partial(own_kernel, total_rows),
        out_shape=(tall,) * 4 + (masked,) + (exact,) * 4 + pair + (exact,) * 2,
        in_specs=[smem] + [vmem] * 5,
        out_specs=(vmem,) * 13,
        compiler_params=limits,
        cost_estimate=pl.CostEstimate(flops=1_000_000_000, bytes_accessed=4_000_000, transcendentals=200_000),
        name="own",
    )(place, tok, cot, adaptive, qkv_weight, output_weight)
    *own, mask, query_raw, query_inv, key_raw, key_inv, attended, grad_query, grad_key, grad_value = prepared
    starts = tuple(range(0, cols + REACH, SPAN))
    middle = starts.index(REACH)
    third = (cols - SPAN) // 2
    part = (
        jax.ShapeDtypeStruct((third, height, width), jnp.bfloat16),
        jax.ShapeDtypeStruct((third, height, width), jnp.float32),
    )
    side = [pltpu.VMEM((REACH, rows, width), jnp.bfloat16)] * 3 + [pltpu.VMEM((RADIUS, rows, width), jnp.bfloat16)]
    from_left = pl.pallas_call(
        functools.partial(left_kernel, starts[:middle], total_cols),
        out_shape=part + (exact,) * 2,
        in_specs=[smem] + [vmem] * 11,
        out_specs=(vmem,) * 4,
        scratch_shapes=side,
        compiler_params=limits,
        cost_estimate=pl.CostEstimate(flops=2_000_000_000, bytes_accessed=2_000_000, transcendentals=400_000),
        name="left",
    )(place, left, adaptive, qkv_weight, output_weight, *own, mask, grad_key, grad_value)
    pieces = width // CORES // LINES * (4 * width // LANES)
    chunks = jax.ShapeDtypeStruct((pieces, LINES + SLOT, LANES), jnp.bfloat16)
    result, grad_tokens, mine, other = pl.pallas_call(
        functools.partial(right_kernel, starts[middle + 1 :], total_cols),
        out_shape=(block, block, chunks, chunks),
        in_specs=[smem] + [vmem] * 21,
        out_specs=(vmem,) * 4,
        scratch_shapes=[
            pltpu.VMEM((third, height, width), jnp.bfloat16),
            pltpu.VMEM((third, height, width), jnp.float32),
            pltpu.VMEM((cols, height, width), jnp.float32),
            pltpu.VMEM((cols, height, width), jnp.float32),
            pltpu.VMEM((width, 4 * width), jnp.float32),
        ]
        + side,
        compiler_params=limits,
        cost_estimate=pl.CostEstimate(flops=3_000_000_000, bytes_accessed=3_000_000, transcendentals=400_000),
        name="right",
    )(
        place,
        tok,
        cot,
        right,
        adaptive,
        qkv_weight,
        output_weight,
        *own,
        mask,
        query_raw,
        query_inv,
        key_raw,
        key_inv,
        attended,
        grad_query,
        *from_left,
    )
    result = result.transpose(1, 0, 2)
    grad_tokens = grad_tokens.transpose(1, 0, 2)

    mine, other = summed(mine, other)
    total_qkv, total_output, total_time = pl.pallas_call(
        functools.partial(finish_kernel, (lax.axis_size("zone") * CORES, lax.axis_size("row") * lax.axis_size("col"))),
        out_shape=(
            jax.ShapeDtypeStruct((width, 3 * width), jnp.float32),
            jax.ShapeDtypeStruct((width, width), jnp.float32),
            jax.ShapeDtypeStruct((CF, width), jnp.float32),
        ),
        in_specs=[smem, vmem, vmem],
        out_specs=(vmem,) * 3,
        compiler_params=pltpu.CompilerParams(vmem_limit_bytes=16 * 2**20),
        name="finish",
    )(place, mine, other)
    return (result[None], grad_tokens[None], total_qkv, total_output, total_time)


def swap(pieces, axes):
    return lax.all_to_all(pieces, axes, 0, 0, tiled=True)


def total(pieces):
    return jnp.sum(pieces.astype(jnp.float32), axis=0).astype(jnp.bfloat16)


def copied(piece, axes):
    count = lax.axis_size(axes)
    return lax.optimization_barrier(jnp.broadcast_to(piece[None], (count,) + piece.shape))


def summed(mine, other):
    partner = [(0, 1), (1, 0)]
    mine = total(jnp.stack([mine, lax.ppermute(other, "core", partner)]))
    piece = total(swap(mine, "col"))
    piece = total(swap(copied(piece, ("zone", "row")), ("zone", "row")))
    mine = swap(copied(piece, "col"), "col")
    return mine, lax.ppermute(mine, "core", partner)


def solution(mesh):
    shape = (mesh.shape["dp"] // CORES, CORES, mesh.shape["row"], mesh.shape["col"])
    mesh = jax.sharding.Mesh(mesh.devices.reshape(shape), ("zone", "core", "row", "col"))
    grid = P(("zone", "core"), "row", "col", None)
    in_specs = (grid, P(("zone", "core")), grid, P(), P(), P())
    out_specs = (grid, grid, P(), P(), P())
    return jax.shard_map(
        on_device, mesh=mesh, in_specs=in_specs, out_specs=out_specs, check_vma=False
    )
```

```python
import functools
import math

import jax
import jax.numpy as jnp
from jax import lax
from jax.experimental import pallas as pl
from jax.experimental.layout import Layout, with_layout_constraint
from jax.experimental.pallas import tpu as pltpu
from jax.sharding import PartitionSpec as P

HEAD_DIM = 64
CF = 256
RADIUS = 3
REACH = 2 * RADIUS
EDGE = 8
SPAN = 2
WINDOW = SPAN + REACH

score_scale = 6.0
epsilon = 1e-06


def fourier(step_value):
    half_count = CF // 2
    ladder = jnp.arange(half_count, dtype=jnp.float32)
    frequency = jnp.exp(ladder * (-math.log(1000.0) / half_count))
    phase_angle = step_value.astype(jnp.float32) * frequency
    return jnp.concatenate([jnp.cos(phase_angle), jnp.sin(phase_angle)])


def exchange(to_next, to_previous, axis):
    count = lax.axis_size(axis)
    forward = [(i, i + 1) for i in range(count - 1)]
    backward = [(target, source) for source, target in forward]
    from_previous = lax.ppermute(to_next, axis, forward)
    from_next = lax.ppermute(to_previous, axis, backward)
    return from_previous, from_next


def nn(left, right):
    return lax.dot_general(left, right, (((1,), (0,)), ((), ())), preferred_element_type=jnp.float32)


def nt(left, right):
    return lax.dot_general(left, right, (((1,), (1,)), ((), ())), preferred_element_type=jnp.float32)


def tn(left, right):
    return lax.dot_general(left, right, (((0,), (0,)), ((), ())), preferred_element_type=jnp.float32)


def average_matrix(width):
    own_head = lax.broadcasted_iota(jnp.int32, (width, width), 0) // HEAD_DIM
    other_head = lax.broadcasted_iota(jnp.int32, (width, width), 1) // HEAD_DIM
    return jnp.where(own_head == other_head, 1.0 / HEAD_DIM, 0.0).astype(jnp.bfloat16)


def head_mean(values, average):
    coarse = values.astype(jnp.bfloat16)
    fine = (values - coarse.astype(jnp.float32)).astype(jnp.bfloat16)
    return nn(coarse, average) + nn(fine, average)


def normalized(pixels, adaptive):
    inverse = lax.rsqrt(jnp.mean(pixels * pixels, axis=-1, keepdims=True) + epsilon)
    return inverse, (pixels * inverse * adaptive).astype(jnp.bfloat16)


def projected(pixels, adaptive, qkv_ref, average):
    width = pixels.shape[-1]
    inverse, normed = normalized(pixels, adaptive)
    project = nn(normed, qkv_ref[...])
    query_raw = project[:, :width]
    key_raw = project[:, width : 2 * width]
    query_inv = lax.rsqrt(head_mean(query_raw * query_raw, average) + epsilon)
    key_inv = lax.rsqrt(head_mean(key_raw * key_raw, average) + epsilon)
    query = query_raw * query_inv * (score_scale / HEAD_DIM)
    return inverse, normed, query, key_raw * key_inv, project[:, 2 * width :], (query_raw, query_inv, key_raw, key_inv)


def head_picks(width):
    lane_head = lax.broadcasted_iota(jnp.int32, (1, width), 1) // HEAD_DIM
    return [jnp.where(lane_head == head, 1.0, 0.0) for head in range(width // HEAD_DIM)]


def spread(part):
    return jnp.concatenate([part * pick.astype(jnp.bfloat16) for pick in head_picks(part.shape[-1])], axis=0)


def soften(scores, slope, mask):
    exponent = jnp.exp(scores - score_scale) * mask
    denominator = jnp.maximum(jnp.sum(exponent, axis=0, keepdims=True), 1e-30)
    weights = (exponent * (1.0 / denominator)).astype(jnp.bfloat16)
    wide = weights.astype(jnp.float32)
    middle = jnp.sum(wide * slope, axis=0, keepdims=True)
    return weights, (wide * (slope - middle)).astype(jnp.bfloat16)


def combined(weights, grad_score, keys, values, queries, grads, rows, height, wanted, first, count):
    width = keys.shape[-1]
    picks = head_picks(width)

    def gathered(part):
        total = part[: SPAN * rows] * picks[0]
        for head in range(1, len(picks)):
            total = total + part[head * SPAN * rows : (head + 1) * SPAN * rows] * picks[head]
        return total.reshape(SPAN, rows, width)[:, :height]

    def kept(part):
        shape = (WINDOW, rows, part.shape[1])
        return part.reshape(shape)[first : first + count, :height].reshape(-1, part.shape[1])

    attended = grad_query = None
    if wanted:
        attended = gathered(tn(weights, values)).astype(jnp.bfloat16)
        grad_query = gathered(tn(grad_score, keys))
    shape = (count, height, width)
    return attended, grad_query, nn(kept(grad_score), queries).reshape(shape), nn(kept(weights), grads).reshape(shape)


def own_kernel(
    total_rows,
    place_ref,
    tok_ref,
    cot_ref,
    adaptive_ref,
    qkv_ref,
    out_ref,
    query_ref,
    key_ref,
    value_ref,
    grad_ref,
    mask_ref,
    query_raw_ref,
    query_inv_ref,
    key_raw_ref,
    key_inv_ref,
    attended_ref,
    grad_query_ref,
    grad_key_ref,
    grad_value_ref,
):
    cols, rows, width = tok_ref.shape
    lanes = mask_ref.shape[2]
    height = rows - 2 * EDGE
    row_first = place_ref[0]
    pixels = tok_ref[...].astype(jnp.float32).reshape(cols * rows, width)
    _, _, query, key, value, raw = projected(pixels, adaptive_ref[...], qkv_ref, average_matrix(width))
    query = query.astype(jnp.bfloat16)
    key = key.astype(jnp.bfloat16)
    value = value.astype(jnp.bfloat16)
    grad = nt(cot_ref[...].reshape(cols * rows, width), out_ref[...]).astype(jnp.bfloat16)
    for ref, values in ((query_ref, query), (key_ref, key), (value_ref, value), (grad_ref, grad)):
        ref[...] = values.reshape(cols, rows, width)
    for ref, values in zip((query_raw_ref, query_inv_ref, key_raw_ref, key_inv_ref), raw):
        ref[...] = values.reshape(cols, rows, width)[:, :height]

    def row_at(position):
        halo = jnp.where(position < height + EDGE, position - height - EDGE, position - EDGE)
        return jnp.where(position < height, position, halo)

    key_row = row_at(lax.broadcasted_iota(jnp.int32, (1, rows, 1), 1))
    key_col = lax.broadcasted_iota(jnp.int32, (WINDOW, 1, 1), 0)
    lane = lax.broadcasted_iota(jnp.int32, (1, 1, lanes), 2) % (SPAN * rows)
    query_row = row_at(lane % rows)
    query_col = lane // rows
    row_gap = key_row - query_row
    col_gap = key_col - query_col
    image_row = jnp.broadcast_to(row_first + key_row, row_gap.shape)
    near_row = (row_gap >= -RADIUS) & (row_gap <= RADIUS) & (image_row >= 0) & (image_row < total_rows)
    near_col = (col_gap >= 0) & (col_gap <= REACH)
    mask = jnp.where(near_row, 1.0, 0.0) * jnp.where(near_col, 1.0, 0.0)
    mask_ref[...] = mask

    pair = slice(RADIUS * rows, (RADIUS + SPAN) * rows)
    queries, grads = spread(query[pair]), spread(grad[pair])
    weights, grad_score = soften(nt(key, queries), nt(value, grads), mask.reshape(cols * rows, lanes))
    attended_ref[...], grad_query_ref[...], grad_key_ref[...], grad_value_ref[...] = combined(
        weights, grad_score, key, value, queries, grads, rows, height, True, 0, cols
    )


def side_pairs(
    starts,
    total_cols,
    place_ref,
    side_ref,
    adaptive_ref,
    qkv_ref,
    out_ref,
    own,
    mask_ref,
    side,
    attended_ref,
    grad_query_ref,
    grad_key_ref,
    grad_value_ref,
):
    cols, rows, width = own[0].shape
    height = rows - 2 * EDGE
    last = REACH + cols
    col_first = place_ref[1]
    left = starts[0] == 0
    pixels = side_ref[:REACH].astype(jnp.float32).reshape(REACH * rows, width)
    _, _, query, key, value, _ = projected(pixels, adaptive_ref[...], qkv_ref, average_matrix(width))
    for ref, values in zip(side, (query, key, value)):
        ref[...] = values.astype(jnp.bfloat16).reshape(REACH, rows, width)
    grad = nt(side_ref[REACH:].reshape(RADIUS * rows, width), out_ref[...])
    side[3][...] = grad.astype(jnp.bfloat16).reshape(RADIUS, rows, width)

    def columns(which, low, high):
        beside = side[which]
        base = (REACH - beside.shape[0]) if left else last
        parts = []
        if left and low < REACH:
            parts.append(beside[low - base : min(high, REACH) - base])
        if max(low, REACH) < min(high, last):
            parts.append(own[which][max(low, REACH) - REACH : min(high, last) - REACH])
        if not left and high > last:
            parts.append(beside[max(low, last) - base : high - base])
        joined = parts[0] if len(parts) == 1 else jnp.concatenate(parts, axis=0)
        return joined.reshape((high - low) * rows, width)

    def scored(start):
        first = start + RADIUS
        keys, values = columns(1, start, start + WINDOW), columns(2, start, start + WINDOW)
        queries, grads = spread(columns(0, first, first + SPAN)), spread(columns(3, first, first + SPAN))
        return nt(keys, queries), nt(values, grads), (keys, values, queries, grads)

    def softened(start, scores, slope):
        masks = []
        for column in range(start, start + WINDOW):
            mask = mask_ref[column - start]
            if column < REACH or column >= last:
                image_col = col_first + (column - REACH)
                mask = mask * jnp.where((image_col >= 0) & (image_col < total_cols), 1.0, 0.0)
            masks.append(mask)
        return soften(scores, slope, jnp.concatenate(masks, axis=0))

    done = 0
    following = scored(starts[0])
    for start in starts:
        scores, slope, blocks = following
        if start != starts[-1]:
            following = scored(start + SPAN)
        weights, grad_score = softened(start, scores, slope)
        low, high = max(start, REACH), min(start + WINDOW, last)
        first = start + RADIUS
        query_low, query_high = max(first, REACH), min(first + SPAN, last)
        attended, grad_query, grad_key, grad_value = combined(
            weights, grad_score, *blocks, rows, height, query_low < query_high, low - start, high - low
        )
        if query_low < query_high:
            there = pl.ds(done, query_high - query_low)
            attended_ref[there] = attended[query_low - first : query_high - first]
            grad_query_ref[there] = grad_query[query_low - first : query_high - first]
            done += query_high - query_low
        there = pl.ds(low - REACH, high - low)
        grad_key_ref[there] += grad_key
        grad_value_ref[there] += grad_value


def left_kernel(
    starts,
    total_cols,
    place_ref,
    side_ref,
    adaptive_ref,
    qkv_ref,
    out_ref,
    query_ref,
    key_ref,
    value_ref,
    grad_ref,
    mask_ref,
    own_grad_key_ref,
    own_grad_value_ref,
    attended_ref,
    grad_query_ref,
    grad_key_ref,
    grad_value_ref,
    *side,
):
    grad_key_ref[...] = own_grad_key_ref[...]
    grad_value_ref[...] = own_grad_value_ref[...]
    own = (query_ref, key_ref, value_ref, grad_ref)
    results = (attended_ref, grad_query_ref, grad_key_ref, grad_value_ref)
    side_pairs(starts, total_cols, place_ref, side_ref, adaptive_ref, qkv_ref, out_ref, own, mask_ref, side, *results)


def right_kernel(
    starts,
    total_cols,
    place_ref,
    tok_ref,
    cot_ref,
    side_ref,
    adaptive_ref,
    qkv_ref,
    out_ref,
    query_ref,
    key_ref,
    value_ref,
    grad_ref,
    mask_ref,
    query_raw_ref,
    query_inv_ref,
    key_raw_ref,
    key_inv_ref,
    own_attended_ref,
    own_grad_query_ref,
    left_attended_ref,
    left_grad_query_ref,
    left_grad_key_ref,
    left_grad_value_ref,
    result_ref,
    grad_tokens_ref,
    mine_ref,
    other_ref,
    attended_ref,
    grad_query_ref,
    grad_key_ref,
    grad_value_ref,
    whole_ref,
    *side,
):
    cols, rows, width = tok_ref.shape
    height = rows - 2 * EDGE
    image = place_ref[2]
    core = place_ref[3]
    step_value = place_ref[4]
    adaptive = adaptive_ref[...]
    factor = score_scale / HEAD_DIM
    average = average_matrix(width)
    grad_key_ref[...] = left_grad_key_ref[...]
    grad_value_ref[...] = left_grad_value_ref[...]
    own = (query_ref, key_ref, value_ref, grad_ref)
    results = (attended_ref, grad_query_ref, grad_key_ref, grad_value_ref)
    side_pairs(starts, total_cols, place_ref, side_ref, adaptive_ref, qkv_ref, out_ref, own, mask_ref, side, *results)

    tokens = cols * height
    pixels = tok_ref[:, :height].astype(jnp.float32).reshape(tokens, width)
    inverse, normed = normalized(pixels, adaptive)
    cot_own = cot_ref[:, :height].reshape(tokens, width)
    parts = (left_attended_ref[...], own_attended_ref[...], attended_ref[...])
    attended = jnp.concatenate(parts, axis=0).reshape(tokens, width)
    result = pixels + nn(attended, out_ref[...])
    result_ref[...] = result.astype(jnp.bfloat16).reshape(cols, height, width)
    whole_ref[:, 3 * width :] = tn(attended, cot_own)

    def back(raw, inv, grad, scale):
        return scale * inv * (grad - raw * inv * inv * head_mean(grad * raw, average))

    parts = (left_grad_query_ref[...], own_grad_query_ref[...], grad_query_ref[...])
    grad_query = jnp.concatenate(parts, axis=0).reshape(tokens, width)
    grad_key = grad_key_ref[...].reshape(tokens, width)
    grad_project = jnp.concatenate(
        [
            back(query_raw_ref[...].reshape(tokens, width), query_inv_ref[...].reshape(tokens, width), grad_query, factor).astype(jnp.bfloat16),
            back(key_raw_ref[...].reshape(tokens, width), key_inv_ref[...].reshape(tokens, width), grad_key, 1.0).astype(jnp.bfloat16),
            grad_value_ref[...].reshape(tokens, width).astype(jnp.bfloat16),
        ],
        axis=1,
    )
    whole_ref[:, : 3 * width] = tn(normed, grad_project)
    grad_normed = nt(grad_project, qkv_ref[...])
    scaled = grad_normed * adaptive
    inner = jnp.mean(scaled * pixels, axis=-1, keepdims=True)
    grad_pixels = inverse * (scaled - pixels * (inverse * inverse * inner))
    grad_tokens = cot_own.astype(jnp.float32) + grad_pixels
    grad_tokens_ref[...] = grad_tokens.astype(jnp.bfloat16).reshape(cols, height, width)
    grad_adaptive = jnp.sum(grad_normed * (pixels * inverse), axis=0, keepdims=True)

    half = width // CORES
    across = 4 * width // LANES
    line = lax.broadcasted_iota(jnp.int32, (SLOT, LANES), 0)
    lane = lax.broadcasted_iota(jnp.int32, (SLOT, LANES), 1)
    high = (step_value // 32).astype(jnp.float32)
    low = (step_value % 32).astype(jnp.float32)
    for ref, which in ((mine_ref, core), (other_ref, 1 - core)):
        part = whole_ref[pl.ds(pl.multiple_of(which * half, half), half), :].astype(jnp.bfloat16)
        for block in range(ref.shape[0]):
            top = block // across * LINES
            first = block % across * LANES
            ref[block, :LINES] = part[top : top + LINES, first : first + LANES]
            if block < width // LANES:
                side = jnp.where(line == image, grad_adaptive[:, block * LANES : (block + 1) * LANES], 0.0)
                if block == 0:
                    there = line == SLOT // 2 + image
                    side = jnp.where(there & (lane == 0), high, side)
                    side = jnp.where(there & (lane == 1), low, side)
                ref[block, LINES:] = side.astype(jnp.bfloat16)
            else:
                ref[block, LINES:] = jnp.zeros((SLOT, LANES), jnp.bfloat16)


def half_gradients(which, half_ref, qkv_ref, output_ref, qkv_half, output_half, sems):
    width = output_ref.shape[0]
    half = width // CORES
    across = 4 * width // LANES
    for block in range(half_ref.shape[0]):
        top = block // across * LINES
        first = block % across * LANES
        values = half_ref[block, :LINES].astype(jnp.float32)
        if first < 3 * width:
            qkv_half[top : top + LINES, first : first + LANES] = values
        else:
            output_half[top : top + LINES, first - 3 * width : first - 3 * width + LANES] = values
    there = pl.ds(pl.multiple_of(which * half, half), half)
    copies = (
        pltpu.make_async_copy(qkv_half, qkv_ref.at[there], sems.at[0]),
        pltpu.make_async_copy(output_half, output_ref.at[there], sems.at[1]),
    )
    for copy in copies:
        copy.start()
    return copies


def mine_kernel(senders, place_ref, mine_ref, qkv_ref, output_ref, time_ref, qkv_half, output_half, sems):
    images, share = senders
    width = output_ref.shape[0]
    copies = half_gradients(place_ref[3], mine_ref, qkv_ref, output_ref, qkv_half, output_half, sems)
    sides = [mine_ref[block, LINES:].astype(jnp.float32) for block in range(width // LANES)]
    adaptives = jnp.concatenate(sides, axis=1)
    adaptives = jnp.where(lax.broadcasted_iota(jnp.int32, adaptives.shape, 0) < images, adaptives, 0.0)
    ladder = lax.broadcasted_iota(jnp.int32, (1, CF // 2), 1).astype(jnp.float32)
    frequency = jnp.exp(ladder * (-math.log(1000.0) / (CF // 2)))
    steps = (sides[0][:, 0:1] * 32.0 + sides[0][:, 1:2]) / share
    steps = jnp.concatenate([steps[SLOT // 2 :], steps[: SLOT // 2] * 0.0], axis=0)
    angle = steps * frequency
    features = jnp.concatenate([jnp.cos(angle), jnp.sin(angle)], axis=1)
    time_ref[...] = lax.dot_general(
        features,
        adaptives,
        (((0,), (0,)), ((), ())),
        precision=lax.Precision.HIGHEST,
        preferred_element_type=jnp.float32,
    )
    for copy in copies:
        copy.wait()


def other_kernel(place_ref, other_ref, qkv_in, output_in, qkv_ref, output_ref, qkv_half, output_half, sems):
    for copy in half_gradients(1 - place_ref[3], other_ref, qkv_ref, output_ref, qkv_half, output_half, sems):
        copy.wait()


CORES = 2
PARTNER = ((0, 1), (1, 0))
SLOT = 8
LINES = 32
LANES = 128


def lying(values):
    return with_layout_constraint(values, Layout(major_to_minor=(0, 1, 2)))


def on_device(tokens, timesteps, cotangent, qkv_weight, output_weight, time_weight):
    height, cols, width = tokens.shape[1:]
    row_first = lax.axis_index("row") * height
    col_first = lax.axis_index("col") * cols
    total_rows = height * lax.axis_size("row")
    total_cols = cols * lax.axis_size("col")
    rows = height + 2 * EDGE

    def edge_rows(low, high):
        return lying(jnp.concatenate([tokens[0, low:high], cotangent[0, low:high]], axis=0))

    both = jnp.concatenate([tokens[0].transpose(1, 0, 2), cotangent[0].transpose(1, 0, 2)], axis=0)
    above, below = exchange(edge_rows(height - EDGE, height), edge_rows(0, EDGE), "row")
    above, below = (lying(rows_).transpose(1, 0, 2).reshape(cols, 2, EDGE, width) for rows_ in (above, below))
    above, below = (rows_.transpose(1, 0, 2, 3).reshape(2 * cols, EDGE, width) for rows_ in (above, below))
    both = jnp.concatenate([both, above, below], axis=1)
    tok, cot = both[:cols], both[cols:]
    to_next = jnp.concatenate([tok[cols - REACH :], cot[cols - RADIUS :]], axis=0)
    to_previous = jnp.concatenate([tok[:REACH], cot[:RADIUS]], axis=0)
    left, right = exchange(to_next, to_previous, "col")
    features = fourier(timesteps[0])
    adaptive = 1.0 + jnp.dot(
        features[None], time_weight.astype(jnp.float32), precision=lax.Precision.HIGHEST
    )
    image = lax.axis_index(("zone", "core"))
    place = [row_first, col_first, image, lax.axis_index("core"), timesteps[0]]
    place = jnp.stack(place).astype(jnp.int32)

    lanes = width // HEAD_DIM * SPAN * rows
    smem = pl.BlockSpec(memory_space=pltpu.SMEM)
    vmem = pl.BlockSpec(memory_space=pltpu.VMEM)
    limits = pltpu.CompilerParams(vmem_limit_bytes=40 * 2**20)
    tall = jax.ShapeDtypeStruct((cols, rows, width), jnp.bfloat16)
    block = jax.ShapeDtypeStruct((cols, height, width), jnp.bfloat16)
    exact = jax.ShapeDtypeStruct((cols, height, width), jnp.float32)
    masked = jax.ShapeDtypeStruct((WINDOW, rows, lanes), jnp.float32)
    pair = (
        jax.ShapeDtypeStruct((SPAN, height, width), jnp.bfloat16),
        jax.ShapeDtypeStruct((SPAN, height, width), jnp.float32),
    )
    prepared = pl.pallas_call(
        functools.partial(own_kernel, total_rows),
        out_shape=(tall,) * 4 + (masked,) + (exact,) * 4 + pair + (exact,) * 2,
        in_specs=[smem] + [vmem] * 5,
        out_specs=(vmem,) * 13,
        compiler_params=limits,
        cost_estimate=pl.CostEstimate(flops=1_000_000_000, bytes_accessed=4_000_000, transcendentals=200_000),
        name="own",
    )(place, tok, cot, adaptive, qkv_weight, output_weight)
    *own, mask, query_raw, query_inv, key_raw, key_inv, attended, grad_query, grad_key, grad_value = prepared
    starts = tuple(range(0, cols + REACH, SPAN))
    middle = starts.index(REACH)
    third = (cols - SPAN) // 2
    part = (
        jax.ShapeDtypeStruct((third, height, width), jnp.bfloat16),
        jax.ShapeDtypeStruct((third, height, width), jnp.float32),
    )
    side = [pltpu.VMEM((REACH, rows, width), jnp.bfloat16)] * 3 + [pltpu.VMEM((RADIUS, rows, width), jnp.bfloat16)]
    from_left = pl.pallas_call(
        functools.partial(left_kernel, starts[:middle], total_cols),
        out_shape=part + (exact,) * 2,
        in_specs=[smem] + [vmem] * 11,
        out_specs=(vmem,) * 4,
        scratch_shapes=side,
        compiler_params=limits,
        cost_estimate=pl.CostEstimate(flops=2_000_000_000, bytes_accessed=2_000_000, transcendentals=400_000),
        name="left",
    )(place, left, adaptive, qkv_weight, output_weight, *own, mask, grad_key, grad_value)
    pieces = width // CORES // LINES * (4 * width // LANES)
    chunks = jax.ShapeDtypeStruct((pieces, LINES + SLOT, LANES), jnp.bfloat16)
    result, grad_tokens, mine, other = pl.pallas_call(
        functools.partial(right_kernel, starts[middle + 1 :], total_cols),
        out_shape=(block, block, chunks, chunks),
        in_specs=[smem] + [vmem] * 21,
        out_specs=(vmem,) * 4,
        scratch_shapes=[
            pltpu.VMEM((third, height, width), jnp.bfloat16),
            pltpu.VMEM((third, height, width), jnp.float32),
            pltpu.VMEM((cols, height, width), jnp.float32),
            pltpu.VMEM((cols, height, width), jnp.float32),
            pltpu.VMEM((width, 4 * width), jnp.float32),
        ]
        + side,
        compiler_params=limits,
        cost_estimate=pl.CostEstimate(flops=3_000_000_000, bytes_accessed=3_000_000, transcendentals=400_000),
        name="right",
    )(
        place,
        tok,
        cot,
        right,
        adaptive,
        qkv_weight,
        output_weight,
        *own,
        mask,
        query_raw,
        query_inv,
        key_raw,
        key_inv,
        attended,
        grad_query,
        *from_left,
    )
    result = lying(result.transpose(1, 0, 2))
    grad_tokens = lying(grad_tokens.transpose(1, 0, 2))

    mine = summed(mine, other)
    mine, result, grad_tokens = lax.optimization_barrier((mine, result, grad_tokens))
    other = lax.ppermute(mine, "core", PARTNER)
    anywhere = pl.BlockSpec(memory_space=pl.ANY)
    gradients = (
        jax.ShapeDtypeStruct((width, 3 * width), jnp.float32),
        jax.ShapeDtypeStruct((width, width), jnp.float32),
    )
    halves = [
        pltpu.VMEM((width // CORES, 3 * width), jnp.float32),
        pltpu.VMEM((width // CORES, width), jnp.float32),
        pltpu.SemaphoreType.DMA((2,)),
    ]
    small = pltpu.CompilerParams(vmem_limit_bytes=8 * 2**20)
    senders = (lax.axis_size("zone") * CORES, lax.axis_size("row") * lax.axis_size("col"))
    total_qkv, total_output, total_time = pl.pallas_call(
        functools.partial(mine_kernel, senders),
        out_shape=gradients + (jax.ShapeDtypeStruct((CF, width), jnp.float32),),
        in_specs=[smem, vmem],
        out_specs=(anywhere, anywhere, vmem),
        scratch_shapes=halves,
        compiler_params=small,
        cost_estimate=pl.CostEstimate(flops=200_000_000, bytes_accessed=1_500_000, transcendentals=2_000),
        name="mine",
    )(place, mine)
    total_qkv, total_output = pl.pallas_call(
        other_kernel,
        out_shape=gradients,
        in_specs=[smem, vmem, anywhere, anywhere],
        out_specs=(anywhere, anywhere),
        scratch_shapes=halves,
        input_output_aliases={2: 0, 3: 1},
        compiler_params=small,
        cost_estimate=pl.CostEstimate(flops=200_000_000, bytes_accessed=1_000_000, transcendentals=0),
        name="other",
    )(place, other, total_qkv, total_output)
    return (result[None], grad_tokens[None], total_qkv, total_output, total_time)


def swap(pieces, axes):
    return lax.all_to_all(pieces, axes, 0, 0, tiled=True)


def total(pieces):
    return jnp.sum(pieces.astype(jnp.float32), axis=0).astype(jnp.bfloat16)


def copied(piece, axes):
    count = lax.axis_size(axes)
    return lax.optimization_barrier(jnp.broadcast_to(piece[None], (count,) + piece.shape))


def summed(mine, other):
    mine = total(jnp.stack([mine, lax.ppermute(other, "core", PARTNER)]))
    piece = total(swap(mine, "col"))
    piece = total(swap(copied(piece, ("zone", "row")), ("zone", "row")))
    return swap(copied(piece, "col"), "col")


def solution(mesh):
    shape = (mesh.shape["dp"] // CORES, CORES, mesh.shape["row"], mesh.shape["col"])
    mesh = jax.sharding.Mesh(mesh.devices.reshape(shape), ("zone", "core", "row", "col"))
    grid = P(("zone", "core"), "row", "col", None)
    in_specs = (grid, P(("zone", "core")), grid, P(), P(), P())
    out_specs = (grid, grid, P(), P(), P())
    return jax.shard_map(
        on_device, mesh=mesh, in_specs=in_specs, out_specs=out_specs, check_vma=False
    )
```

```python
import functools
import math

import jax
import jax.numpy as jnp
from jax import lax
from jax.experimental import pallas as pl
from jax.experimental.layout import Layout, with_layout_constraint
from jax.experimental.pallas import tpu as pltpu
from jax.sharding import PartitionSpec as P

HEAD_DIM = 64
CF = 256
RADIUS = 3
REACH = 2 * RADIUS
EDGE = 8
SPAN = 2
WINDOW = SPAN + REACH

score_scale = 6.0
epsilon = 1e-06


def fourier(step_value):
    half_count = CF // 2
    ladder = jnp.arange(half_count, dtype=jnp.float32)
    frequency = jnp.exp(ladder * (-math.log(1000.0) / half_count))
    phase_angle = step_value.astype(jnp.float32) * frequency
    return jnp.concatenate([jnp.cos(phase_angle), jnp.sin(phase_angle)])


def exchange(to_next, to_previous, axis):
    count = lax.axis_size(axis)
    forward = [(i, i + 1) for i in range(count - 1)]
    backward = [(target, source) for source, target in forward]
    from_previous = lax.ppermute(to_next, axis, forward)
    from_next = lax.ppermute(to_previous, axis, backward)
    return from_previous, from_next


def nn(left, right):
    return lax.dot_general(left, right, (((1,), (0,)), ((), ())), preferred_element_type=jnp.float32)


def nt(left, right):
    return lax.dot_general(left, right, (((1,), (1,)), ((), ())), preferred_element_type=jnp.float32)


def tn(left, right):
    return lax.dot_general(left, right, (((0,), (0,)), ((), ())), preferred_element_type=jnp.float32)


def average_matrix(width):
    own_head = lax.broadcasted_iota(jnp.int32, (width, width), 0) // HEAD_DIM
    other_head = lax.broadcasted_iota(jnp.int32, (width, width), 1) // HEAD_DIM
    return jnp.where(own_head == other_head, 1.0 / HEAD_DIM, 0.0).astype(jnp.bfloat16)


def head_mean(values, average):
    coarse = values.astype(jnp.bfloat16)
    fine = (values - coarse.astype(jnp.float32)).astype(jnp.bfloat16)
    return nn(coarse, average) + nn(fine, average)


def normalized(pixels, adaptive):
    inverse = lax.rsqrt(jnp.mean(pixels * pixels, axis=-1, keepdims=True) + epsilon)
    return inverse, (pixels * inverse * adaptive).astype(jnp.bfloat16)


def projected(pixels, adaptive, qkv_ref, average):
    width = pixels.shape[-1]
    inverse, normed = normalized(pixels, adaptive)
    project = nn(normed, qkv_ref[...])
    query_raw = project[:, :width]
    key_raw = project[:, width : 2 * width]
    query_inv = lax.rsqrt(head_mean(query_raw * query_raw, average) + epsilon)
    key_inv = lax.rsqrt(head_mean(key_raw * key_raw, average) + epsilon)
    query = query_raw * query_inv * (score_scale / HEAD_DIM)
    return inverse, normed, query, key_raw * key_inv, project[:, 2 * width :], (query_raw, query_inv, key_raw, key_inv)


def head_picks(width):
    lane_head = lax.broadcasted_iota(jnp.int32, (1, width), 1) // HEAD_DIM
    return [jnp.where(lane_head == head, 1.0, 0.0) for head in range(width // HEAD_DIM)]


def spread(part):
    return jnp.concatenate([part * pick.astype(jnp.bfloat16) for pick in head_picks(part.shape[-1])], axis=0)


def soften(scores, slope, mask):
    exponent = jnp.exp(scores - score_scale) * mask
    denominator = jnp.maximum(jnp.sum(exponent, axis=0, keepdims=True), 1e-30)
    weights = (exponent * (1.0 / denominator)).astype(jnp.bfloat16)
    wide = weights.astype(jnp.float32)
    middle = jnp.sum(wide * slope, axis=0, keepdims=True)
    return weights, (wide * (slope - middle)).astype(jnp.bfloat16)


def combined(weights, grad_score, keys, values, queries, grads, rows, height, wanted, first, count):
    width = keys.shape[-1]
    picks = head_picks(width)

    def gathered(part):
        total = part[: SPAN * rows] * picks[0]
        for head in range(1, len(picks)):
            total = total + part[head * SPAN * rows : (head + 1) * SPAN * rows] * picks[head]
        return total.reshape(SPAN, rows, width)[:, :height]

    def kept(part):
        shape = (WINDOW, rows, part.shape[1])
        return part.reshape(shape)[first : first + count, :height].reshape(-1, part.shape[1])

    attended = grad_query = None
    if wanted:
        attended = gathered(tn(weights, values)).astype(jnp.bfloat16)
        grad_query = gathered(tn(grad_score, keys))
    shape = (count, height, width)
    return attended, grad_query, nn(kept(grad_score), queries).reshape(shape), nn(kept(weights), grads).reshape(shape)


def own_kernel(
    total_rows,
    place_ref,
    tok_ref,
    cot_ref,
    adaptive_ref,
    qkv_ref,
    out_ref,
    query_ref,
    key_ref,
    value_ref,
    grad_ref,
    mask_ref,
    query_raw_ref,
    query_inv_ref,
    key_raw_ref,
    key_inv_ref,
    attended_ref,
    grad_query_ref,
    grad_key_ref,
    grad_value_ref,
):
    cols, rows, width = tok_ref.shape
    lanes = mask_ref.shape[2]
    height = rows - 2 * EDGE
    row_first = place_ref[0]
    pixels = tok_ref[...].astype(jnp.float32).reshape(cols * rows, width)
    _, _, query, key, value, raw = projected(pixels, adaptive_ref[...], qkv_ref, average_matrix(width))
    query = query.astype(jnp.bfloat16)
    key = key.astype(jnp.bfloat16)
    value = value.astype(jnp.bfloat16)
    grad = nt(cot_ref[...].reshape(cols * rows, width), out_ref[...]).astype(jnp.bfloat16)
    for ref, values in ((query_ref, query), (key_ref, key), (value_ref, value), (grad_ref, grad)):
        ref[...] = values.reshape(cols, rows, width)
    for ref, values in zip((query_raw_ref, query_inv_ref, key_raw_ref, key_inv_ref), raw):
        ref[...] = values.reshape(cols, rows, width)[:, :height]

    def row_at(position):
        halo = jnp.where(position < height + EDGE, position - height - EDGE, position - EDGE)
        return jnp.where(position < height, position, halo)

    key_row = row_at(lax.broadcasted_iota(jnp.int32, (1, rows, 1), 1))
    key_col = lax.broadcasted_iota(jnp.int32, (WINDOW, 1, 1), 0)
    lane = lax.broadcasted_iota(jnp.int32, (1, 1, lanes), 2) % (SPAN * rows)
    query_row = row_at(lane % rows)
    query_col = lane // rows
    row_gap = key_row - query_row
    col_gap = key_col - query_col
    image_row = jnp.broadcast_to(row_first + key_row, row_gap.shape)
    near_row = (row_gap >= -RADIUS) & (row_gap <= RADIUS) & (image_row >= 0) & (image_row < total_rows)
    near_col = (col_gap >= 0) & (col_gap <= REACH)
    mask = jnp.where(near_row, 1.0, 0.0) * jnp.where(near_col, 1.0, 0.0)
    mask_ref[...] = mask

    pair = slice(RADIUS * rows, (RADIUS + SPAN) * rows)
    queries, grads = spread(query[pair]), spread(grad[pair])
    weights, grad_score = soften(nt(key, queries), nt(value, grads), mask.reshape(cols * rows, lanes))
    attended_ref[...], grad_query_ref[...], grad_key_ref[...], grad_value_ref[...] = combined(
        weights, grad_score, key, value, queries, grads, rows, height, True, 0, cols
    )


def side_pairs(
    starts,
    total_cols,
    place_ref,
    side_ref,
    adaptive_ref,
    qkv_ref,
    out_ref,
    own,
    mask_ref,
    side,
    attended_ref,
    grad_query_ref,
    grad_key_ref,
    grad_value_ref,
):
    cols, rows, width = own[0].shape
    height = rows - 2 * EDGE
    last = REACH + cols
    col_first = place_ref[1]
    left = starts[0] == 0
    pixels = side_ref[:REACH].astype(jnp.float32).reshape(REACH * rows, width)
    _, _, query, key, value, _ = projected(pixels, adaptive_ref[...], qkv_ref, average_matrix(width))
    for ref, values in zip(side, (query, key, value)):
        ref[...] = values.astype(jnp.bfloat16).reshape(REACH, rows, width)
    grad = nt(side_ref[REACH:].reshape(RADIUS * rows, width), out_ref[...])
    side[3][...] = grad.astype(jnp.bfloat16).reshape(RADIUS, rows, width)

    def columns(which, low, high):
        beside = side[which]
        base = (REACH - beside.shape[0]) if left else last
        parts = []
        if left and low < REACH:
            parts.append(beside[low - base : min(high, REACH) - base])
        if max(low, REACH) < min(high, last):
            parts.append(own[which][max(low, REACH) - REACH : min(high, last) - REACH])
        if not left and high > last:
            parts.append(beside[max(low, last) - base : high - base])
        joined = parts[0] if len(parts) == 1 else jnp.concatenate(parts, axis=0)
        return joined.reshape((high - low) * rows, width)

    def scored(start):
        first = start + RADIUS
        keys, values = columns(1, start, start + WINDOW), columns(2, start, start + WINDOW)
        queries, grads = spread(columns(0, first, first + SPAN)), spread(columns(3, first, first + SPAN))
        return nt(keys, queries), nt(values, grads), (keys, values, queries, grads)

    def softened(start, scores, slope):
        masks = []
        for column in range(start, start + WINDOW):
            mask = mask_ref[column - start]
            if column < REACH or column >= last:
                image_col = col_first + (column - REACH)
                mask = mask * jnp.where((image_col >= 0) & (image_col < total_cols), 1.0, 0.0)
            masks.append(mask)
        return soften(scores, slope, jnp.concatenate(masks, axis=0))

    done = 0
    following = scored(starts[0])
    for start in starts:
        scores, slope, blocks = following
        if start != starts[-1]:
            following = scored(start + SPAN)
        weights, grad_score = softened(start, scores, slope)
        low, high = max(start, REACH), min(start + WINDOW, last)
        first = start + RADIUS
        query_low, query_high = max(first, REACH), min(first + SPAN, last)
        attended, grad_query, grad_key, grad_value = combined(
            weights, grad_score, *blocks, rows, height, query_low < query_high, low - start, high - low
        )
        if query_low < query_high:
            there = pl.ds(done, query_high - query_low)
            attended_ref[there] = attended[query_low - first : query_high - first]
            grad_query_ref[there] = grad_query[query_low - first : query_high - first]
            done += query_high - query_low
        there = pl.ds(low - REACH, high - low)
        grad_key_ref[there] += grad_key
        grad_value_ref[there] += grad_value


def left_kernel(
    starts,
    total_cols,
    place_ref,
    side_ref,
    adaptive_ref,
    qkv_ref,
    out_ref,
    query_ref,
    key_ref,
    value_ref,
    grad_ref,
    mask_ref,
    own_grad_key_ref,
    own_grad_value_ref,
    attended_ref,
    grad_query_ref,
    grad_key_ref,
    grad_value_ref,
    *side,
):
    grad_key_ref[...] = own_grad_key_ref[...]
    grad_value_ref[...] = own_grad_value_ref[...]
    own = (query_ref, key_ref, value_ref, grad_ref)
    results = (attended_ref, grad_query_ref, grad_key_ref, grad_value_ref)
    side_pairs(starts, total_cols, place_ref, side_ref, adaptive_ref, qkv_ref, out_ref, own, mask_ref, side, *results)


def right_kernel(
    starts,
    total_cols,
    place_ref,
    tok_ref,
    cot_ref,
    side_ref,
    adaptive_ref,
    qkv_ref,
    out_ref,
    query_ref,
    key_ref,
    value_ref,
    grad_ref,
    mask_ref,
    query_raw_ref,
    query_inv_ref,
    key_raw_ref,
    key_inv_ref,
    own_attended_ref,
    own_grad_query_ref,
    left_attended_ref,
    left_grad_query_ref,
    left_grad_key_ref,
    left_grad_value_ref,
    result_ref,
    grad_tokens_ref,
    mine_ref,
    other_ref,
    attended_ref,
    grad_query_ref,
    grad_key_ref,
    grad_value_ref,
    whole_ref,
    *side,
):
    cols, rows, width = tok_ref.shape
    height = rows - 2 * EDGE
    image = place_ref[2]
    core = place_ref[3]
    step_value = place_ref[4]
    adaptive = adaptive_ref[...]
    factor = score_scale / HEAD_DIM
    average = average_matrix(width)
    grad_key_ref[...] = left_grad_key_ref[...]
    grad_value_ref[...] = left_grad_value_ref[...]
    own = (query_ref, key_ref, value_ref, grad_ref)
    results = (attended_ref, grad_query_ref, grad_key_ref, grad_value_ref)
    side_pairs(starts, total_cols, place_ref, side_ref, adaptive_ref, qkv_ref, out_ref, own, mask_ref, side, *results)

    tokens = cols * height
    pixels = tok_ref[:, :height].astype(jnp.float32).reshape(tokens, width)
    inverse, normed = normalized(pixels, adaptive)
    cot_own = cot_ref[:, :height].reshape(tokens, width)
    parts = (left_attended_ref[...], own_attended_ref[...], attended_ref[...])
    attended = jnp.concatenate(parts, axis=0).reshape(tokens, width)
    result = pixels + nn(attended, out_ref[...])
    result_ref[...] = result.astype(jnp.bfloat16).reshape(cols, height, width)
    whole_ref[:, 3 * width :] = tn(attended, cot_own)

    def back(raw, inv, grad, scale):
        return scale * inv * (grad - raw * inv * inv * head_mean(grad * raw, average))

    parts = (left_grad_query_ref[...], own_grad_query_ref[...], grad_query_ref[...])
    grad_query = jnp.concatenate(parts, axis=0).reshape(tokens, width)
    grad_key = grad_key_ref[...].reshape(tokens, width)
    grad_project = jnp.concatenate(
        [
            back(query_raw_ref[...].reshape(tokens, width), query_inv_ref[...].reshape(tokens, width), grad_query, factor).astype(jnp.bfloat16),
            back(key_raw_ref[...].reshape(tokens, width), key_inv_ref[...].reshape(tokens, width), grad_key, 1.0).astype(jnp.bfloat16),
            grad_value_ref[...].reshape(tokens, width).astype(jnp.bfloat16),
        ],
        axis=1,
    )
    whole_ref[:, : 3 * width] = tn(normed, grad_project)
    grad_normed = nt(grad_project, qkv_ref[...])
    scaled = grad_normed * adaptive
    inner = jnp.mean(scaled * pixels, axis=-1, keepdims=True)
    grad_pixels = inverse * (scaled - pixels * (inverse * inverse * inner))
    grad_tokens = cot_own.astype(jnp.float32) + grad_pixels
    grad_tokens_ref[...] = grad_tokens.astype(jnp.bfloat16).reshape(cols, height, width)
    grad_adaptive = jnp.sum(grad_normed * (pixels * inverse), axis=0, keepdims=True)

    half = width // CORES
    across = 4 * width // LANES
    line = lax.broadcasted_iota(jnp.int32, (SLOT, LANES), 0)
    lane = lax.broadcasted_iota(jnp.int32, (SLOT, LANES), 1)
    low_half, high_half = grad_adaptive[:, :LANES], grad_adaptive[:, LANES:]
    adaptives = jnp.where(line == image, low_half, jnp.where(line == SLOT // 2 + image, high_half, 0.0))
    high = (step_value // 32).astype(jnp.float32)
    low = (step_value % 32).astype(jnp.float32)
    steps = jnp.where(line == image, jnp.where(lane == 0, high, jnp.where(lane == 1, low, 0.0)), 0.0)
    for ref, which in ((mine_ref, core), (other_ref, 1 - core)):
        part = whole_ref[pl.ds(pl.multiple_of(which * half, half), half), :].astype(jnp.bfloat16)
        for block in range(half // LINES * across):
            top = block // across * LINES
            first = block % across * LANES
            ref[pl.ds(block_line(block), LINES), :] = part[top : top + LINES, first : first + LANES]
            if block % 2 == 0:
                side = adaptives if block == 0 else steps if block == 2 else jnp.zeros((SLOT, LANES), jnp.float32)
                ref[pl.ds(block_line(block) + LINES, SLOT), :] = side.astype(jnp.bfloat16)


def block_line(block):
    return (2 * LINES + SLOT) * (block // 2) + (LINES + SLOT) * (block % 2)


def finish_kernel(senders, place_ref, mine_ref, other_ref, qkv_ref, output_ref, time_ref, qkv, output, time, sems):
    images, share = senders
    width = output.shape[0]
    half = width // CORES
    across = 4 * width // LANES
    core = place_ref[3]
    copies = []

    def send(source, target):
        copies.append(pltpu.make_async_copy(source, target, sems.at[len(copies)]))
        copies[-1].start()

    for ref, which in ((mine_ref, core), (other_ref, 1 - core)):
        for band in range(half // LINES):
            there = pl.ds(pl.multiple_of(which * half + band * LINES, LINES), LINES)
            for place in range(across):
                values = ref[pl.ds(block_line(band * across + place), LINES), :].astype(jnp.float32)
                first = place * LANES
                if first < 3 * width:
                    qkv[there, first : first + LANES] = values
                else:
                    output[there, first - 3 * width : first - 3 * width + LANES] = values
            send(qkv.at[there], qkv_ref.at[there])
        there = pl.ds(pl.multiple_of(which * half, half), half)
        send(output.at[there], output_ref.at[there])
    side = mine_ref[LINES : LINES + SLOT, :].astype(jnp.float32)
    half_slot = SLOT // 2
    adaptives = jnp.concatenate([side, jnp.concatenate([side[half_slot:], side[:half_slot]], axis=0)], axis=1)
    line = lax.broadcasted_iota(jnp.int32, (SLOT, 1), 0)
    adaptives = jnp.where(line < images, adaptives, 0.0)
    steps = mine_ref[pl.ds(block_line(2) + LINES, SLOT), :].astype(jnp.float32)
    steps = (steps[:, 0:1] * 32.0 + steps[:, 1:2]) / share
    ladder = lax.broadcasted_iota(jnp.int32, (1, CF // 2), 1).astype(jnp.float32)
    frequency = jnp.exp(ladder * (-math.log(1000.0) / (CF // 2)))
    angle = steps * frequency
    features = jnp.concatenate([jnp.cos(angle), jnp.sin(angle)], axis=1)
    time[...] = lax.dot_general(
        features,
        adaptives,
        (((0,), (0,)), ((), ())),
        precision=lax.Precision.HIGHEST,
        preferred_element_type=jnp.float32,
    )
    send(time, time_ref)
    for copy in copies:
        copy.wait()


CORES = 2
PARTNER = ((0, 1), (1, 0))
SLOT = 8
LINES = 32
LANES = 128


def lying(values):
    return with_layout_constraint(values, Layout(major_to_minor=(0, 1, 2)))


def on_device(tokens, timesteps, cotangent, qkv_weight, output_weight, time_weight):
    height, cols, width = tokens.shape[1:]
    row_first = lax.axis_index("row") * height
    col_first = lax.axis_index("col") * cols
    total_rows = height * lax.axis_size("row")
    total_cols = cols * lax.axis_size("col")
    rows = height + 2 * EDGE

    def edge_rows(low, high):
        return lying(jnp.concatenate([tokens[0, low:high], cotangent[0, low:high]], axis=0))

    both = jnp.concatenate([tokens[0].transpose(1, 0, 2), cotangent[0].transpose(1, 0, 2)], axis=0)
    above, below = exchange(edge_rows(height - EDGE, height), edge_rows(0, EDGE), "row")
    above, below = (lying(rows_).transpose(1, 0, 2).reshape(cols, 2, EDGE, width) for rows_ in (above, below))
    above, below = (rows_.transpose(1, 0, 2, 3).reshape(2 * cols, EDGE, width) for rows_ in (above, below))
    both = jnp.concatenate([both, above, below], axis=1)
    tok, cot = both[:cols], both[cols:]
    to_next = jnp.concatenate([tok[cols - REACH :], cot[cols - RADIUS :]], axis=0)
    to_previous = jnp.concatenate([tok[:REACH], cot[:RADIUS]], axis=0)
    left, right = exchange(to_next, to_previous, "col")
    features = fourier(timesteps[0])
    adaptive = 1.0 + jnp.dot(
        features[None], time_weight.astype(jnp.float32), precision=lax.Precision.HIGHEST
    )
    image = lax.axis_index(("zone", "core"))
    place = [row_first, col_first, image, lax.axis_index("core"), timesteps[0]]
    place = jnp.stack(place).astype(jnp.int32)

    lanes = width // HEAD_DIM * SPAN * rows
    smem = pl.BlockSpec(memory_space=pltpu.SMEM)
    vmem = pl.BlockSpec(memory_space=pltpu.VMEM)
    limits = pltpu.CompilerParams(vmem_limit_bytes=40 * 2**20)
    tall = jax.ShapeDtypeStruct((cols, rows, width), jnp.bfloat16)
    block = jax.ShapeDtypeStruct((cols, height, width), jnp.bfloat16)
    exact = jax.ShapeDtypeStruct((cols, height, width), jnp.float32)
    masked = jax.ShapeDtypeStruct((WINDOW, rows, lanes), jnp.float32)
    pair = (
        jax.ShapeDtypeStruct((SPAN, height, width), jnp.bfloat16),
        jax.ShapeDtypeStruct((SPAN, height, width), jnp.float32),
    )
    prepared = pl.pallas_call(
        functools.partial(own_kernel, total_rows),
        out_shape=(tall,) * 4 + (masked,) + (exact,) * 4 + pair + (exact,) * 2,
        in_specs=[smem] + [vmem] * 5,
        out_specs=(vmem,) * 13,
        compiler_params=limits,
        cost_estimate=pl.CostEstimate(flops=1_000_000_000, bytes_accessed=4_000_000, transcendentals=200_000),
        name="own",
    )(place, tok, cot, adaptive, qkv_weight, output_weight)
    *own, mask, query_raw, query_inv, key_raw, key_inv, attended, grad_query, grad_key, grad_value = prepared
    starts = tuple(range(0, cols + REACH, SPAN))
    middle = starts.index(REACH)
    third = (cols - SPAN) // 2
    part = (
        jax.ShapeDtypeStruct((third, height, width), jnp.bfloat16),
        jax.ShapeDtypeStruct((third, height, width), jnp.float32),
    )
    side = [pltpu.VMEM((REACH, rows, width), jnp.bfloat16)] * 3 + [pltpu.VMEM((RADIUS, rows, width), jnp.bfloat16)]
    from_left = pl.pallas_call(
        functools.partial(left_kernel, starts[:middle], total_cols),
        out_shape=part + (exact,) * 2,
        in_specs=[smem] + [vmem] * 11,
        out_specs=(vmem,) * 4,
        scratch_shapes=side,
        compiler_params=limits,
        cost_estimate=pl.CostEstimate(flops=2_000_000_000, bytes_accessed=2_000_000, transcendentals=400_000),
        name="left",
    )(place, left, adaptive, qkv_weight, output_weight, *own, mask, grad_key, grad_value)
    pieces = width // CORES // LINES * (4 * width // LANES)
    chunks = jax.ShapeDtypeStruct((pieces * (LINES + SLOT // 2), LANES), jnp.bfloat16)
    result, grad_tokens, mine, other = pl.pallas_call(
        functools.partial(right_kernel, starts[middle + 1 :], total_cols),
        out_shape=(block, block, chunks, chunks),
        in_specs=[smem] + [vmem] * 21,
        out_specs=(vmem,) * 4,
        scratch_shapes=[
            pltpu.VMEM((third, height, width), jnp.bfloat16),
            pltpu.VMEM((third, height, width), jnp.float32),
            pltpu.VMEM((cols, height, width), jnp.float32),
            pltpu.VMEM((cols, height, width), jnp.float32),
            pltpu.VMEM((width, 4 * width), jnp.float32),
        ]
        + side,
        compiler_params=limits,
        cost_estimate=pl.CostEstimate(flops=3_000_000_000, bytes_accessed=3_000_000, transcendentals=400_000),
        name="right",
    )(
        place,
        tok,
        cot,
        right,
        adaptive,
        qkv_weight,
        output_weight,
        *own,
        mask,
        query_raw,
        query_inv,
        key_raw,
        key_inv,
        attended,
        grad_query,
        *from_left,
    )
    result = result.transpose(1, 0, 2)
    grad_tokens = grad_tokens.transpose(1, 0, 2)
    mine = summed(mine, other)
    other = lax.ppermute(mine, "core", PARTNER)
    anywhere = pl.BlockSpec(memory_space=pl.ANY)
    gradients = ((width, 3 * width), (width, width), (CF, width))
    senders = (lax.axis_size("zone") * CORES, lax.axis_size("row") * lax.axis_size("col"))
    total_qkv, total_output, total_time = pl.pallas_call(
        functools.partial(finish_kernel, senders),
        out_shape=tuple(jax.ShapeDtypeStruct(shape, jnp.float32) for shape in gradients),
        in_specs=[smem, vmem, vmem],
        out_specs=(anywhere,) * 3,
        scratch_shapes=[pltpu.VMEM(shape, jnp.float32) for shape in gradients]
        + [pltpu.SemaphoreType.DMA((CORES * (width // CORES // LINES + 1) + 1,))],
        compiler_params=pltpu.CompilerParams(vmem_limit_bytes=16 * 2**20),
        cost_estimate=pl.CostEstimate(flops=200_000_000, bytes_accessed=2_000_000, transcendentals=2_000),
        name="finish",
    )(place, mine, other)
    return (result[None], grad_tokens[None], total_qkv, total_output, total_time)


def swap(pieces, axes):
    return lax.all_to_all(pieces, axes, 0, 0, tiled=True)


def total(pieces):
    return jnp.sum(pieces.astype(jnp.float32), axis=0).astype(jnp.bfloat16)


def copied(piece, axes):
    count = lax.axis_size(axes)
    return lax.optimization_barrier(jnp.broadcast_to(piece[None], (count,) + piece.shape))


def summed(mine, other):
    mine = total(jnp.stack([mine, lax.ppermute(other, "core", PARTNER)]))
    parts = lax.axis_size("col")
    pieces = mine.reshape(parts, mine.shape[0] // parts // 4, 4, LANES)
    piece = total(swap(pieces, "col"))
    piece = total(swap(copied(piece, ("zone", "row")), ("zone", "row")))
    return swap(copied(piece, "col"), "col").reshape(mine.shape)


def solution(mesh):
    shape = (mesh.shape["dp"] // CORES, CORES, mesh.shape["row"], mesh.shape["col"])
    mesh = jax.sharding.Mesh(mesh.devices.reshape(shape), ("zone", "core", "row", "col"))
    grid = P(("zone", "core"), "row", "col", None)
    in_specs = (grid, P(("zone", "core")), grid, P(), P(), P())
    out_specs = (grid, grid, P(), P(), P())
    return jax.shard_map(
        on_device, mesh=mesh, in_specs=in_specs, out_specs=out_specs, check_vma=False
    )
```

```python
import functools
import math

import jax
import jax.numpy as jnp
from jax import lax
from jax.experimental import pallas as pl
from jax.experimental.layout import Layout, with_layout_constraint
from jax.experimental.pallas import tpu as pltpu
from jax.sharding import PartitionSpec as P

HEAD_DIM = 64
CF = 256
RADIUS = 3
REACH = 2 * RADIUS
EDGE = 8
SPAN = 2
WINDOW = SPAN + REACH

score_scale = 6.0
epsilon = 1e-06


def fourier(step_value):
    half_count = CF // 2
    ladder = jnp.arange(half_count, dtype=jnp.float32)
    frequency = jnp.exp(ladder * (-math.log(1000.0) / half_count))
    phase_angle = step_value.astype(jnp.float32) * frequency
    return jnp.concatenate([jnp.cos(phase_angle), jnp.sin(phase_angle)])


def exchange(to_next, to_previous, axis):
    count = lax.axis_size(axis)
    forward = [(i, i + 1) for i in range(count - 1)]
    backward = [(target, source) for source, target in forward]
    from_previous = lax.ppermute(to_next, axis, forward)
    from_next = lax.ppermute(to_previous, axis, backward)
    return from_previous, from_next


def nn(left, right):
    return lax.dot_general(left, right, (((1,), (0,)), ((), ())), preferred_element_type=jnp.float32)


def nt(left, right):
    return lax.dot_general(left, right, (((1,), (1,)), ((), ())), preferred_element_type=jnp.float32)


def tn(left, right):
    return lax.dot_general(left, right, (((0,), (0,)), ((), ())), preferred_element_type=jnp.float32)


def average_matrix(width):
    own_head = lax.broadcasted_iota(jnp.int32, (width, width), 0) // HEAD_DIM
    other_head = lax.broadcasted_iota(jnp.int32, (width, width), 1) // HEAD_DIM
    return jnp.where(own_head == other_head, 1.0 / HEAD_DIM, 0.0).astype(jnp.bfloat16)


def head_mean(values, average):
    coarse = values.astype(jnp.bfloat16)
    fine = (values - coarse.astype(jnp.float32)).astype(jnp.bfloat16)
    return nn(coarse, average) + nn(fine, average)


def normalized(pixels, adaptive):
    inverse = lax.rsqrt(jnp.mean(pixels * pixels, axis=-1, keepdims=True) + epsilon)
    return inverse, (pixels * inverse * adaptive).astype(jnp.bfloat16)


def projected(pixels, adaptive, qkv_ref, average):
    width = pixels.shape[-1]
    inverse, normed = normalized(pixels, adaptive)
    project = nn(normed, qkv_ref[...])
    query_raw = project[:, :width]
    key_raw = project[:, width : 2 * width]
    query_inv = lax.rsqrt(head_mean(query_raw * query_raw, average) + epsilon)
    key_inv = lax.rsqrt(head_mean(key_raw * key_raw, average) + epsilon)
    query = query_raw * query_inv * (score_scale / HEAD_DIM)
    return inverse, normed, query, key_raw * key_inv, project[:, 2 * width :], (query_raw, query_inv, key_raw, key_inv)


def head_picks(width):
    lane_head = lax.broadcasted_iota(jnp.int32, (1, width), 1) // HEAD_DIM
    return [jnp.where(lane_head == head, 1.0, 0.0) for head in range(width // HEAD_DIM)]


def spread(part):
    return jnp.concatenate([part * pick.astype(jnp.bfloat16) for pick in head_picks(part.shape[-1])], axis=0)


def soften(scores, slope, mask):
    exponent = jnp.exp(scores - score_scale) * mask
    denominator = jnp.maximum(jnp.sum(exponent, axis=0, keepdims=True), 1e-30)
    weights = (exponent * (1.0 / denominator)).astype(jnp.bfloat16)
    wide = weights.astype(jnp.float32)
    middle = jnp.sum(wide * slope, axis=0, keepdims=True)
    return weights, (wide * (slope - middle)).astype(jnp.bfloat16)


def combined(weights, grad_score, keys, values, queries, grads, rows, height, wanted, first, count):
    width = keys.shape[-1]
    picks = head_picks(width)

    def gathered(part):
        total = part[: SPAN * rows] * picks[0]
        for head in range(1, len(picks)):
            total = total + part[head * SPAN * rows : (head + 1) * SPAN * rows] * picks[head]
        return total.reshape(SPAN, rows, width)[:, :height]

    def kept(part):
        shape = (WINDOW, rows, part.shape[1])
        return part.reshape(shape)[first : first + count, :height].reshape(-1, part.shape[1])

    attended = grad_query = None
    if wanted:
        attended = gathered(tn(weights, values)).astype(jnp.bfloat16)
        grad_query = gathered(tn(grad_score, keys))
    shape = (count, height, width)
    return attended, grad_query, nn(kept(grad_score), queries).reshape(shape), nn(kept(weights), grads).reshape(shape)


def early_kernel(
    total_rows,
    place_ref,
    tok_ref,
    cot_ref,
    adaptive_ref,
    qkv_ref,
    out_ref,
    query_ref,
    key_ref,
    value_ref,
    grad_ref,
    mask_ref,
    query_raw_ref,
    query_inv_ref,
    key_raw_ref,
    key_inv_ref,
):
    shape = tok_ref.shape
    cols, height, width = shape
    _, rows, lanes = mask_ref.shape
    row_first = place_ref[0]
    pixels = tok_ref[...].astype(jnp.float32).reshape(cols * height, width)
    _, _, query, key, value, raw = projected(pixels, adaptive_ref[...], qkv_ref, average_matrix(width))
    grad = nt(cot_ref[...].reshape(cols * height, width), out_ref[...])
    for ref, values in ((query_ref, query), (key_ref, key), (value_ref, value), (grad_ref, grad)):
        ref[...] = values.astype(jnp.bfloat16).reshape(shape)
    for ref, values in zip((query_raw_ref, query_inv_ref, key_raw_ref, key_inv_ref), raw):
        ref[...] = values.reshape(shape)

    def row_at(position):
        halo = jnp.where(position < height + EDGE, position - height - EDGE, position - EDGE)
        return jnp.where(position < height, position, halo)

    key_row = row_at(lax.broadcasted_iota(jnp.int32, (1, rows, 1), 1))
    key_col = lax.broadcasted_iota(jnp.int32, (WINDOW, 1, 1), 0)
    lane = lax.broadcasted_iota(jnp.int32, (1, 1, lanes), 2) % (SPAN * rows)
    query_row = row_at(lane % rows)
    query_col = lane // rows
    row_gap = key_row - query_row
    col_gap = key_col - query_col
    image_row = jnp.broadcast_to(row_first + key_row, row_gap.shape)
    near_row = (row_gap >= -RADIUS) & (row_gap <= RADIUS) & (image_row >= 0) & (image_row < total_rows)
    near_col = (col_gap >= 0) & (col_gap <= REACH)
    mask_ref[...] = jnp.where(near_row, 1.0, 0.0) * jnp.where(near_col, 1.0, 0.0)


def own_kernel(
    tok_ref,
    cot_ref,
    adaptive_ref,
    qkv_ref,
    out_ref,
    early_query_ref,
    early_key_ref,
    early_value_ref,
    early_grad_ref,
    mask_ref,
    query_ref,
    key_ref,
    value_ref,
    grad_ref,
    attended_ref,
    grad_query_ref,
    grad_key_ref,
    grad_value_ref,
):
    cols, rows, width = tok_ref.shape
    lanes = mask_ref.shape[2]
    height = rows - 2 * EDGE
    pixels = tok_ref[:, height:].astype(jnp.float32).reshape(cols * 2 * EDGE, width)
    _, _, query, key, value, _ = projected(pixels, adaptive_ref[...], qkv_ref, average_matrix(width))
    grad = nt(cot_ref[:, height:].reshape(cols * 2 * EDGE, width), out_ref[...])
    early = (early_query_ref, early_key_ref, early_value_ref, early_grad_ref)
    blocks = (query_ref, key_ref, value_ref, grad_ref)
    for ref, source, values in zip(blocks, early, (query, key, value, grad)):
        ref[:, :height] = source[...]
        ref[:, height:] = values.astype(jnp.bfloat16).reshape(cols, 2 * EDGE, width)

    key, value = (ref[...].reshape(cols * rows, width) for ref in (key_ref, value_ref))
    pair = pl.ds(RADIUS, SPAN)
    queries, grads = (spread(ref[pair].reshape(SPAN * rows, width)) for ref in (query_ref, grad_ref))
    mask = mask_ref[...].reshape(cols * rows, lanes)
    weights, grad_score = soften(nt(key, queries), nt(value, grads), mask)
    attended_ref[...], grad_query_ref[...], grad_key_ref[...], grad_value_ref[...] = combined(
        weights, grad_score, key, value, queries, grads, rows, height, True, 0, cols
    )


def side_pairs(
    starts,
    total_cols,
    place_ref,
    side_ref,
    adaptive_ref,
    qkv_ref,
    out_ref,
    own,
    mask_ref,
    side,
    attended_ref,
    grad_query_ref,
    grad_key_ref,
    grad_value_ref,
):
    cols, rows, width = own[0].shape
    height = rows - 2 * EDGE
    last = REACH + cols
    col_first = place_ref[1]
    left = starts[0] == 0
    pixels = side_ref[:REACH].astype(jnp.float32).reshape(REACH * rows, width)
    _, _, query, key, value, _ = projected(pixels, adaptive_ref[...], qkv_ref, average_matrix(width))
    for ref, values in zip(side, (query, key, value)):
        ref[...] = values.astype(jnp.bfloat16).reshape(REACH, rows, width)
    grad = nt(side_ref[REACH:].reshape(RADIUS * rows, width), out_ref[...])
    side[3][...] = grad.astype(jnp.bfloat16).reshape(RADIUS, rows, width)

    def columns(which, low, high):
        beside = side[which]
        base = (REACH - beside.shape[0]) if left else last
        parts = []
        if left and low < REACH:
            parts.append(beside[low - base : min(high, REACH) - base])
        if max(low, REACH) < min(high, last):
            parts.append(own[which][max(low, REACH) - REACH : min(high, last) - REACH])
        if not left and high > last:
            parts.append(beside[max(low, last) - base : high - base])
        joined = parts[0] if len(parts) == 1 else jnp.concatenate(parts, axis=0)
        return joined.reshape((high - low) * rows, width)

    def scored(start):
        first = start + RADIUS
        keys, values = columns(1, start, start + WINDOW), columns(2, start, start + WINDOW)
        queries, grads = spread(columns(0, first, first + SPAN)), spread(columns(3, first, first + SPAN))
        return nt(keys, queries), nt(values, grads), (keys, values, queries, grads)

    def softened(start, scores, slope):
        masks = []
        for column in range(start, start + WINDOW):
            mask = mask_ref[column - start]
            if column < REACH or column >= last:
                image_col = col_first + (column - REACH)
                mask = mask * jnp.where((image_col >= 0) & (image_col < total_cols), 1.0, 0.0)
            masks.append(mask)
        return soften(scores, slope, jnp.concatenate(masks, axis=0))

    done = 0
    following = scored(starts[0])
    for start in starts:
        scores, slope, blocks = following
        if start != starts[-1]:
            following = scored(start + SPAN)
        weights, grad_score = softened(start, scores, slope)
        low, high = max(start, REACH), min(start + WINDOW, last)
        first = start + RADIUS
        query_low, query_high = max(first, REACH), min(first + SPAN, last)
        attended, grad_query, grad_key, grad_value = combined(
            weights, grad_score, *blocks, rows, height, query_low < query_high, low - start, high - low
        )
        if query_low < query_high:
            there = pl.ds(done, query_high - query_low)
            attended_ref[there] = attended[query_low - first : query_high - first]
            grad_query_ref[there] = grad_query[query_low - first : query_high - first]
            done += query_high - query_low
        there = pl.ds(low - REACH, high - low)
        grad_key_ref[there] += grad_key
        grad_value_ref[there] += grad_value


def left_kernel(
    starts,
    total_cols,
    place_ref,
    side_ref,
    adaptive_ref,
    qkv_ref,
    out_ref,
    query_ref,
    key_ref,
    value_ref,
    grad_ref,
    mask_ref,
    own_grad_key_ref,
    own_grad_value_ref,
    attended_ref,
    grad_query_ref,
    grad_key_ref,
    grad_value_ref,
    *side,
):
    grad_key_ref[...] = own_grad_key_ref[...]
    grad_value_ref[...] = own_grad_value_ref[...]
    own = (query_ref, key_ref, value_ref, grad_ref)
    results = (attended_ref, grad_query_ref, grad_key_ref, grad_value_ref)
    side_pairs(starts, total_cols, place_ref, side_ref, adaptive_ref, qkv_ref, out_ref, own, mask_ref, side, *results)


def right_kernel(
    starts,
    total_cols,
    place_ref,
    tok_ref,
    cot_ref,
    side_ref,
    adaptive_ref,
    qkv_ref,
    out_ref,
    query_ref,
    key_ref,
    value_ref,
    grad_ref,
    mask_ref,
    query_raw_ref,
    query_inv_ref,
    key_raw_ref,
    key_inv_ref,
    own_attended_ref,
    own_grad_query_ref,
    left_attended_ref,
    left_grad_query_ref,
    left_grad_key_ref,
    left_grad_value_ref,
    result_ref,
    grad_tokens_ref,
    mine_ref,
    other_ref,
    attended_ref,
    grad_query_ref,
    grad_key_ref,
    grad_value_ref,
    whole_ref,
    *side,
):
    cols, rows, width = tok_ref.shape
    height = rows - 2 * EDGE
    image = place_ref[2]
    core = place_ref[3]
    step_value = place_ref[4]
    adaptive = adaptive_ref[...]
    factor = score_scale / HEAD_DIM
    average = average_matrix(width)
    grad_key_ref[...] = left_grad_key_ref[...]
    grad_value_ref[...] = left_grad_value_ref[...]
    own = (query_ref, key_ref, value_ref, grad_ref)
    results = (attended_ref, grad_query_ref, grad_key_ref, grad_value_ref)
    side_pairs(starts, total_cols, place_ref, side_ref, adaptive_ref, qkv_ref, out_ref, own, mask_ref, side, *results)

    tokens = cols * height
    pixels = tok_ref[:, :height].astype(jnp.float32).reshape(tokens, width)
    inverse, normed = normalized(pixels, adaptive)
    cot_own = cot_ref[:, :height].reshape(tokens, width)
    parts = (left_attended_ref[...], own_attended_ref[...], attended_ref[...])
    attended = jnp.concatenate(parts, axis=0).reshape(tokens, width)
    result = pixels + nn(attended, out_ref[...])
    result_ref[...] = result.astype(jnp.bfloat16).reshape(cols, height, width)
    whole_ref[:, 3 * width :] = tn(attended, cot_own)

    def back(raw, inv, grad, scale):
        return scale * inv * (grad - raw * inv * inv * head_mean(grad * raw, average))

    parts = (left_grad_query_ref[...], own_grad_query_ref[...], grad_query_ref[...])
    grad_query = jnp.concatenate(parts, axis=0).reshape(tokens, width)
    grad_key = grad_key_ref[...].reshape(tokens, width)
    grad_project = jnp.concatenate(
        [
            back(query_raw_ref[...].reshape(tokens, width), query_inv_ref[...].reshape(tokens, width), grad_query, factor).astype(jnp.bfloat16),
            back(key_raw_ref[...].reshape(tokens, width), key_inv_ref[...].reshape(tokens, width), grad_key, 1.0).astype(jnp.bfloat16),
            grad_value_ref[...].reshape(tokens, width).astype(jnp.bfloat16),
        ],
        axis=1,
    )
    whole_ref[:, : 3 * width] = tn(normed, grad_project)
    grad_normed = nt(grad_project, qkv_ref[...])
    scaled = grad_normed * adaptive
    inner = jnp.mean(scaled * pixels, axis=-1, keepdims=True)
    grad_pixels = inverse * (scaled - pixels * (inverse * inverse * inner))
    grad_tokens = cot_own.astype(jnp.float32) + grad_pixels
    grad_tokens_ref[...] = grad_tokens.astype(jnp.bfloat16).reshape(cols, height, width)
    grad_adaptive = jnp.sum(grad_normed * (pixels * inverse), axis=0, keepdims=True)

    half = width // CORES
    across = 4 * width // LANES
    line = lax.broadcasted_iota(jnp.int32, (SLOT, LANES), 0)
    lane = lax.broadcasted_iota(jnp.int32, (SLOT, LANES), 1)
    low_half, high_half = grad_adaptive[:, :LANES], grad_adaptive[:, LANES:]
    adaptives = jnp.where(line == image, low_half, jnp.where(line == SLOT // 2 + image, high_half, 0.0))
    high = (step_value // 32).astype(jnp.float32)
    low = (step_value % 32).astype(jnp.float32)
    steps = jnp.where(line == image, jnp.where(lane == 0, high, jnp.where(lane == 1, low, 0.0)), 0.0)
    for ref, which in ((mine_ref, core), (other_ref, 1 - core)):
        part = whole_ref[pl.ds(pl.multiple_of(which * half, half), half), :].astype(jnp.bfloat16)
        for block in range(half // LINES * across):
            top = block // across * LINES
            first = block % across * LANES
            ref[pl.ds(block_line(block), LINES), :] = part[top : top + LINES, first : first + LANES]
            if block % 2 == 0:
                side = adaptives if block == 0 else steps if block == 2 else jnp.zeros((SLOT, LANES), jnp.float32)
                ref[pl.ds(block_line(block) + LINES, SLOT), :] = side.astype(jnp.bfloat16)


def block_line(block):
    return (2 * LINES + SLOT) * (block // 2) + (LINES + SLOT) * (block % 2)


def finish_kernel(senders, place_ref, mine_ref, other_ref, qkv_ref, output_ref, time_ref, qkv, output, time, sems):
    images, share = senders
    width = output.shape[0]
    half = width // CORES
    across = 4 * width // LANES
    core = place_ref[3]
    copies = []

    def send(source, target):
        copies.append(pltpu.make_async_copy(source, target, sems.at[len(copies)]))
        copies[-1].start()

    for ref, which in ((mine_ref, core), (other_ref, 1 - core)):
        for band in range(half // LINES):
            there = pl.ds(pl.multiple_of(which * half + band * LINES, LINES), LINES)
            for place in range(across):
                values = ref[pl.ds(block_line(band * across + place), LINES), :].astype(jnp.float32)
                first = place * LANES
                if first < 3 * width:
                    qkv[there, first : first + LANES] = values
                else:
                    output[there, first - 3 * width : first - 3 * width + LANES] = values
            send(qkv.at[there], qkv_ref.at[there])
        there = pl.ds(pl.multiple_of(which * half, half), half)
        send(output.at[there], output_ref.at[there])
    side = mine_ref[LINES : LINES + SLOT, :].astype(jnp.float32)
    half_slot = SLOT // 2
    adaptives = jnp.concatenate([side, jnp.concatenate([side[half_slot:], side[:half_slot]], axis=0)], axis=1)
    line = lax.broadcasted_iota(jnp.int32, (SLOT, 1), 0)
    adaptives = jnp.where(line < images, adaptives, 0.0)
    steps = mine_ref[pl.ds(block_line(2) + LINES, SLOT), :].astype(jnp.float32)
    steps = (steps[:, 0:1] * 32.0 + steps[:, 1:2]) / share
    ladder = lax.broadcasted_iota(jnp.int32, (1, CF // 2), 1).astype(jnp.float32)
    frequency = jnp.exp(ladder * (-math.log(1000.0) / (CF // 2)))
    angle = steps * frequency
    features = jnp.concatenate([jnp.cos(angle), jnp.sin(angle)], axis=1)
    time[...] = lax.dot_general(
        features,
        adaptives,
        (((0,), (0,)), ((), ())),
        precision=lax.Precision.HIGHEST,
        preferred_element_type=jnp.float32,
    )
    send(time, time_ref)
    for copy in copies:
        copy.wait()


CORES = 2
PARTNER = ((0, 1), (1, 0))
SLOT = 8
LINES = 32
LANES = 128


def lying(values):
    return with_layout_constraint(values, Layout(major_to_minor=(0, 1, 2)))


def on_device(tokens, timesteps, cotangent, qkv_weight, output_weight, time_weight):
    height, cols, width = tokens.shape[1:]
    row_first = lax.axis_index("row") * height
    col_first = lax.axis_index("col") * cols
    total_rows = height * lax.axis_size("row")
    total_cols = cols * lax.axis_size("col")
    rows = height + 2 * EDGE

    def edge_rows(low, high):
        return lying(jnp.concatenate([tokens[0, low:high], cotangent[0, low:high]], axis=0))

    both = jnp.concatenate([tokens[0].transpose(1, 0, 2), cotangent[0].transpose(1, 0, 2)], axis=0)
    above, below = exchange(edge_rows(height - EDGE, height), edge_rows(0, EDGE), "row")
    above, below = (lying(rows_).transpose(1, 0, 2).reshape(cols, 2, EDGE, width) for rows_ in (above, below))
    above, below = (rows_.transpose(1, 0, 2, 3).reshape(2 * cols, EDGE, width) for rows_ in (above, below))
    both = jnp.concatenate([both, above, below], axis=1)
    tok, cot = both[:cols], both[cols:]
    early_tok, early_cot = tokens[0].transpose(1, 0, 2), cotangent[0].transpose(1, 0, 2)
    to_next = jnp.concatenate([tok[cols - REACH :], cot[cols - RADIUS :]], axis=0)
    to_previous = jnp.concatenate([tok[:REACH], cot[:RADIUS]], axis=0)
    left, right = exchange(to_next, to_previous, "col")
    features = fourier(timesteps[0])
    adaptive = 1.0 + jnp.dot(
        features[None], time_weight.astype(jnp.float32), precision=lax.Precision.HIGHEST
    )
    image = lax.axis_index(("zone", "core"))
    place = [row_first, col_first, image, lax.axis_index("core"), timesteps[0]]
    place = jnp.stack(place).astype(jnp.int32)

    lanes = width // HEAD_DIM * SPAN * rows
    smem = pl.BlockSpec(memory_space=pltpu.SMEM)
    vmem = pl.BlockSpec(memory_space=pltpu.VMEM)
    limits = pltpu.CompilerParams(vmem_limit_bytes=40 * 2**20)
    tall = jax.ShapeDtypeStruct((cols, rows, width), jnp.bfloat16)
    block = jax.ShapeDtypeStruct((cols, height, width), jnp.bfloat16)
    exact = jax.ShapeDtypeStruct((cols, height, width), jnp.float32)
    masked = jax.ShapeDtypeStruct((WINDOW, rows, lanes), jnp.float32)
    pair = (
        jax.ShapeDtypeStruct((SPAN, height, width), jnp.bfloat16),
        jax.ShapeDtypeStruct((SPAN, height, width), jnp.float32),
    )
    *early, mask, query_raw, query_inv, key_raw, key_inv = pl.pallas_call(
        functools.partial(early_kernel, total_rows),
        out_shape=(block,) * 4 + (masked,) + (exact,) * 4,
        in_specs=[smem] + [vmem] * 5,
        out_specs=(vmem,) * 9,
        compiler_params=limits,
        cost_estimate=pl.CostEstimate(flops=700_000_000, bytes_accessed=3_000_000, transcendentals=200_000),
        name="early",
    )(place, early_tok, early_cot, adaptive, qkv_weight, output_weight)
    *own, attended, grad_query, grad_key, grad_value = pl.pallas_call(
        own_kernel,
        out_shape=(tall,) * 4 + pair + (exact,) * 2,
        in_specs=[vmem] * 10,
        out_specs=(vmem,) * 8,
        compiler_params=limits,
        cost_estimate=pl.CostEstimate(flops=1_000_000_000, bytes_accessed=3_000_000, transcendentals=200_000),
        name="own",
    )(tok, cot, adaptive, qkv_weight, output_weight, *early, mask)
    starts = tuple(range(0, cols + REACH, SPAN))
    middle = starts.index(REACH)
    third = (cols - SPAN) // 2
    part = (
        jax.ShapeDtypeStruct((third, height, width), jnp.bfloat16),
        jax.ShapeDtypeStruct((third, height, width), jnp.float32),
    )
    side = [pltpu.VMEM((REACH, rows, width), jnp.bfloat16)] * 3 + [pltpu.VMEM((RADIUS, rows, width), jnp.bfloat16)]
    from_left = pl.pallas_call(
        functools.partial(left_kernel, starts[:middle], total_cols),
        out_shape=part + (exact,) * 2,
        in_specs=[smem] + [vmem] * 11,
        out_specs=(vmem,) * 4,
        scratch_shapes=side,
        compiler_params=limits,
        cost_estimate=pl.CostEstimate(flops=2_000_000_000, bytes_accessed=2_000_000, transcendentals=400_000),
        name="left",
    )(place, left, adaptive, qkv_weight, output_weight, *own, mask, grad_key, grad_value)
    pieces = width // CORES // LINES * (4 * width // LANES)
    chunks = jax.ShapeDtypeStruct((pieces * (LINES + SLOT // 2), LANES), jnp.bfloat16)
    result, grad_tokens, mine, other = pl.pallas_call(
        functools.partial(right_kernel, starts[middle + 1 :], total_cols),
        out_shape=(block, block, chunks, chunks),
        in_specs=[smem] + [vmem] * 21,
        out_specs=(vmem,) * 4,
        scratch_shapes=[
            pltpu.VMEM((third, height, width), jnp.bfloat16),
            pltpu.VMEM((third, height, width), jnp.float32),
            pltpu.VMEM((cols, height, width), jnp.float32),
            pltpu.VMEM((cols, height, width), jnp.float32),
            pltpu.VMEM((width, 4 * width), jnp.float32),
        ]
        + side,
        compiler_params=limits,
        cost_estimate=pl.CostEstimate(flops=3_000_000_000, bytes_accessed=3_000_000, transcendentals=400_000),
        name="right",
    )(
        place,
        tok,
        cot,
        right,
        adaptive,
        qkv_weight,
        output_weight,
        *own,
        mask,
        query_raw,
        query_inv,
        key_raw,
        key_inv,
        attended,
        grad_query,
        *from_left,
    )
    result = result.transpose(1, 0, 2)
    grad_tokens = grad_tokens.transpose(1, 0, 2)
    mine = summed(mine, other)
    other = lax.ppermute(mine, "core", PARTNER)
    anywhere = pl.BlockSpec(memory_space=pl.ANY)
    gradients = ((width, 3 * width), (width, width), (CF, width))
    senders = (lax.axis_size("zone") * CORES, lax.axis_size("row") * lax.axis_size("col"))
    total_qkv, total_output, total_time = pl.pallas_call(
        functools.partial(finish_kernel, senders),
        out_shape=tuple(jax.ShapeDtypeStruct(shape, jnp.float32) for shape in gradients),
        in_specs=[smem, vmem, vmem],
        out_specs=(anywhere,) * 3,
        scratch_shapes=[pltpu.VMEM(shape, jnp.float32) for shape in gradients]
        + [pltpu.SemaphoreType.DMA((CORES * (width // CORES // LINES + 1) + 1,))],
        compiler_params=pltpu.CompilerParams(vmem_limit_bytes=16 * 2**20),
        cost_estimate=pl.CostEstimate(flops=200_000_000, bytes_accessed=2_000_000, transcendentals=2_000),
        name="finish",
    )(place, mine, other)
    return (result[None], grad_tokens[None], total_qkv, total_output, total_time)


def swap(pieces, axes):
    return lax.all_to_all(pieces, axes, 0, 0, tiled=True)


def total(pieces):
    return jnp.sum(pieces.astype(jnp.float32), axis=0).astype(jnp.bfloat16)


def copied(piece, axes):
    count = lax.axis_size(axes)
    return lax.optimization_barrier(jnp.broadcast_to(piece[None], (count,) + piece.shape))


def summed(mine, other):
    mine = total(jnp.stack([mine, lax.ppermute(other, "core", PARTNER)]))
    parts = lax.axis_size("col")
    pieces = mine.reshape(parts, mine.shape[0] // parts // 4, 4, LANES)
    piece = total(swap(pieces, "col"))
    piece = total(swap(copied(piece, ("zone", "row")), ("zone", "row")))
    return swap(copied(piece, "col"), "col").reshape(mine.shape)


def solution(mesh):
    shape = (mesh.shape["dp"] // CORES, CORES, mesh.shape["row"], mesh.shape["col"])
    mesh = jax.sharding.Mesh(mesh.devices.reshape(shape), ("zone", "core", "row", "col"))
    grid = P(("zone", "core"), "row", "col", None)
    in_specs = (grid, P(("zone", "core")), grid, P(), P(), P())
    out_specs = (grid, grid, P(), P(), P())
    return jax.shard_map(
        on_device, mesh=mesh, in_specs=in_specs, out_specs=out_specs, check_vma=False
    )
```

```python
import functools
import math

import jax
import jax.numpy as jnp
from jax import lax
from jax.experimental import pallas as pl
from jax.experimental.layout import Layout, with_layout_constraint
from jax.experimental.pallas import tpu as pltpu
from jax.sharding import PartitionSpec as P

HEAD_DIM = 64
CF = 256
RADIUS = 3
REACH = 2 * RADIUS
EDGE = 8
SPAN = 2
WINDOW = SPAN + REACH

score_scale = 6.0
epsilon = 1e-06


def fourier(step_value):
    half_count = CF // 2
    ladder = jnp.arange(half_count, dtype=jnp.float32)
    frequency = jnp.exp(ladder * (-math.log(1000.0) / half_count))
    phase_angle = step_value.astype(jnp.float32) * frequency
    return jnp.concatenate([jnp.cos(phase_angle), jnp.sin(phase_angle)])


def exchange(to_next, to_previous, axis):
    count = lax.axis_size(axis)
    forward = [(i, i + 1) for i in range(count - 1)]
    backward = [(target, source) for source, target in forward]
    from_previous = lax.ppermute(to_next, axis, forward)
    from_next = lax.ppermute(to_previous, axis, backward)
    return from_previous, from_next


def nn(left, right):
    return lax.dot_general(left, right, (((1,), (0,)), ((), ())), preferred_element_type=jnp.float32)


def nt(left, right):
    return lax.dot_general(left, right, (((1,), (1,)), ((), ())), preferred_element_type=jnp.float32)


def tn(left, right):
    return lax.dot_general(left, right, (((0,), (0,)), ((), ())), preferred_element_type=jnp.float32)


def average_matrix(width):
    own_head = lax.broadcasted_iota(jnp.int32, (width, width), 0) // HEAD_DIM
    other_head = lax.broadcasted_iota(jnp.int32, (width, width), 1) // HEAD_DIM
    return jnp.where(own_head == other_head, 1.0 / HEAD_DIM, 0.0).astype(jnp.bfloat16)


def head_mean(values, average):
    coarse = values.astype(jnp.bfloat16)
    fine = (values - coarse.astype(jnp.float32)).astype(jnp.bfloat16)
    return nn(coarse, average) + nn(fine, average)


def normalized(pixels, adaptive):
    inverse = lax.rsqrt(jnp.mean(pixels * pixels, axis=-1, keepdims=True) + epsilon)
    return inverse, (pixels * inverse * adaptive).astype(jnp.bfloat16)


def projected(pixels, adaptive, qkv_ref, average):
    width = pixels.shape[-1]
    inverse, normed = normalized(pixels, adaptive)
    project = nn(normed, qkv_ref[...])
    query_raw = project[:, :width]
    key_raw = project[:, width : 2 * width]
    query_inv = lax.rsqrt(head_mean(query_raw * query_raw, average) + epsilon)
    key_inv = lax.rsqrt(head_mean(key_raw * key_raw, average) + epsilon)
    query = query_raw * query_inv * (score_scale / HEAD_DIM)
    return inverse, normed, query, key_raw * key_inv, project[:, 2 * width :], (query_raw, query_inv, key_raw, key_inv)


def head_picks(width):
    lane_head = lax.broadcasted_iota(jnp.int32, (1, width), 1) // HEAD_DIM
    return [jnp.where(lane_head == head, 1.0, 0.0) for head in range(width // HEAD_DIM)]


def spread(part):
    return jnp.concatenate([part * pick.astype(jnp.bfloat16) for pick in head_picks(part.shape[-1])], axis=0)


def soften(scores, slope, mask):
    exponent = jnp.exp(scores - score_scale) * mask
    denominator = jnp.maximum(jnp.sum(exponent, axis=0, keepdims=True), 1e-30)
    weights = (exponent * (1.0 / denominator)).astype(jnp.bfloat16)
    wide = weights.astype(jnp.float32)
    middle = jnp.sum(wide * slope, axis=0, keepdims=True)
    return weights, (wide * (slope - middle)).astype(jnp.bfloat16)


def combined(weights, grad_score, keys, values, queries, grads, rows, height, wanted, first, count):
    width = keys.shape[-1]
    picks = head_picks(width)

    def gathered(part):
        total = part[: SPAN * rows] * picks[0]
        for head in range(1, len(picks)):
            total = total + part[head * SPAN * rows : (head + 1) * SPAN * rows] * picks[head]
        return total.reshape(SPAN, rows, width)[:, :height]

    def kept(part):
        shape = (WINDOW, rows, part.shape[1])
        return part.reshape(shape)[first : first + count, :height].reshape(-1, part.shape[1])

    attended = grad_query = None
    if wanted:
        attended = gathered(tn(weights, values)).astype(jnp.bfloat16)
        grad_query = gathered(tn(grad_score, keys))
    shape = (count, height, width)
    return attended, grad_query, nn(kept(grad_score), queries).reshape(shape), nn(kept(weights), grads).reshape(shape)


def own_kernel(
    total_rows,
    place_ref,
    tok_ref,
    cot_ref,
    adaptive_ref,
    qkv_ref,
    out_ref,
    query_ref,
    key_ref,
    value_ref,
    grad_ref,
    mask_ref,
    query_raw_ref,
    query_inv_ref,
    key_raw_ref,
    key_inv_ref,
    attended_ref,
    grad_query_ref,
    grad_key_ref,
    grad_value_ref,
):
    cols, rows, width = tok_ref.shape
    lanes = mask_ref.shape[2]
    height = rows - 2 * EDGE
    row_first = place_ref[0]
    pixels = tok_ref[...].astype(jnp.float32).reshape(cols * rows, width)
    _, _, query, key, value, raw = projected(pixels, adaptive_ref[...], qkv_ref, average_matrix(width))
    query = query.astype(jnp.bfloat16)
    key = key.astype(jnp.bfloat16)
    value = value.astype(jnp.bfloat16)
    grad = nt(cot_ref[...].reshape(cols * rows, width), out_ref[...]).astype(jnp.bfloat16)
    for ref, values in ((query_ref, query), (key_ref, key), (value_ref, value), (grad_ref, grad)):
        ref[...] = values.reshape(cols, rows, width)
    for ref, values in zip((query_raw_ref, query_inv_ref, key_raw_ref, key_inv_ref), raw):
        ref[...] = values.reshape(cols, rows, width)[:, :height]

    def row_at(position):
        halo = jnp.where(position < height + EDGE, position - height - EDGE, position - EDGE)
        return jnp.where(position < height, position, halo)

    key_row = row_at(lax.broadcasted_iota(jnp.int32, (1, rows, 1), 1))
    key_col = lax.broadcasted_iota(jnp.int32, (WINDOW, 1, 1), 0)
    lane = lax.broadcasted_iota(jnp.int32, (1, 1, lanes), 2) % (SPAN * rows)
    query_row = row_at(lane % rows)
    query_col = lane // rows
    row_gap = key_row - query_row
    col_gap = key_col - query_col
    image_row = jnp.broadcast_to(row_first + key_row, row_gap.shape)
    near_row = (row_gap >= -RADIUS) & (row_gap <= RADIUS) & (image_row >= 0) & (image_row < total_rows)
    near_col = (col_gap >= 0) & (col_gap <= REACH)
    mask = jnp.where(near_row, 1.0, 0.0) * jnp.where(near_col, 1.0, 0.0)
    mask_ref[...] = mask

    pair = slice(RADIUS * rows, (RADIUS + SPAN) * rows)
    queries, grads = spread(query[pair]), spread(grad[pair])
    weights, grad_score = soften(nt(key, queries), nt(value, grads), mask.reshape(cols * rows, lanes))
    attended_ref[...], grad_query_ref[...], grad_key_ref[...], grad_value_ref[...] = combined(
        weights, grad_score, key, value, queries, grads, rows, height, True, 0, cols
    )


def side_pairs(
    starts,
    total_cols,
    place_ref,
    side_ref,
    adaptive_ref,
    qkv_ref,
    out_ref,
    own,
    mask_ref,
    side,
    attended_ref,
    grad_query_ref,
    grad_key_ref,
    grad_value_ref,
):
    cols, rows, width = own[0].shape
    height = rows - 2 * EDGE
    last = REACH + cols
    col_first = place_ref[1]
    left = starts[0] == 0
    pixels = side_ref[:REACH].astype(jnp.float32).reshape(REACH * rows, width)
    average = average_matrix(width)
    _, normed = normalized(pixels, adaptive_ref[...])
    project = nn(normed, qkv_ref[:, width:])
    key_raw = project[:, :width]
    key = key_raw * lax.rsqrt(head_mean(key_raw * key_raw, average) + epsilon)
    for ref, values in zip(side[1:3], (key, project[:, width:])):
        ref[...] = values.astype(jnp.bfloat16).reshape(REACH, rows, width)
    asking = slice((REACH - RADIUS) * rows, REACH * rows) if left else slice(0, RADIUS * rows)
    query_raw = nn(normed[asking], qkv_ref[:, :width])
    query_inv = lax.rsqrt(head_mean(query_raw * query_raw, average) + epsilon)
    query = query_raw * query_inv * (score_scale / HEAD_DIM)
    side[0][...] = query.astype(jnp.bfloat16).reshape(RADIUS, rows, width)
    grad = nt(side_ref[REACH:].reshape(RADIUS * rows, width), out_ref[...])
    side[3][...] = grad.astype(jnp.bfloat16).reshape(RADIUS, rows, width)

    def columns(which, low, high):
        beside = side[which]
        base = (REACH - beside.shape[0]) if left else last
        parts = []
        if left and low < REACH:
            parts.append(beside[low - base : min(high, REACH) - base])
        if max(low, REACH) < min(high, last):
            parts.append(own[which][max(low, REACH) - REACH : min(high, last) - REACH])
        if not left and high > last:
            parts.append(beside[max(low, last) - base : high - base])
        joined = parts[0] if len(parts) == 1 else jnp.concatenate(parts, axis=0)
        return joined.reshape((high - low) * rows, width)

    def scored(start):
        first = start + RADIUS
        keys, values = columns(1, start, start + WINDOW), columns(2, start, start + WINDOW)
        queries, grads = spread(columns(0, first, first + SPAN)), spread(columns(3, first, first + SPAN))
        return nt(keys, queries), nt(values, grads), (keys, values, queries, grads)

    def softened(start, scores, slope):
        masks = []
        for column in range(start, start + WINDOW):
            mask = mask_ref[column - start]
            if column < REACH or column >= last:
                image_col = col_first + (column - REACH)
                mask = mask * jnp.where((image_col >= 0) & (image_col < total_cols), 1.0, 0.0)
            masks.append(mask)
        return soften(scores, slope, jnp.concatenate(masks, axis=0))

    done = 0
    following = scored(starts[0])
    for start in starts:
        scores, slope, blocks = following
        if start != starts[-1]:
            following = scored(start + SPAN)
        weights, grad_score = softened(start, scores, slope)
        low, high = max(start, REACH), min(start + WINDOW, last)
        first = start + RADIUS
        query_low, query_high = max(first, REACH), min(first + SPAN, last)
        attended, grad_query, grad_key, grad_value = combined(
            weights, grad_score, *blocks, rows, height, query_low < query_high, low - start, high - low
        )
        if query_low < query_high:
            there = pl.ds(done, query_high - query_low)
            attended_ref[there] = attended[query_low - first : query_high - first]
            grad_query_ref[there] = grad_query[query_low - first : query_high - first]
            done += query_high - query_low
        there = pl.ds(low - REACH, high - low)
        grad_key_ref[there] += grad_key
        grad_value_ref[there] += grad_value


def left_kernel(
    starts,
    total_cols,
    place_ref,
    side_ref,
    adaptive_ref,
    qkv_ref,
    out_ref,
    query_ref,
    key_ref,
    value_ref,
    grad_ref,
    mask_ref,
    own_grad_key_ref,
    own_grad_value_ref,
    attended_ref,
    grad_query_ref,
    grad_key_ref,
    grad_value_ref,
    *side,
):
    grad_key_ref[...] = own_grad_key_ref[...]
    grad_value_ref[...] = own_grad_value_ref[...]
    own = (query_ref, key_ref, value_ref, grad_ref)
    results = (attended_ref, grad_query_ref, grad_key_ref, grad_value_ref)
    side_pairs(starts, total_cols, place_ref, side_ref, adaptive_ref, qkv_ref, out_ref, own, mask_ref, side, *results)


def right_kernel(
    starts,
    total_cols,
    place_ref,
    tok_ref,
    cot_ref,
    side_ref,
    adaptive_ref,
    qkv_ref,
    out_ref,
    query_ref,
    key_ref,
    value_ref,
    grad_ref,
    mask_ref,
    query_raw_ref,
    query_inv_ref,
    key_raw_ref,
    key_inv_ref,
    own_attended_ref,
    own_grad_query_ref,
    left_attended_ref,
    left_grad_query_ref,
    left_grad_key_ref,
    left_grad_value_ref,
    result_ref,
    grad_tokens_ref,
    mine_ref,
    other_ref,
    attended_ref,
    grad_query_ref,
    grad_key_ref,
    grad_value_ref,
    whole_ref,
    *side,
):
    cols, rows, width = tok_ref.shape
    height = rows - 2 * EDGE
    image = place_ref[2]
    core = place_ref[3]
    step_value = place_ref[4]
    adaptive = adaptive_ref[...]
    factor = score_scale / HEAD_DIM
    average = average_matrix(width)
    grad_key_ref[...] = left_grad_key_ref[...]
    grad_value_ref[...] = left_grad_value_ref[...]
    own = (query_ref, key_ref, value_ref, grad_ref)
    results = (attended_ref, grad_query_ref, grad_key_ref, grad_value_ref)
    side_pairs(starts, total_cols, place_ref, side_ref, adaptive_ref, qkv_ref, out_ref, own, mask_ref, side, *results)

    tokens = cols * height
    pixels = tok_ref[:, :height].astype(jnp.float32).reshape(tokens, width)
    inverse, normed = normalized(pixels, adaptive)
    cot_own = cot_ref[:, :height].reshape(tokens, width)
    parts = (left_attended_ref[...], own_attended_ref[...], attended_ref[...])
    attended = jnp.concatenate(parts, axis=0).reshape(tokens, width)
    result = pixels + nn(attended, out_ref[...])
    result_ref[...] = result.astype(jnp.bfloat16).reshape(cols, height, width)
    whole_ref[:, 3 * width :] = tn(attended, cot_own)

    def back(raw, inv, grad, scale):
        return scale * inv * (grad - raw * inv * inv * head_mean(grad * raw, average))

    parts = (left_grad_query_ref[...], own_grad_query_ref[...], grad_query_ref[...])
    grad_query = jnp.concatenate(parts, axis=0).reshape(tokens, width)
    grad_key = grad_key_ref[...].reshape(tokens, width)
    grad_project = jnp.concatenate(
        [
            back(query_raw_ref[...].reshape(tokens, width), query_inv_ref[...].reshape(tokens, width), grad_query, factor).astype(jnp.bfloat16),
            back(key_raw_ref[...].reshape(tokens, width), key_inv_ref[...].reshape(tokens, width), grad_key, 1.0).astype(jnp.bfloat16),
            grad_value_ref[...].reshape(tokens, width).astype(jnp.bfloat16),
        ],
        axis=1,
    )
    whole_ref[:, : 3 * width] = tn(normed, grad_project)
    grad_normed = nt(grad_project, qkv_ref[...])
    scaled = grad_normed * adaptive
    inner = jnp.mean(scaled * pixels, axis=-1, keepdims=True)
    grad_pixels = inverse * (scaled - pixels * (inverse * inverse * inner))
    grad_tokens = cot_own.astype(jnp.float32) + grad_pixels
    grad_tokens_ref[...] = grad_tokens.astype(jnp.bfloat16).reshape(cols, height, width)
    grad_adaptive = jnp.sum(grad_normed * (pixels * inverse), axis=0, keepdims=True)

    half = width // CORES
    across = 4 * width // LANES
    line = lax.broadcasted_iota(jnp.int32, (SLOT, LANES), 0)
    lane = lax.broadcasted_iota(jnp.int32, (SLOT, LANES), 1)
    low_half, high_half = grad_adaptive[:, :LANES], grad_adaptive[:, LANES:]
    adaptives = jnp.where(line == image, low_half, jnp.where(line == SLOT // 2 + image, high_half, 0.0))
    high = (step_value // 32).astype(jnp.float32)
    low = (step_value % 32).astype(jnp.float32)
    steps = jnp.where(line == image, jnp.where(lane == 0, high, jnp.where(lane == 1, low, 0.0)), 0.0)
    for ref, which in ((mine_ref, core), (other_ref, 1 - core)):
        part = whole_ref[pl.ds(pl.multiple_of(which * half, half), half), :].astype(jnp.bfloat16)
        for block in range(half // LINES * across):
            top = block // across * LINES
            first = block % across * LANES
            ref[pl.ds(block_line(block), LINES), :] = part[top : top + LINES, first : first + LANES]
            if block % 2 == 0:
                side = adaptives if block == 0 else steps if block == 2 else jnp.zeros((SLOT, LANES), jnp.float32)
                ref[pl.ds(block_line(block) + LINES, SLOT), :] = side.astype(jnp.bfloat16)


def block_line(block):
    return (2 * LINES + SLOT) * (block // 2) + (LINES + SLOT) * (block % 2)


def finish_kernel(senders, place_ref, mine_ref, other_ref, qkv_ref, output_ref, time_ref, qkv, output, time, sems):
    images, share = senders
    width = output.shape[0]
    half = width // CORES
    across = 4 * width // LANES
    core = place_ref[3]
    copies = []

    def send(source, target):
        copies.append(pltpu.make_async_copy(source, target, sems.at[len(copies)]))
        copies[-1].start()

    for ref, which in ((mine_ref, core), (other_ref, 1 - core)):
        for band in range(half // LINES):
            there = pl.ds(pl.multiple_of(which * half + band * LINES, LINES), LINES)
            for place in range(across):
                values = ref[pl.ds(block_line(band * across + place), LINES), :].astype(jnp.float32)
                first = place * LANES
                if first < 3 * width:
                    qkv[there, first : first + LANES] = values
                else:
                    output[there, first - 3 * width : first - 3 * width + LANES] = values
            send(qkv.at[there], qkv_ref.at[there])
        there = pl.ds(pl.multiple_of(which * half, half), half)
        send(output.at[there], output_ref.at[there])
    side = mine_ref[LINES : LINES + SLOT, :].astype(jnp.float32)
    half_slot = SLOT // 2
    adaptives = jnp.concatenate([side, jnp.concatenate([side[half_slot:], side[:half_slot]], axis=0)], axis=1)
    line = lax.broadcasted_iota(jnp.int32, (SLOT, 1), 0)
    adaptives = jnp.where(line < images, adaptives, 0.0)
    steps = mine_ref[pl.ds(block_line(2) + LINES, SLOT), :].astype(jnp.float32)
    steps = (steps[:, 0:1] * 32.0 + steps[:, 1:2]) / share
    ladder = lax.broadcasted_iota(jnp.int32, (1, CF // 2), 1).astype(jnp.float32)
    frequency = jnp.exp(ladder * (-math.log(1000.0) / (CF // 2)))
    angle = steps * frequency
    features = jnp.concatenate([jnp.cos(angle), jnp.sin(angle)], axis=1)
    time[...] = lax.dot_general(
        features,
        adaptives,
        (((0,), (0,)), ((), ())),
        precision=lax.Precision.HIGHEST,
        preferred_element_type=jnp.float32,
    )
    send(time, time_ref)
    for copy in copies:
        copy.wait()


CORES = 2
PARTNER = ((0, 1), (1, 0))
SLOT = 8
LINES = 32
LANES = 128


def lying(values):
    return with_layout_constraint(values, Layout(major_to_minor=(0, 1, 2)))


def on_device(tokens, timesteps, cotangent, qkv_weight, output_weight, time_weight):
    height, cols, width = tokens.shape[1:]
    row_first = lax.axis_index("row") * height
    col_first = lax.axis_index("col") * cols
    total_rows = height * lax.axis_size("row")
    total_cols = cols * lax.axis_size("col")
    rows = height + 2 * EDGE

    def edge_rows(low, high):
        return lying(jnp.concatenate([tokens[0, low:high], cotangent[0, low:high]], axis=0))

    both = jnp.concatenate([tokens[0].transpose(1, 0, 2), cotangent[0].transpose(1, 0, 2)], axis=0)
    above, below = exchange(edge_rows(height - EDGE, height), edge_rows(0, EDGE), "row")
    above, below = (lying(rows_).transpose(1, 0, 2).reshape(cols, 2, EDGE, width) for rows_ in (above, below))
    above, below = (rows_.transpose(1, 0, 2, 3).reshape(2 * cols, EDGE, width) for rows_ in (above, below))
    both = jnp.concatenate([both, above, below], axis=1)
    tok, cot = both[:cols], both[cols:]
    to_next = jnp.concatenate([tok[cols - REACH :], cot[cols - RADIUS :]], axis=0)
    to_previous = jnp.concatenate([tok[:REACH], cot[:RADIUS]], axis=0)
    left, right = exchange(to_next, to_previous, "col")
    features = fourier(timesteps[0])
    adaptive = 1.0 + jnp.dot(
        features[None], time_weight.astype(jnp.float32), precision=lax.Precision.HIGHEST
    )
    image = lax.axis_index(("zone", "core"))
    place = [row_first, col_first, image, lax.axis_index("core"), timesteps[0]]
    place = jnp.stack(place).astype(jnp.int32)

    lanes = width // HEAD_DIM * SPAN * rows
    smem = pl.BlockSpec(memory_space=pltpu.SMEM)
    vmem = pl.BlockSpec(memory_space=pltpu.VMEM)
    limits = pltpu.CompilerParams(vmem_limit_bytes=40 * 2**20)
    tall = jax.ShapeDtypeStruct((cols, rows, width), jnp.bfloat16)
    block = jax.ShapeDtypeStruct((cols, height, width), jnp.bfloat16)
    exact = jax.ShapeDtypeStruct((cols, height, width), jnp.float32)
    masked = jax.ShapeDtypeStruct((WINDOW, rows, lanes), jnp.float32)
    pair = (
        jax.ShapeDtypeStruct((SPAN, height, width), jnp.bfloat16),
        jax.ShapeDtypeStruct((SPAN, height, width), jnp.float32),
    )
    prepared = pl.pallas_call(
        functools.partial(own_kernel, total_rows),
        out_shape=(tall,) * 4 + (masked,) + (exact,) * 4 + pair + (exact,) * 2,
        in_specs=[smem] + [vmem] * 5,
        out_specs=(vmem,) * 13,
        compiler_params=limits,
        cost_estimate=pl.CostEstimate(flops=1_000_000_000, bytes_accessed=4_000_000, transcendentals=200_000),
        name="own",
    )(place, tok, cot, adaptive, qkv_weight, output_weight)
    *own, mask, query_raw, query_inv, key_raw, key_inv, attended, grad_query, grad_key, grad_value = prepared
    starts = tuple(range(0, cols + REACH, SPAN))
    middle = starts.index(REACH)
    third = (cols - SPAN) // 2
    part = (
        jax.ShapeDtypeStruct((third, height, width), jnp.bfloat16),
        jax.ShapeDtypeStruct((third, height, width), jnp.float32),
    )
    near, far = (pltpu.VMEM((count, rows, width), jnp.bfloat16) for count in (RADIUS, REACH))
    side = [near, far, far, near]
    from_left = pl.pallas_call(
        functools.partial(left_kernel, starts[:middle], total_cols),
        out_shape=part + (exact,) * 2,
        in_specs=[smem] + [vmem] * 11,
        out_specs=(vmem,) * 4,
        scratch_shapes=side,
        compiler_params=limits,
        cost_estimate=pl.CostEstimate(flops=2_000_000_000, bytes_accessed=2_000_000, transcendentals=400_000),
        name="left",
    )(place, left, adaptive, qkv_weight, output_weight, *own, mask, grad_key, grad_value)
    pieces = width // CORES // LINES * (4 * width // LANES)
    chunks = jax.ShapeDtypeStruct((pieces * (LINES + SLOT // 2), LANES), jnp.bfloat16)
    result, grad_tokens, mine, other = pl.pallas_call(
        functools.partial(right_kernel, starts[middle + 1 :], total_cols),
        out_shape=(block, block, chunks, chunks),
        in_specs=[smem] + [vmem] * 21,
        out_specs=(vmem,) * 4,
        scratch_shapes=[
            pltpu.VMEM((third, height, width), jnp.bfloat16),
            pltpu.VMEM((third, height, width), jnp.float32),
            pltpu.VMEM((cols, height, width), jnp.float32),
            pltpu.VMEM((cols, height, width), jnp.float32),
            pltpu.VMEM((width, 4 * width), jnp.float32),
        ]
        + side,
        compiler_params=limits,
        cost_estimate=pl.CostEstimate(flops=3_000_000_000, bytes_accessed=3_000_000, transcendentals=400_000),
        name="right",
    )(
        place,
        tok,
        cot,
        right,
        adaptive,
        qkv_weight,
        output_weight,
        *own,
        mask,
        query_raw,
        query_inv,
        key_raw,
        key_inv,
        attended,
        grad_query,
        *from_left,
    )
    result = result.transpose(1, 0, 2)
    grad_tokens = grad_tokens.transpose(1, 0, 2)
    mine = summed(mine, other)
    other = lax.ppermute(mine, "core", PARTNER)
    anywhere = pl.BlockSpec(memory_space=pl.ANY)
    gradients = ((width, 3 * width), (width, width), (CF, width))
    senders = (lax.axis_size("zone") * CORES, lax.axis_size("row") * lax.axis_size("col"))
    total_qkv, total_output, total_time = pl.pallas_call(
        functools.partial(finish_kernel, senders),
        out_shape=tuple(jax.ShapeDtypeStruct(shape, jnp.float32) for shape in gradients),
        in_specs=[smem, vmem, vmem],
        out_specs=(anywhere,) * 3,
        scratch_shapes=[pltpu.VMEM(shape, jnp.float32) for shape in gradients]
        + [pltpu.SemaphoreType.DMA((CORES * (width // CORES // LINES + 1) + 1,))],
        compiler_params=pltpu.CompilerParams(vmem_limit_bytes=16 * 2**20),
        cost_estimate=pl.CostEstimate(flops=200_000_000, bytes_accessed=2_000_000, transcendentals=2_000),
        name="finish",
    )(place, mine, other)
    return (result[None], grad_tokens[None], total_qkv, total_output, total_time)


def swap(pieces, axes):
    return lax.all_to_all(pieces, axes, 0, 0, tiled=True)


def total(pieces):
    return jnp.sum(pieces.astype(jnp.float32), axis=0).astype(jnp.bfloat16)


def copied(piece, axes):
    count = lax.axis_size(axes)
    return lax.optimization_barrier(jnp.broadcast_to(piece[None], (count,) + piece.shape))


def summed(mine, other):
    mine = total(jnp.stack([mine, lax.ppermute(other, "core", PARTNER)]))
    parts = lax.axis_size("col")
    pieces = mine.reshape(parts, mine.shape[0] // parts // 4, 4, LANES)
    piece = total(swap(pieces, "col"))
    piece = total(swap(copied(piece, ("zone", "row")), ("zone", "row")))
    return swap(copied(piece, "col"), "col").reshape(mine.shape)


def solution(mesh):
    shape = (mesh.shape["dp"] // CORES, CORES, mesh.shape["row"], mesh.shape["col"])
    mesh = jax.sharding.Mesh(mesh.devices.reshape(shape), ("zone", "core", "row", "col"))
    grid = P(("zone", "core"), "row", "col", None)
    in_specs = (grid, P(("zone", "core")), grid, P(), P(), P())
    out_specs = (grid, grid, P(), P(), P())
    return jax.shard_map(
        on_device, mesh=mesh, in_specs=in_specs, out_specs=out_specs, check_vma=False
    )
```

```python
import functools
import math

import jax
import jax.numpy as jnp
from jax import lax
from jax.experimental import pallas as pl
from jax.experimental.layout import Layout, with_layout_constraint
from jax.experimental.pallas import tpu as pltpu
from jax.sharding import PartitionSpec as P

HEAD_DIM = 64
CF = 256
RADIUS = 3
REACH = 2 * RADIUS
EDGE = 8
SPAN = 2
WINDOW = SPAN + REACH

score_scale = 6.0
epsilon = 1e-06


def fourier(step_value):
    half_count = CF // 2
    ladder = jnp.arange(half_count, dtype=jnp.float32)
    frequency = jnp.exp(ladder * (-math.log(1000.0) / half_count))
    phase_angle = step_value.astype(jnp.float32) * frequency
    return jnp.concatenate([jnp.cos(phase_angle), jnp.sin(phase_angle)])


def exchange(to_next, to_previous, axis):
    count = lax.axis_size(axis)
    forward = [(i, i + 1) for i in range(count - 1)]
    backward = [(target, source) for source, target in forward]
    from_previous = lax.ppermute(to_next, axis, forward)
    from_next = lax.ppermute(to_previous, axis, backward)
    return from_previous, from_next


def nn(left, right):
    return lax.dot_general(left, right, (((1,), (0,)), ((), ())), preferred_element_type=jnp.float32)


def nt(left, right):
    return lax.dot_general(left, right, (((1,), (1,)), ((), ())), preferred_element_type=jnp.float32)


def tn(left, right):
    return lax.dot_general(left, right, (((0,), (0,)), ((), ())), preferred_element_type=jnp.float32)


def average_matrix(width):
    own_head = lax.broadcasted_iota(jnp.int32, (width, width), 0) // HEAD_DIM
    other_head = lax.broadcasted_iota(jnp.int32, (width, width), 1) // HEAD_DIM
    return jnp.where(own_head == other_head, 1.0 / HEAD_DIM, 0.0).astype(jnp.bfloat16)


def head_mean(values, average):
    coarse = values.astype(jnp.bfloat16)
    fine = (values - coarse.astype(jnp.float32)).astype(jnp.bfloat16)
    return nn(coarse, average) + nn(fine, average)


def normalized(pixels, adaptive):
    inverse = lax.rsqrt(jnp.mean(pixels * pixels, axis=-1, keepdims=True) + epsilon)
    return inverse, (pixels * inverse * adaptive).astype(jnp.bfloat16)


def projected(pixels, adaptive, qkv_ref, average):
    width = pixels.shape[-1]
    inverse, normed = normalized(pixels, adaptive)
    project = nn(normed, qkv_ref[...])
    query_raw = project[:, :width]
    key_raw = project[:, width : 2 * width]
    query_inv = lax.rsqrt(head_mean(query_raw * query_raw, average) + epsilon)
    key_inv = lax.rsqrt(head_mean(key_raw * key_raw, average) + epsilon)
    query = query_raw * query_inv * (score_scale / HEAD_DIM)
    return inverse, normed, query, key_raw * key_inv, project[:, 2 * width :], (query_raw, query_inv, key_raw, key_inv)


def head_picks(width):
    lane_head = lax.broadcasted_iota(jnp.int32, (1, width), 1) // HEAD_DIM
    return [jnp.where(lane_head == head, 1.0, 0.0) for head in range(width // HEAD_DIM)]


def spread(part):
    return jnp.concatenate([part * pick.astype(jnp.bfloat16) for pick in head_picks(part.shape[-1])], axis=0)


def soften(scores, slope, mask):
    exponent = jnp.exp(scores - score_scale) * mask
    denominator = jnp.maximum(jnp.sum(exponent, axis=0, keepdims=True), 1e-30)
    weights = (exponent * (1.0 / denominator)).astype(jnp.bfloat16)
    wide = weights.astype(jnp.float32)
    middle = jnp.sum(wide * slope, axis=0, keepdims=True)
    return weights, (wide * (slope - middle)).astype(jnp.bfloat16)


def combined(weights, grad_score, keys, values, queries, grads, rows, height, wanted, first, count):
    width = keys.shape[-1]
    picks = head_picks(width)

    def gathered(part):
        total = part[: SPAN * rows] * picks[0]
        for head in range(1, len(picks)):
            total = total + part[head * SPAN * rows : (head + 1) * SPAN * rows] * picks[head]
        return total.reshape(SPAN, rows, width)[:, :height]

    def kept(part):
        shape = (WINDOW, rows, part.shape[1])
        return part.reshape(shape)[first : first + count, :height].reshape(-1, part.shape[1])

    attended = grad_query = None
    if wanted:
        attended = gathered(tn(weights, values)).astype(jnp.bfloat16)
        grad_query = gathered(tn(grad_score, keys))
    shape = (count, height, width)
    return attended, grad_query, nn(kept(grad_score), queries).reshape(shape), nn(kept(weights), grads).reshape(shape)


def own_kernel(
    total_rows,
    place_ref,
    tok_ref,
    cot_ref,
    adaptive_ref,
    qkv_ref,
    out_ref,
    query_ref,
    key_ref,
    value_ref,
    grad_ref,
    mask_ref,
    query_raw_ref,
    query_inv_ref,
    key_raw_ref,
    key_inv_ref,
    attended_ref,
    grad_query_ref,
    grad_key_ref,
    grad_value_ref,
):
    cols, rows, width = tok_ref.shape
    lanes = mask_ref.shape[2]
    height = rows - 2 * EDGE
    row_first = place_ref[0]
    pixels = tok_ref[...].astype(jnp.float32).reshape(cols * rows, width)
    _, _, query, key, value, raw = projected(pixels, adaptive_ref[...], qkv_ref, average_matrix(width))
    query = query.astype(jnp.bfloat16)
    key = key.astype(jnp.bfloat16)
    value = value.astype(jnp.bfloat16)
    grad = nt(cot_ref[...].reshape(cols * rows, width), out_ref[...]).astype(jnp.bfloat16)
    for ref, values in ((query_ref, query), (key_ref, key), (value_ref, value), (grad_ref, grad)):
        ref[...] = values.reshape(cols, rows, width)
    for ref, values in zip((query_raw_ref, query_inv_ref, key_raw_ref, key_inv_ref), raw):
        ref[...] = values.reshape(cols, rows, width)[:, :height]

    def row_at(position):
        halo = jnp.where(position < height + EDGE, position - height - EDGE, position - EDGE)
        return jnp.where(position < height, position, halo)

    key_row = row_at(lax.broadcasted_iota(jnp.int32, (1, rows, 1), 1))
    key_col = lax.broadcasted_iota(jnp.int32, (WINDOW, 1, 1), 0)
    lane = lax.broadcasted_iota(jnp.int32, (1, 1, lanes), 2) % (SPAN * rows)
    query_row = row_at(lane % rows)
    query_col = lane // rows
    row_gap = key_row - query_row
    col_gap = key_col - query_col
    image_row = jnp.broadcast_to(row_first + key_row, row_gap.shape)
    near_row = (row_gap >= -RADIUS) & (row_gap <= RADIUS) & (image_row >= 0) & (image_row < total_rows)
    near_col = (col_gap >= 0) & (col_gap <= REACH)
    mask = jnp.where(near_row, 1.0, 0.0) * jnp.where(near_col, 1.0, 0.0)
    mask_ref[...] = mask

    pair = slice(RADIUS * rows, (RADIUS + SPAN) * rows)
    queries, grads = spread(query[pair]), spread(grad[pair])
    weights, grad_score = soften(nt(key, queries), nt(value, grads), mask.reshape(cols * rows, lanes))
    attended_ref[...], grad_query_ref[...], grad_key_ref[...], grad_value_ref[...] = combined(
        weights, grad_score, key, value, queries, grads, rows, height, True, 0, cols
    )


def side_pairs(
    starts,
    total_cols,
    place_ref,
    side_ref,
    adaptive_ref,
    qkv_ref,
    out_ref,
    own,
    mask_ref,
    side,
    attended_ref,
    grad_query_ref,
    grad_key_ref,
    grad_value_ref,
):
    cols, rows, width = own[0].shape
    height = rows - 2 * EDGE
    last = REACH + cols
    col_first = place_ref[1]
    left = starts[0] == 0
    pixels = side_ref[:REACH].astype(jnp.float32).reshape(REACH * rows, width)
    average = average_matrix(width)
    _, normed = normalized(pixels, adaptive_ref[...])
    project = nn(normed, qkv_ref[:, width:])
    key_raw = project[:, :width]
    key = key_raw * lax.rsqrt(head_mean(key_raw * key_raw, average) + epsilon)
    for ref, values in zip(side[1:3], (key, project[:, width:])):
        ref[...] = values.astype(jnp.bfloat16).reshape(REACH, rows, width)
    asking = slice((REACH - RADIUS) * rows, REACH * rows) if left else slice(0, RADIUS * rows)
    query_raw = nn(normed[asking], qkv_ref[:, :width])
    query_inv = lax.rsqrt(head_mean(query_raw * query_raw, average) + epsilon)
    query = query_raw * query_inv * (score_scale / HEAD_DIM)
    side[0][...] = query.astype(jnp.bfloat16).reshape(RADIUS, rows, width)
    grad = nt(side_ref[REACH:].reshape(RADIUS * rows, width), out_ref[...])
    side[3][...] = grad.astype(jnp.bfloat16).reshape(RADIUS, rows, width)

    def columns(which, low, high):
        beside = side[which]
        base = (REACH - beside.shape[0]) if left else last
        parts = []
        if left and low < REACH:
            parts.append(beside[low - base : min(high, REACH) - base])
        if max(low, REACH) < min(high, last):
            parts.append(own[which][max(low, REACH) - REACH : min(high, last) - REACH])
        if not left and high > last:
            parts.append(beside[max(low, last) - base : high - base])
        joined = parts[0] if len(parts) == 1 else jnp.concatenate(parts, axis=0)
        return joined.reshape((high - low) * rows, width)

    def scored(start):
        first = start + RADIUS
        keys, values = columns(1, start, start + WINDOW), columns(2, start, start + WINDOW)
        queries, grads = spread(columns(0, first, first + SPAN)), spread(columns(3, first, first + SPAN))
        return nt(keys, queries), nt(values, grads), (keys, values, queries, grads)

    def softened(start, scores, slope):
        masks = []
        for column in range(start, start + WINDOW):
            mask = mask_ref[column - start]
            if column < REACH or column >= last:
                image_col = col_first + (column - REACH)
                mask = mask * jnp.where((image_col >= 0) & (image_col < total_cols), 1.0, 0.0)
            masks.append(mask)
        return soften(scores, slope, jnp.concatenate(masks, axis=0))

    done = 0
    following = scored(starts[0])
    for start in starts:
        scores, slope, blocks = following
        if start != starts[-1]:
            following = scored(start + SPAN)
        weights, grad_score = softened(start, scores, slope)
        low, high = max(start, REACH), min(start + WINDOW, last)
        first = start + RADIUS
        query_low, query_high = max(first, REACH), min(first + SPAN, last)
        attended, grad_query, grad_key, grad_value = combined(
            weights, grad_score, *blocks, rows, height, query_low < query_high, low - start, high - low
        )
        if query_low < query_high:
            there = pl.ds(done, query_high - query_low)
            attended_ref[there] = attended[query_low - first : query_high - first]
            grad_query_ref[there] = grad_query[query_low - first : query_high - first]
            done += query_high - query_low
        there = pl.ds(low - REACH, high - low)
        grad_key_ref[there] += grad_key
        grad_value_ref[there] += grad_value


def left_kernel(
    starts,
    total_cols,
    place_ref,
    side_ref,
    adaptive_ref,
    qkv_ref,
    out_ref,
    query_ref,
    key_ref,
    value_ref,
    grad_ref,
    mask_ref,
    own_grad_key_ref,
    own_grad_value_ref,
    attended_ref,
    grad_query_ref,
    grad_key_ref,
    grad_value_ref,
    *side,
):
    grad_key_ref[...] = own_grad_key_ref[...]
    grad_value_ref[...] = own_grad_value_ref[...]
    own = (query_ref, key_ref, value_ref, grad_ref)
    results = (attended_ref, grad_query_ref, grad_key_ref, grad_value_ref)
    side_pairs(starts, total_cols, place_ref, side_ref, adaptive_ref, qkv_ref, out_ref, own, mask_ref, side, *results)


def right_kernel(
    starts,
    total_cols,
    place_ref,
    tok_ref,
    cot_ref,
    side_ref,
    adaptive_ref,
    qkv_ref,
    out_ref,
    query_ref,
    key_ref,
    value_ref,
    grad_ref,
    mask_ref,
    query_raw_ref,
    query_inv_ref,
    key_raw_ref,
    key_inv_ref,
    own_attended_ref,
    own_grad_query_ref,
    left_attended_ref,
    left_grad_query_ref,
    left_grad_key_ref,
    left_grad_value_ref,
    result_ref,
    grad_tokens_ref,
    mine_ref,
    other_ref,
    attended_ref,
    grad_query_ref,
    grad_key_ref,
    grad_value_ref,
    whole_ref,
    *side,
):
    cols, rows, width = tok_ref.shape
    height = rows - 2 * EDGE
    image = place_ref[2]
    core = place_ref[3]
    step_value = place_ref[4]
    adaptive = adaptive_ref[...]
    factor = score_scale / HEAD_DIM
    average = average_matrix(width)
    grad_key_ref[...] = left_grad_key_ref[...]
    grad_value_ref[...] = left_grad_value_ref[...]
    own = (query_ref, key_ref, value_ref, grad_ref)
    results = (attended_ref, grad_query_ref, grad_key_ref, grad_value_ref)
    side_pairs(starts, total_cols, place_ref, side_ref, adaptive_ref, qkv_ref, out_ref, own, mask_ref, side, *results)

    tokens = cols * height
    pixels = tok_ref[:, :height].astype(jnp.float32).reshape(tokens, width)
    inverse, normed = normalized(pixels, adaptive)
    cot_own = cot_ref[:, :height].reshape(tokens, width)
    parts = (left_attended_ref[...], own_attended_ref[...], attended_ref[...])
    attended = jnp.concatenate(parts, axis=0).reshape(tokens, width)
    result = pixels + nn(attended, out_ref[...])
    result_ref[...] = result.astype(jnp.bfloat16).reshape(cols, height, width)
    whole_ref[:, 3 * width :] = tn(attended, cot_own)

    def back(raw, inv, grad, scale):
        return scale * inv * (grad - raw * inv * inv * head_mean(grad * raw, average))

    parts = (left_grad_query_ref[...], own_grad_query_ref[...], grad_query_ref[...])
    grad_query = jnp.concatenate(parts, axis=0).reshape(tokens, width)
    grad_key = grad_key_ref[...].reshape(tokens, width)
    grad_project = jnp.concatenate(
        [
            back(query_raw_ref[...].reshape(tokens, width), query_inv_ref[...].reshape(tokens, width), grad_query, factor).astype(jnp.bfloat16),
            back(key_raw_ref[...].reshape(tokens, width), key_inv_ref[...].reshape(tokens, width), grad_key, 1.0).astype(jnp.bfloat16),
            grad_value_ref[...].reshape(tokens, width).astype(jnp.bfloat16),
        ],
        axis=1,
    )
    whole_ref[:, : 3 * width] = tn(normed, grad_project)
    grad_normed = nt(grad_project, qkv_ref[...])
    scaled = grad_normed * adaptive
    inner = jnp.mean(scaled * pixels, axis=-1, keepdims=True)
    grad_pixels = inverse * (scaled - pixels * (inverse * inverse * inner))
    grad_tokens = cot_own.astype(jnp.float32) + grad_pixels
    grad_tokens_ref[...] = grad_tokens.astype(jnp.bfloat16).reshape(cols, height, width)
    grad_adaptive = jnp.sum(grad_normed * (pixels * inverse), axis=0, keepdims=True)

    half = width // CORES
    across = 4 * width // LANES
    line = lax.broadcasted_iota(jnp.int32, (SLOT, LANES), 0)
    lane = lax.broadcasted_iota(jnp.int32, (SLOT, LANES), 1)
    low_half, high_half = grad_adaptive[:, :LANES], grad_adaptive[:, LANES:]
    adaptives = jnp.where(line == image, low_half, jnp.where(line == SLOT // 2 + image, high_half, 0.0))
    high = (step_value // 32).astype(jnp.float32)
    low = (step_value % 32).astype(jnp.float32)
    steps = jnp.where(line == image, jnp.where(lane == 0, high, jnp.where(lane == 1, low, 0.0)), 0.0)
    for ref, which in ((mine_ref, core), (other_ref, 1 - core)):
        part = whole_ref[pl.ds(pl.multiple_of(which * half, half), half), :].astype(jnp.bfloat16)
        for block in range(half // LINES * across):
            top = block // across * LINES
            first = block % across * LANES
            ref[pl.ds(block_line(block), LINES), :] = part[top : top + LINES, first : first + LANES]
            if block % 2 == 0:
                side = adaptives if block == 0 else steps if block == 2 else jnp.zeros((SLOT, LANES), jnp.float32)
                ref[pl.ds(block_line(block) + LINES, SLOT), :] = side.astype(jnp.bfloat16)


def block_line(block):
    return (2 * LINES + SLOT) * (block // 2) + (LINES + SLOT) * (block % 2)


def finish_kernel(senders, place_ref, mine_ref, other_ref, qkv_ref, output_ref, time_ref, qkv, output, time, sems):
    images, share = senders
    width = output.shape[0]
    half = width // CORES
    across = 4 * width // LANES
    core = place_ref[3]
    copies = []

    def send(source, target):
        copies.append(pltpu.make_async_copy(source, target, sems.at[len(copies)]))
        copies[-1].start()

    for ref, which in ((mine_ref, core), (other_ref, 1 - core)):
        for band in range(half // LINES):
            there = pl.ds(pl.multiple_of(which * half + band * LINES, LINES), LINES)
            for place in range(across):
                values = ref[pl.ds(block_line(band * across + place), LINES), :].astype(jnp.float32)
                first = place * LANES
                if first < 3 * width:
                    qkv[there, first : first + LANES] = values
                else:
                    output[there, first - 3 * width : first - 3 * width + LANES] = values
            send(qkv.at[there], qkv_ref.at[there])
        there = pl.ds(pl.multiple_of(which * half, half), half)
        send(output.at[there], output_ref.at[there])
    side = mine_ref[LINES : LINES + SLOT, :].astype(jnp.float32)
    half_slot = SLOT // 2
    adaptives = jnp.concatenate([side, jnp.concatenate([side[half_slot:], side[:half_slot]], axis=0)], axis=1)
    line = lax.broadcasted_iota(jnp.int32, (SLOT, 1), 0)
    adaptives = jnp.where(line < images, adaptives, 0.0)
    steps = mine_ref[pl.ds(block_line(2) + LINES, SLOT), :].astype(jnp.float32)
    steps = (steps[:, 0:1] * 32.0 + steps[:, 1:2]) / share
    ladder = lax.broadcasted_iota(jnp.int32, (1, CF // 2), 1).astype(jnp.float32)
    frequency = jnp.exp(ladder * (-math.log(1000.0) / (CF // 2)))
    angle = steps * frequency
    features = jnp.concatenate([jnp.cos(angle), jnp.sin(angle)], axis=1)
    time[...] = lax.dot_general(
        features,
        adaptives,
        (((0,), (0,)), ((), ())),
        precision=lax.Precision.HIGHEST,
        preferred_element_type=jnp.float32,
    )
    send(time, time_ref)
    for copy in copies:
        copy.wait()


CORES = 2
PARTNER = ((0, 1), (1, 0))
SLOT = 8
LINES = 32
LANES = 128


def edge_kernel(tok_ref, cot_ref, last_ref, first_ref, sems):
    height = tok_ref.shape[0]
    copies = []
    for target, low in ((last_ref, height - EDGE), (first_ref, 0)):
        for half, source in enumerate((tok_ref, cot_ref)):
            there = target.at[pl.ds(half * EDGE, EDGE)]
            copies.append(pltpu.make_async_copy(source.at[pl.ds(low, EDGE)], there, sems.at[len(copies)]))
    for copy in copies:
        copy.start()
    for copy in copies:
        copy.wait()


def lying(values):
    return with_layout_constraint(values, Layout(major_to_minor=(0, 1, 2)))


def on_device(tokens, timesteps, cotangent, qkv_weight, output_weight, time_weight):
    height, cols, width = tokens.shape[1:]
    row_first = lax.axis_index("row") * height
    col_first = lax.axis_index("col") * cols
    total_rows = height * lax.axis_size("row")
    total_cols = cols * lax.axis_size("col")
    rows = height + 2 * EDGE

    message = jax.ShapeDtypeStruct((2 * EDGE, cols, width), jnp.bfloat16)
    last_rows, first_rows = pl.pallas_call(
        edge_kernel,
        out_shape=(message,) * 2,
        in_specs=[pl.BlockSpec(memory_space=pl.ANY)] * 2,
        out_specs=(pl.BlockSpec(memory_space=pltpu.VMEM),) * 2,
        scratch_shapes=[pltpu.SemaphoreType.DMA((4,))],
        compiler_params=pltpu.CompilerParams(vmem_limit_bytes=8 * 2**20),
        cost_estimate=pl.CostEstimate(flops=0, bytes_accessed=300_000, transcendentals=0),
        name="edges",
    )(tokens[0], cotangent[0])
    both = jnp.concatenate([tokens[0].transpose(1, 0, 2), cotangent[0].transpose(1, 0, 2)], axis=0)
    above, below = exchange(lying(last_rows), lying(first_rows), "row")
    above, below = (lying(rows_).transpose(1, 0, 2).reshape(cols, 2, EDGE, width) for rows_ in (above, below))
    above, below = (rows_.transpose(1, 0, 2, 3).reshape(2 * cols, EDGE, width) for rows_ in (above, below))
    both = jnp.concatenate([both, above, below], axis=1)
    tok, cot = both[:cols], both[cols:]
    to_next = jnp.concatenate([tok[cols - REACH :], cot[cols - RADIUS :]], axis=0)
    to_previous = jnp.concatenate([tok[:REACH], cot[:RADIUS]], axis=0)
    left, right = exchange(to_next, to_previous, "col")
    features = fourier(timesteps[0])
    adaptive = 1.0 + jnp.dot(
        features[None], time_weight.astype(jnp.float32), precision=lax.Precision.HIGHEST
    )
    image = lax.axis_index(("zone", "core"))
    place = [row_first, col_first, image, lax.axis_index("core"), timesteps[0]]
    place = jnp.stack(place).astype(jnp.int32)

    lanes = width // HEAD_DIM * SPAN * rows
    smem = pl.BlockSpec(memory_space=pltpu.SMEM)
    vmem = pl.BlockSpec(memory_space=pltpu.VMEM)
    limits = pltpu.CompilerParams(vmem_limit_bytes=40 * 2**20)
    tall = jax.ShapeDtypeStruct((cols, rows, width), jnp.bfloat16)
    block = jax.ShapeDtypeStruct((cols, height, width), jnp.bfloat16)
    exact = jax.ShapeDtypeStruct((cols, height, width), jnp.float32)
    masked = jax.ShapeDtypeStruct((WINDOW, rows, lanes), jnp.float32)
    pair = (
        jax.ShapeDtypeStruct((SPAN, height, width), jnp.bfloat16),
        jax.ShapeDtypeStruct((SPAN, height, width), jnp.float32),
    )
    prepared = pl.pallas_call(
        functools.partial(own_kernel, total_rows),
        out_shape=(tall,) * 4 + (masked,) + (exact,) * 4 + pair + (exact,) * 2,
        in_specs=[smem] + [vmem] * 5,
        out_specs=(vmem,) * 13,
        compiler_params=limits,
        cost_estimate=pl.CostEstimate(flops=1_000_000_000, bytes_accessed=4_000_000, transcendentals=200_000),
        name="own",
    )(place, tok, cot, adaptive, qkv_weight, output_weight)
    *own, mask, query_raw, query_inv, key_raw, key_inv, attended, grad_query, grad_key, grad_value = prepared
    starts = tuple(range(0, cols + REACH, SPAN))
    middle = starts.index(REACH)
    third = (cols - SPAN) // 2
    part = (
        jax.ShapeDtypeStruct((third, height, width), jnp.bfloat16),
        jax.ShapeDtypeStruct((third, height, width), jnp.float32),
    )
    near, far = (pltpu.VMEM((count, rows, width), jnp.bfloat16) for count in (RADIUS, REACH))
    side = [near, far, far, near]
    from_left = pl.pallas_call(
        functools.partial(left_kernel, starts[:middle], total_cols),
        out_shape=part + (exact,) * 2,
        in_specs=[smem] + [vmem] * 11,
        out_specs=(vmem,) * 4,
        scratch_shapes=side,
        compiler_params=limits,
        cost_estimate=pl.CostEstimate(flops=2_000_000_000, bytes_accessed=2_000_000, transcendentals=400_000),
        name="left",
    )(place, left, adaptive, qkv_weight, output_weight, *own, mask, grad_key, grad_value)
    pieces = width // CORES // LINES * (4 * width // LANES)
    chunks = jax.ShapeDtypeStruct((pieces * (LINES + SLOT // 2), LANES), jnp.bfloat16)
    result, grad_tokens, mine, other = pl.pallas_call(
        functools.partial(right_kernel, starts[middle + 1 :], total_cols),
        out_shape=(block, block, chunks, chunks),
        in_specs=[smem] + [vmem] * 21,
        out_specs=(vmem,) * 4,
        scratch_shapes=[
            pltpu.VMEM((third, height, width), jnp.bfloat16),
            pltpu.VMEM((third, height, width), jnp.float32),
            pltpu.VMEM((cols, height, width), jnp.float32),
            pltpu.VMEM((cols, height, width), jnp.float32),
            pltpu.VMEM((width, 4 * width), jnp.float32),
        ]
        + side,
        compiler_params=limits,
        cost_estimate=pl.CostEstimate(flops=3_000_000_000, bytes_accessed=3_000_000, transcendentals=400_000),
        name="right",
    )(
        place,
        tok,
        cot,
        right,
        adaptive,
        qkv_weight,
        output_weight,
        *own,
        mask,
        query_raw,
        query_inv,
        key_raw,
        key_inv,
        attended,
        grad_query,
        *from_left,
    )
    result = result.transpose(1, 0, 2)
    grad_tokens = grad_tokens.transpose(1, 0, 2)
    mine = summed(mine, other)
    other = lax.ppermute(mine, "core", PARTNER)
    anywhere = pl.BlockSpec(memory_space=pl.ANY)
    gradients = ((width, 3 * width), (width, width), (CF, width))
    senders = (lax.axis_size("zone") * CORES, lax.axis_size("row") * lax.axis_size("col"))
    total_qkv, total_output, total_time = pl.pallas_call(
        functools.partial(finish_kernel, senders),
        out_shape=tuple(jax.ShapeDtypeStruct(shape, jnp.float32) for shape in gradients),
        in_specs=[smem, vmem, vmem],
        out_specs=(anywhere,) * 3,
        scratch_shapes=[pltpu.VMEM(shape, jnp.float32) for shape in gradients]
        + [pltpu.SemaphoreType.DMA((CORES * (width // CORES // LINES + 1) + 1,))],
        compiler_params=pltpu.CompilerParams(vmem_limit_bytes=16 * 2**20),
        cost_estimate=pl.CostEstimate(flops=200_000_000, bytes_accessed=2_000_000, transcendentals=2_000),
        name="finish",
    )(place, mine, other)
    return (result[None], grad_tokens[None], total_qkv, total_output, total_time)


def swap(pieces, axes):
    return lax.all_to_all(pieces, axes, 0, 0, tiled=True)


def total(pieces):
    return jnp.sum(pieces.astype(jnp.float32), axis=0).astype(jnp.bfloat16)


def copied(piece, axes):
    count = lax.axis_size(axes)
    return lax.optimization_barrier(jnp.broadcast_to(piece[None], (count,) + piece.shape))


def summed(mine, other):
    mine = total(jnp.stack([mine, lax.ppermute(other, "core", PARTNER)]))
    parts = lax.axis_size("col")
    pieces = mine.reshape(parts, mine.shape[0] // parts // 4, 4, LANES)
    piece = total(swap(pieces, "col"))
    piece = total(swap(copied(piece, ("zone", "row")), ("zone", "row")))
    return swap(copied(piece, "col"), "col").reshape(mine.shape)


def solution(mesh):
    shape = (mesh.shape["dp"] // CORES, CORES, mesh.shape["row"], mesh.shape["col"])
    mesh = jax.sharding.Mesh(mesh.devices.reshape(shape), ("zone", "core", "row", "col"))
    grid = P(("zone", "core"), "row", "col", None)
    in_specs = (grid, P(("zone", "core")), grid, P(), P(), P())
    out_specs = (grid, grid, P(), P(), P())
    return jax.shard_map(
        on_device, mesh=mesh, in_specs=in_specs, out_specs=out_specs, check_vma=False
    )
```
